128 devices in a mesh: user: 8 (over y, core), item: 16 (over x, z).
Axes of the slice: x: 4, y: 4, z: 4, core: 2. Of those that a mesh axis runs over, the one named last changes fastest.
Arguments:
- item_factor: float32 [32768, 256], P(('item', 'user')), may hold values from -36 to 36
- context_factor: float32 [4096, 256], replicated, may hold values from -6 to 6
- tile_count: int32 [8, 16], P('user', 'item'), may hold values from 16 to 128, as said below
- tile_rows: int32 [8, 16, 128], P('user', 'item'), may hold values from 0 to 63
- tile_cols: int32 [8, 16, 128], P('user', 'item'), may hold values from 0 to 31
- tile_ctx: int32 [8, 16, 128], P('user', 'item'), may hold values from 0 to 63
- nz_offsets: int32 [8, 16, 3, 128, 512], P('user', 'item'), may hold values from 0 to 63
- nz_values: float32 [8, 16, 128, 512], P('user', 'item'), may hold values from -6 to 6
Outputs:
- user_factor: float32 [32768, 256], P(('user', 'item'))
- new_items: float32 [32768, 256], P(('item', 'user'))
The draws below stay inside these ranges and needn't reach their ends.
Inputs may be any that keep to these rules, and one draw needn't show every extreme that they name: `tile_count`: some device has all 128 tiles live; the others 128, half, a quarter or an eighth of them.
All inputs are finite; a program needn't handle non-finite values.
Results may differ from the reference program's by a relative error of at most 0.0066.
Values may be sent and summed in bfloat16 or wider, within the bound.
A program may use at most 128 MiB of HBM per device.

```python
import math
import jax
import jax.numpy as jnp
import numpy as np
from jax import lax

R = 256
TILE = 64
USR_DEV = 256
ITM_DEV = 256
CTX = 4096
TILES_DEV = 128
NNZ_TILE = 512
ITEMS = 32768
TROWS = 64
TCOLS = 32
CTILES = 64
N_USER = 8
N_ITEM = 16


def draw_tile_count(key, part):
    shift_key = jax.random.fold_in(key, 11)
    pick_key = jax.random.fold_in(key, 12)
    shifts = jax.random.randint(shift_key, (N_USER * N_ITEM,), 0, 4)
    counts = jnp.right_shift(jnp.full((N_USER * N_ITEM,), TILES_DEV, jnp.int32), shifts.astype(jnp.int32))
    chosen = jax.random.randint(pick_key, (), 0, N_USER * N_ITEM)
    counts = jnp.where(jnp.arange(N_USER * N_ITEM) == chosen, TILES_DEV, counts)
    return counts.reshape(N_USER, N_ITEM).astype(jnp.int32)


def draw_item_factor(key, part):
    base_key = jax.random.fold_in(key, 21)
    row_key = jax.random.fold_in(key, 22)
    col_key = jax.random.fold_in(key, 23)
    log_ten = math.log(10.0)
    row_scale = jnp.exp(jax.random.uniform(row_key, (ITEMS, 1), minval=0.0, maxval=log_ten))
    col_scale = jnp.exp(jax.random.uniform(col_key, (1, R), minval=0.0, maxval=log_ten))
    ramped = jnp.sqrt(1.0 + 2.0 * jnp.arange(ITEMS, dtype=jnp.float32)[:, None] / ITEMS)
    base = jax.random.truncated_normal(base_key, -4.0, 4.0, (ITEMS, R))
    return (0.05 * base * row_scale * col_scale * ramped).astype(jnp.float32)


def set_ends(drawn, own_key, smallest, largest):
    index_at = [jax.random.randint(jax.random.fold_in(own_key, axis), (), 0, length) for axis, length in enumerate(drawn.shape)]
    main_axis = drawn.shape.index(max(drawn.shape))
    next_to = index_at[:main_axis] + [(index_at[main_axis] + 1) % drawn.shape[main_axis]] + index_at[main_axis + 1:]
    return drawn.at[tuple(index_at)].set(smallest).at[tuple(next_to)].set(largest)


def block_levels(key, extent, shards, least, largest):
    gain, own = 1.0, jax.random.fold_in(key, 6)
    for axis_at, parts in shards:
        heights = jnp.exp(jax.random.uniform(jax.random.fold_in(own, axis_at), (parts,), jnp.float32, least / len(shards), largest / len(shards)))
        gain = gain * jnp.repeat(heights, extent[axis_at] // parts).reshape([-1 if axis == axis_at else 1 for axis in range(len(extent))])
    return gain


def rank_table(amount, slope):
    weights = [(1 << 20) // math.isqrt(rank ** slope) + 1 for rank in range(1, amount + 1)]
    width = 1 + sum(weights) // (1 << 30)
    return np.cumsum(np.array([max(1, weight // width) for weight in weights]))


def skewed_ids(own_key, extent, count, skew):
    listing = rank_table(count, skew)
    pick = jax.random.randint(jax.random.fold_in(own_key, 1), extent, 0, int(listing[count - 1]))
    rank = jnp.searchsorted(jnp.asarray(listing, jnp.int32), pick, side="right")
    return jax.random.permutation(jax.random.fold_in(own_key, 2), count)[rank].astype(jnp.int32)


def centred(own_key, shape, scale, most, split=(), kind=jnp.bfloat16):
    factor_of = block_levels(own_key, shape, split, -0.22, 0.18) if split else 1.0
    values = jax.random.normal(own_key, shape, jnp.float32) * scale * factor_of
    return jnp.minimum(jnp.maximum(values, -most), most).astype(kind)


def setup_inputs(seed: int = 0) -> dict:
    seeds = jax.random.split(jax.random.key(seed), 9)
    item_factor = draw_item_factor(jax.random.fold_in(seeds[8], 71), 0)
    context_factor = centred(seeds[1], (CTX, R), 1.0, 6.0, (), jnp.float32)
    tile_count = draw_tile_count(jax.random.fold_in(seeds[8], 71), 0)
    tile_rows = set_ends(skewed_ids(seeds[3], (N_USER, N_ITEM, TILES_DEV), TROWS, 2), jax.random.fold_in(seeds[3], 3), 0, TROWS - 1).astype(jnp.int32)
    tile_cols = set_ends(jax.random.randint(seeds[4], (N_USER, N_ITEM, TILES_DEV), 0, TCOLS), jax.random.fold_in(seeds[4], 1), 0, TCOLS - 1).astype(jnp.int32)
    tile_ctx = set_ends(jax.random.randint(seeds[5], (N_USER, N_ITEM, TILES_DEV), 0, CTILES), jax.random.fold_in(seeds[5], 1), 0, CTILES - 1).astype(jnp.int32)
    nz_offsets = set_ends(jax.random.randint(seeds[6], (N_USER, N_ITEM, 3, TILES_DEV, NNZ_TILE), 0, TILE), jax.random.fold_in(seeds[6], 1), 0, TILE - 1).astype(jnp.int32)
    nz_values = centred(seeds[7], (N_USER, N_ITEM, TILES_DEV, NNZ_TILE), 1.0, 6.0, ((0, 8), (1, 16)), jnp.float32)
    return dict(item_factor=item_factor, context_factor=context_factor, tile_count=tile_count, tile_rows=tile_rows, tile_cols=tile_cols, tile_ctx=tile_ctx, nz_offsets=nz_offsets, nz_values=nz_values)


def solve_rows(right_side, gram):
    lower_factor = jnp.linalg.cholesky(gram)
    partway = lax.linalg.triangular_solve(lower_factor, right_side, left_side=False, lower=True, transpose_a=True)
    return lax.linalg.triangular_solve(lower_factor, partway, left_side=False, lower=True, transpose_a=False)

def reference(item_factor, context_factor, tile_count, tile_rows, tile_cols, tile_ctx, nz_offsets, nz_values):
    highest = lax.Precision.HIGHEST
    user_block = USR_DEV * N_ITEM
    item_block = ITM_DEV * N_USER
    users_total = user_block * N_USER
    items_total = item_block * N_ITEM
    context_copy = context_factor.astype(jnp.bfloat16)
    item_copy = item_factor.astype(jnp.bfloat16)
    context_gram = jnp.dot(context_factor.T.astype(jnp.float32), context_factor.astype(jnp.float32), precision=highest, preferred_element_type=jnp.float32)
    item_gram = jnp.dot(item_factor.T.astype(jnp.float32), item_factor.astype(jnp.float32), precision=highest, preferred_element_type=jnp.float32)

    def coordinates(device):
        row_dev = device // N_ITEM
        col_dev = device % N_ITEM
        alive = (jnp.arange(TILES_DEV, dtype=jnp.int32) < tile_count[row_dev, col_dev]).astype(jnp.float32)
        users = row_dev * user_block + TILE * tile_rows[row_dev, col_dev][:, None] + nz_offsets[row_dev, col_dev, 0]
        items = col_dev * item_block + TILE * tile_cols[row_dev, col_dev][:, None] + nz_offsets[row_dev, col_dev, 1]
        contexts = TILE * tile_ctx[row_dev, col_dev][:, None] + nz_offsets[row_dev, col_dev, 2]
        values = nz_values[row_dev, col_dev] * alive[:, None]
        return (users.reshape(-1), items.reshape(-1), contexts.reshape(-1), values.reshape(-1))

    def mttkrp(source_copy, total_rows, user_target):

        def visit(totals, device):
            users, items, contexts, values = coordinates(device)
            if user_target:
                targets, sources = (users, items)
            else:
                targets, sources = (items, users)
            terms = (values[:, None] * source_copy[sources].astype(jnp.float32) * context_copy[contexts].astype(jnp.float32)).astype(jnp.bfloat16)
            return (totals.at[targets].add(terms.astype(jnp.float32)), None)
        totals, _ = lax.scan(visit, jnp.zeros((total_rows, R), jnp.float32), jnp.arange(N_USER * N_ITEM, dtype=jnp.int32))
        return totals
    user_raw = solve_rows(mttkrp(item_copy, users_total, True), item_gram * context_gram)
    user_factor = user_raw * jnp.sqrt(users_total / (lax.optimization_barrier(jnp.sum(user_raw * user_raw, axis=0)) + 1e-06))
    user_copy = user_factor.astype(jnp.bfloat16)
    user_gram = jnp.dot(user_factor.T.astype(jnp.float32), user_factor.astype(jnp.float32), precision=highest, preferred_element_type=jnp.float32)
    item_raw = solve_rows(mttkrp(user_copy, items_total, False), user_gram * context_gram)
    new_items = item_raw * jnp.sqrt(items_total / (lax.optimization_barrier(jnp.sum(item_raw * item_raw, axis=0)) + 1e-06))
    return (user_factor, new_items)
```

```python
import functools

import jax
import jax.numpy as jnp
from jax import lax
from jax.experimental import pallas as pl
from jax.experimental.pallas import tpu as pltpu
from jax.sharding import PartitionSpec as P

TILE = 64
UNROLL = 16
BLOCK = 32
HIGHEST = lax.Precision.HIGHEST
MESH = pl.DeviceIdType.MESH
VMEM_SPEC = pl.BlockSpec(memory_space=pltpu.VMEM)
SMEM_SPEC = pl.BlockSpec(memory_space=pltpu.SMEM)


def dot(left, right):
    return jnp.dot(left, right, precision=HIGHEST, preferred_element_type=jnp.float32)


def dot_rows(left, right):
    return lax.dot_general(
        left, right, (((0,), (0,)), ((), ())), precision=HIGHEST, preferred_element_type=jnp.float32
    )


def mttkrp_kernel(
    count,
    target_ids,
    source_ids,
    context_ids,
    target_offsets,
    source_offsets,
    context_offsets,
    values,
    source,
    context,
    out,
    totals,
):
    totals[...] = jnp.zeros_like(totals)
    positions = lax.broadcasted_iota(jnp.int32, (TILE, target_offsets.shape[1]), 0)

    def one_hot(row):
        return jnp.where(positions == row, 1.0, 0.0).astype(jnp.bfloat16)

    def gather(tile, row):
        return lax.dot_general(
            tile, one_hot(row), (((0,), (0,)), ((), ())), preferred_element_type=jnp.float32
        )

    def group(step, carry):
        first = pl.multiple_of(step * UNROLL, UNROLL)
        targets = target_offsets[pl.ds(first, UNROLL), :]
        sources = source_offsets[pl.ds(first, UNROLL), :]
        contexts = context_offsets[pl.ds(first, UNROLL), :]
        weights = values[pl.ds(first, UNROLL), :]
        for at in range(UNROLL):
            row = slice(at, at + 1)
            source_rows = gather(source[source_ids[first + at]], sources[row])
            context_rows = gather(context[context_ids[first + at]], contexts[row])
            terms = (weights[row] * source_rows * context_rows).astype(jnp.bfloat16)
            totals[target_ids[first + at]] += lax.dot_general(
                one_hot(targets[row]),
                terms,
                (((1,), (1,)), ((), ())),
                preferred_element_type=jnp.float32,
            )
        return carry

    lax.fori_loop(0, count[0] // UNROLL, group, 0)
    out[...] = totals[...].astype(out.dtype)


def mttkrp(count, target, source, context, values, source_tiles, context_tiles, tiles):
    shape = (tiles, TILE, source_tiles.shape[2])
    return pl.pallas_call(
        mttkrp_kernel,
        out_shape=jax.ShapeDtypeStruct(shape, jnp.bfloat16),
        in_specs=[SMEM_SPEC] * 4 + [VMEM_SPEC] * 6,
        out_specs=VMEM_SPEC,
        scratch_shapes=[pltpu.VMEM(shape, jnp.float32)],
        compiler_params=pltpu.CompilerParams(vmem_limit_bytes=48 * 2**20),
        name="mttkrp",
    )(
        count,
        target[0],
        source[0],
        context[0],
        target[1],
        source[1],
        context[1],
        values,
        source_tiles,
        context_tiles,
    )


def greet(groups):
    barrier = pltpu.get_barrier_semaphore()
    total = 0
    for axis, size in groups:
        me = lax.axis_index(axis)
        for ahead in range(1, size):
            pl.semaphore_signal(
                barrier, inc=1, device_id={axis: lax.rem(me + ahead, size)}, device_id_type=MESH
            )
        total += size - 1
    pl.semaphore_wait(barrier, total)


def send_all(axis, size, source, target, sems):
    me = lax.axis_index(axis)
    copies = []
    for ahead in range(1, size):
        peer = lax.rem(me + ahead, size)
        copy = pltpu.make_async_remote_copy(
            src_ref=source(peer, ahead),
            dst_ref=target(me, ahead),
            send_sem=sems.at[0, ahead - 1],
            recv_sem=sems.at[1, ahead - 1],
            device_id={axis: peer},
            device_id_type=MESH,
        )
        copy.start()
        copies.append(copy)
    return copies


def all_reduce(gram, scattered, summed, sems, result, axis_sizes):
    users, items = axis_sizes
    rows = gram.shape[0] // items
    user, item = lax.axis_index("user"), lax.axis_index("item")
    first = send_all(
        "item",
        items,
        lambda peer, ahead: gram.at[pl.ds(pl.multiple_of(peer * rows, rows), rows)],
        lambda me, ahead: scattered.at[me],
        sems.at[0],
    )
    scattered[item] = gram[pl.ds(pl.multiple_of(item * rows, rows), rows), :]
    for copy in first:
        copy.wait_recv()
    summed[user] = jnp.sum(scattered[...], axis=0)
    second = send_all(
        "user",
        users,
        lambda peer, ahead: summed.at[user],
        lambda me, ahead: summed.at[me],
        sems.at[1],
    )
    for copy in second:
        copy.wait_recv()
    own = pl.ds(pl.multiple_of(item * rows, rows), rows)
    result[own, :] = jnp.sum(summed[...], axis=0)
    third = send_all(
        "item",
        items,
        lambda peer, ahead: result.at[own],
        lambda me, ahead: result.at[own],
        sems.at[2],
    )
    for copy in third:
        copy.wait_recv()
    for copy in first + second + third:
        copy.wait_send()


def reduce_scratch(axis_sizes, width):
    users, items = axis_sizes
    rows = width // items
    return [
        pltpu.VMEM((width, width), jnp.float32),
        pltpu.VMEM((items, rows, width), jnp.float32),
        pltpu.VMEM((users, rows, width), jnp.float32),
        pltpu.SemaphoreType.DMA((3, 2, items - 1)),
    ]


def invert(work):
    width = work.shape[0]
    down = lax.broadcasted_iota(jnp.int32, (BLOCK, BLOCK), 0)
    across = lax.broadcasted_iota(jnp.int32, (BLOCK, BLOCK), 1)
    lanes = lax.broadcasted_iota(jnp.int32, (BLOCK, width), 1) // BLOCK
    rows = lax.broadcasted_iota(jnp.int32, (width, BLOCK), 0) // BLOCK
    full_lanes = lax.broadcasted_iota(jnp.int32, (width, width), 1) // BLOCK
    for block in range(width // BLOCK):
        span = slice(block * BLOCK, (block + 1) * BLOCK)
        pivot = work[span, span]
        for at in range(BLOCK):
            inverse = 1.0 / pivot[at : at + 1, at : at + 1]
            row = jnp.where(across[:1] == at, inverse, pivot[at : at + 1, :] * inverse)
            column = pivot[:, at : at + 1]
            kept = jnp.where(across == at, 0.0, pivot)
            pivot = jnp.where(down == at, row, kept - column * row)
        panel = dot(pivot, work[span, :])
        panel = jnp.where(lanes == block, jnp.concatenate([pivot] * (width // BLOCK), axis=1), panel)
        column = jnp.where(rows == block, 0.0, work[:, span])
        kept = jnp.where(full_lanes == block, 0.0, work[...])
        work[...] = kept - dot(column, panel)
        work[span, :] = panel


def gather_kernel(
    axis_sizes, item_factor, context_factor, items, context, system, context_gram, gram, scattered,
    summed, gram_sems, sems
):
    users = axis_sizes[0]
    user = lax.axis_index("user")
    items[user] = item_factor[...].astype(jnp.bfloat16)
    greet((("user", axis_sizes[0]), ("item", axis_sizes[1])))
    copies = send_all(
        "user", users, lambda peer, ahead: items.at[user], lambda me, ahead: items.at[me], sems
    )
    gram[...] = dot_rows(item_factor[...], item_factor[...])
    step_rows = 512
    context_gram[...] = jnp.zeros_like(context_gram)

    def step(index, carry):
        span = pl.ds(pl.multiple_of(index * step_rows, step_rows), step_rows)
        chunk = context_factor[span, :]
        context[span, :] = chunk.astype(jnp.bfloat16)
        context_gram[...] += dot_rows(chunk, chunk)
        return carry

    lax.fori_loop(0, context_factor.shape[0] // step_rows, step, 0)
    all_reduce(gram, scattered, summed, gram_sems, system, axis_sizes)
    system[...] = system[...] * context_gram[...]
    for copy in copies:
        copy.wait_recv()
    for copy in copies:
        copy.wait_send()


def gather_items(item_factor, context_factor, axis_sizes):
    users, items = axis_sizes
    rows, width = item_factor.shape
    square = jax.ShapeDtypeStruct((width, width), jnp.float32)
    return pl.pallas_call(
        functools.partial(gather_kernel, axis_sizes),
        out_shape=(
            jax.ShapeDtypeStruct((users, rows, width), jnp.bfloat16),
            jax.ShapeDtypeStruct(context_factor.shape, jnp.bfloat16),
            square,
            square,
        ),
        in_specs=[VMEM_SPEC] * 2,
        out_specs=(VMEM_SPEC,) * 4,
        scratch_shapes=reduce_scratch(axis_sizes, width)
        + [pltpu.SemaphoreType.DMA((2, users - 1))],
        compiler_params=pltpu.CompilerParams(
            collective_id=0, has_side_effects=True, vmem_limit_bytes=32 * 2**20
        ),
        name="gather_items",
    )(item_factor, context_factor)


def user_kernel(
    axis_sizes, partial, system, raw, gathered, raw_gram, arrived, work, gram, scattered, summed,
    gram_sems, sems
):
    items = axis_sizes[1]
    item = lax.axis_index("item")
    greet((("user", axis_sizes[0]), ("item", axis_sizes[1])))
    copies = send_all(
        "item",
        items,
        lambda peer, ahead: partial.at[peer],
        lambda me, ahead: arrived.at[ahead - 1],
        sems.at[0],
    )
    work[...] = system[...]
    invert(work)
    total = partial[item].astype(jnp.float32)
    for ahead in range(1, items):
        copies[ahead - 1].wait_recv()
        total = total + arrived[ahead - 1].astype(jnp.float32)
    raw[...] = dot(total, work[...])
    gathered[item] = raw[...].astype(jnp.bfloat16)
    spread = send_all(
        "item", items, lambda peer, ahead: gathered.at[item], lambda me, ahead: gathered.at[me], sems.at[1]
    )
    gram[...] = dot_rows(raw[...], raw[...])
    all_reduce(gram, scattered, summed, gram_sems, raw_gram, axis_sizes)
    for copy in spread:
        copy.wait_recv()
    for copy in copies + spread:
        copy.wait_send()


def update_users(partial, system, axis_sizes):
    users, items = axis_sizes
    _, rows, width = partial.shape
    square = jax.ShapeDtypeStruct((width, width), jnp.float32)
    return pl.pallas_call(
        functools.partial(user_kernel, axis_sizes),
        out_shape=(
            jax.ShapeDtypeStruct((rows, width), jnp.float32),
            jax.ShapeDtypeStruct(partial.shape, jnp.bfloat16),
            square,
        ),
        in_specs=[VMEM_SPEC] * 2,
        out_specs=(VMEM_SPEC,) * 3,
        scratch_shapes=[
            pltpu.VMEM((items - 1, rows, width), jnp.bfloat16),
            pltpu.VMEM((width, width), jnp.float32),
        ]
        + reduce_scratch(axis_sizes, width)
        + [pltpu.SemaphoreType.DMA((2, 2, items - 1))],
        compiler_params=pltpu.CompilerParams(
            collective_id=1, has_side_effects=True, vmem_limit_bytes=32 * 2**20
        ),
        name="update_users",
    )(partial, system)


def item_kernel(
    axis_sizes, partial, raw_gram, context_gram, raw, new_items, user_factor, arrived, work,
    user_sums, item_sums, user_sems, item_sems, sems
):
    users, items = axis_sizes
    user, item = lax.axis_index("user"), lax.axis_index("item")
    greet((("user", users), ("item", items)))
    copies = send_all(
        "user",
        users,
        lambda peer, ahead: partial.at[peer],
        lambda me, ahead: arrived.at[ahead - 1],
        sems,
    )
    width = work.shape[0]
    rows_total = jnp.float32(user_factor.shape[0] * users * items)
    down = lax.broadcasted_iota(jnp.int32, (width, width), 0)
    across = lax.broadcasted_iota(jnp.int32, (width, width), 1)
    diagonal = jnp.where(down == across, raw_gram[...], 0.0)
    scale_row = jnp.sqrt(rows_total / (jnp.sum(diagonal, axis=0, keepdims=True) + 1e-06))
    scale_column = jnp.sqrt(rows_total / (jnp.sum(diagonal, axis=1, keepdims=True) + 1e-06))
    user_factor[...] = raw[...] * scale_row
    work[...] = raw_gram[...] * scale_column * scale_row * context_gram[...]
    invert(work)
    total = partial[user].astype(jnp.float32)
    for ahead in range(1, users):
        copies[ahead - 1].wait_recv()
        total = total + arrived[ahead - 1].astype(jnp.float32)
    item_raw = dot(total * scale_row, work[...])
    squares = jnp.sum(item_raw * item_raw, axis=0, keepdims=True)
    user_sums[user] = jnp.broadcast_to(squares, user_sums.shape[1:])
    first = send_all(
        "user", users, lambda peer, ahead: user_sums.at[user], lambda me, ahead: user_sums.at[me], user_sems
    )
    for copy in first:
        copy.wait_recv()
    item_sums[item] = jnp.sum(user_sums[...], axis=0)
    second = send_all(
        "item", items, lambda peer, ahead: item_sums.at[item], lambda me, ahead: item_sums.at[me], item_sems
    )
    for copy in second:
        copy.wait_recv()
    squares = jnp.sum(item_sums[...], axis=0)[:1]
    new_items[...] = item_raw * jnp.sqrt(rows_total / (squares + 1e-06))
    for copy in copies + first + second:
        copy.wait_send()


def update_items(partial, raw_gram, context_gram, raw, axis_sizes):
    users, items = axis_sizes
    _, rows, width = partial.shape
    out = jax.ShapeDtypeStruct((rows, width), jnp.float32)
    return pl.pallas_call(
        functools.partial(item_kernel, axis_sizes),
        out_shape=(out, out),
        in_specs=[VMEM_SPEC] * 4,
        out_specs=(VMEM_SPEC,) * 2,
        scratch_shapes=[
            pltpu.VMEM((users - 1, rows, width), jnp.bfloat16),
            pltpu.VMEM((width, width), jnp.float32),
            pltpu.VMEM((users, 8, width), jnp.float32),
            pltpu.VMEM((items, 8, width), jnp.float32),
            pltpu.SemaphoreType.DMA((2, users - 1)),
            pltpu.SemaphoreType.DMA((2, items - 1)),
            pltpu.SemaphoreType.DMA((2, users - 1)),
        ],
        compiler_params=pltpu.CompilerParams(
            collective_id=2, has_side_effects=True, vmem_limit_bytes=32 * 2**20
        ),
        name="update_items",
    )(partial, raw_gram, context_gram, raw)


def local(
    item_factor, context_factor, tile_count, tile_rows, tile_cols, tile_ctx, nz_offsets, nz_values
):
    axis_sizes = (lax.axis_size("user"), lax.axis_size("item"))
    users, items = axis_sizes
    rows, width = item_factor.shape
    count = tile_count.reshape(1)
    offsets = nz_offsets[0, 0]
    values = nz_values[0, 0]
    user_side = (tile_rows[0, 0], offsets[0])
    item_side = (tile_cols[0, 0], offsets[1])
    context_side = (tile_ctx[0, 0], offsets[2])
    item_rows, context, system, context_gram = gather_items(item_factor, context_factor, axis_sizes)
    context_tiles = context.reshape(-1, TILE, width)
    partial_users = mttkrp(
        count, user_side, item_side, context_side, values,
        item_rows.reshape(-1, TILE, width), context_tiles, items * rows // TILE,
    )
    raw, user_rows, raw_gram = update_users(
        partial_users.reshape(items, rows, width), system, axis_sizes
    )
    partial_items = mttkrp(
        count, item_side, user_side, context_side, values,
        user_rows.reshape(-1, TILE, width), context_tiles, users * rows // TILE,
    )
    new_items, user_factor = update_items(
        partial_items.reshape(users, rows, width), raw_gram, context_gram, raw, axis_sizes
    )
    return (user_factor, new_items)


def solution(mesh):
    in_specs = (
        P(("item", "user"), None),
        P(),
        P("user", "item"),
        P("user", "item", None),
        P("user", "item", None),
        P("user", "item", None),
        P("user", "item", None, None, None),
        P("user", "item", None, None),
    )
    out_specs = (P(("user", "item"), None), P(("item", "user"), None))
    return jax.shard_map(local, mesh=mesh, in_specs=in_specs, out_specs=out_specs, check_vma=False)
```

```python
import functools
import math

import jax
import jax.numpy as jnp
from jax import lax
from jax.experimental import pallas as pl
from jax.experimental.pallas import tpu as pltpu
from jax.sharding import PartitionSpec as P

TILE = 64
UNROLL = 32
PAIR = 2 * TILE
BLOCK = 64
PIVOTS = 4
HIGHEST = lax.Precision.HIGHEST
MESH = pl.DeviceIdType.MESH
VMEM_SPEC = pl.BlockSpec(memory_space=pltpu.VMEM)
SMEM_SPEC = pl.BlockSpec(memory_space=pltpu.SMEM)


def dot(left, right):
    return jnp.dot(left, right, precision=HIGHEST, preferred_element_type=jnp.float32)


def gram_of(columns):
    return lax.dot_general(
        columns,
        columns,
        (((1,), (1,)), ((), ())),
        precision=HIGHEST,
        preferred_element_type=jnp.float32,
    )


def mttkrp_kernel(
    target_at,
    count,
    target_ids,
    source_ids,
    context_ids,
    offsets,
    values,
    source,
    context,
    out,
    totals,
):
    totals[...] = jnp.zeros_like(totals)
    rank, entries = totals.shape[2], offsets.shape[2]

    def one_hot(row, extent):
        positions = lax.broadcasted_iota(jnp.int32, (extent, entries), 0)
        return jnp.where(positions == row, 1.0, 0.0).astype(jnp.bfloat16)

    def lanes_of(pair, row):
        wide = pair.astype(jnp.float32)
        picked = [
            jnp.take_along_axis(
                wide,
                jnp.broadcast_to(row[:, at : at + PAIR], (rank, PAIR)),
                axis=1,
                mode="promise_in_bounds",
            )
            for at in range(0, entries, PAIR)
        ]
        return jnp.concatenate(picked, axis=1)

    def group(step, carry):
        first = pl.multiple_of(step * UNROLL, UNROLL)
        targets = offsets[target_at, pl.ds(first, UNROLL), :]
        sources = offsets[1 - target_at, pl.ds(first, UNROLL), :]
        contexts = offsets[2, pl.ds(first, UNROLL), :]
        weights = values[pl.ds(first, UNROLL), :]
        for at in range(UNROLL):
            row = slice(at, at + 1)
            source_id, context_id = source_ids[first + at], context_ids[first + at]
            source_row = sources[row] + TILE * lax.rem(source_id, 2)
            context_row = contexts[row] + TILE * lax.rem(context_id, 2)
            source_part = jnp.dot(
                source[lax.div(source_id, 2)],
                one_hot(source_row, PAIR),
                preferred_element_type=jnp.float32,
            )
            context_part = lanes_of(context[lax.div(context_id, 2)], context_row)
            weight = jnp.where(first + at < count[0], weights[row], 0.0)
            terms = (weight * source_part * context_part).astype(jnp.bfloat16)
            totals[target_ids[first + at]] += lax.dot_general(
                one_hot(targets[row], TILE),
                terms,
                (((1,), (1,)), ((), ())),
                preferred_element_type=jnp.float32,
            )
        return carry

    lax.fori_loop(0, (count[0] + UNROLL - 1) // UNROLL, group, 0)
    out[...] = totals[...].astype(out.dtype)


def mttkrp(target_at, count, ids, offsets, values, source_pairs, context_pairs, tiles):
    shape = (tiles, TILE, source_pairs.shape[1])
    return pl.pallas_call(
        functools.partial(mttkrp_kernel, target_at),
        out_shape=jax.ShapeDtypeStruct(shape, jnp.bfloat16),
        in_specs=[SMEM_SPEC] * 4 + [VMEM_SPEC] * 4,
        out_specs=VMEM_SPEC,
        scratch_shapes=[pltpu.VMEM(shape, jnp.float32)],
        compiler_params=pltpu.CompilerParams(vmem_limit_bytes=48 * 2**20),
        name="mttkrp",
    )(
        count,
        ids[target_at],
        ids[1 - target_at],
        ids[2],
        offsets,
        values,
        source_pairs,
        context_pairs,
    )


def greet(groups):
    barrier = pltpu.get_barrier_semaphore()
    total = 0
    for axis, size in groups:
        me = lax.axis_index(axis)
        for ahead in range(1, size):
            pl.semaphore_signal(
                barrier, inc=1, device_id={axis: lax.rem(me + ahead, size)}, device_id_type=MESH
            )
        total += size - 1
    pl.semaphore_wait(barrier, total)


def send_all(axis, size, source, target, sems):
    me = lax.axis_index(axis)
    copies = []
    for ahead in range(1, size):
        peer = lax.rem(me + ahead, size)
        copy = pltpu.make_async_remote_copy(
            src_ref=source(peer, ahead),
            dst_ref=target(me, ahead),
            send_sem=sems.at[0, ahead - 1],
            recv_sem=sems.at[1, ahead - 1],
            device_id={axis: peer},
            device_id_type=MESH,
        )
        copy.start()
        copies.append(copy)
    return copies


def copy_to(source, target, sems, user, item):
    copy = pltpu.make_async_remote_copy(
        src_ref=source,
        dst_ref=target,
        send_sem=sems.at[0],
        recv_sem=sems.at[1],
        device_id=(user, item),
        device_id_type=MESH,
    )
    copy.start()
    return copy


def receive(copies):
    for copy in copies:
        copy.wait_recv()


def rows_of(item, rows):
    return pl.ds(pl.multiple_of(item * rows, rows), rows)


def start_gram_sum(gram, scattered, sems, items):
    rows = scattered.shape[1]
    item = lax.axis_index("item")
    scattered[item] = gram[rows_of(item, rows), :]
    return send_all(
        "item",
        items,
        lambda peer, ahead: gram.at[rows_of(peer, rows)],
        lambda me, ahead: scattered.at[me],
        sems,
    )


def pass_gram_sum(first, scattered, summed, sems, users):
    receive(first)
    user = lax.axis_index("user")
    summed[user] = jnp.sum(scattered[...], axis=0)
    return send_all(
        "user", users, lambda peer, ahead: summed.at[user], lambda me, ahead: summed.at[me], sems
    )


def spread_gram(result, own, sems, items):
    rows = own.shape[0]
    span = rows_of(lax.axis_index("item"), rows)
    result[span, :] = own[...]
    return send_all("item", items, lambda peer, ahead: own, lambda me, ahead: result.at[span], sems)


def gram_scratch(axis_sizes, width):
    users, items = axis_sizes
    rows = width // items
    return [
        pltpu.VMEM((width, width), jnp.float32),
        pltpu.VMEM((items, rows, width), jnp.float32),
        pltpu.VMEM((users, rows, width), jnp.float32),
        pltpu.SemaphoreType.DMA((2, items - 1)),
        pltpu.SemaphoreType.DMA((2, users - 1)),
        pltpu.SemaphoreType.DMA((2, items - 1)),
    ]


def small_inverse(matrix):
    size = len(matrix)
    if size == 2:
        (first, off), (_, last) = matrix
        scale = 1.0 / (first * last - off * off)
        cross = -off * scale
        return [[last * scale, cross], [cross, first * scale]]
    half = size // 2

    def product(left, right):
        return [
            [sum(left[i][k] * right[k][j] for k in range(1, half)) + left[i][0] * right[0][j] for j in range(half)]
            for i in range(half)
        ]

    corner = small_inverse([row[:half] for row in matrix[:half]])
    side = [row[half:] for row in matrix[:half]]
    solved = product(corner, side)
    lowered = product([list(column) for column in zip(*side)], solved)
    rest = small_inverse(
        [[matrix[half + i][half + j] - lowered[i][j] for j in range(half)] for i in range(half)]
    )
    spread = product(solved, rest)
    update = product(spread, [list(column) for column in zip(*solved)])
    top = [
        [corner[i][j] + update[i][j] for j in range(half)] + [-spread[i][j] for j in range(half)]
        for i in range(half)
    ]
    bottom = [[-spread[j][i] for j in range(half)] + rest[i] for i in range(half)]
    return top + bottom


def invert(work, first_block, last_block):
    width = work.shape[0]
    down = lax.broadcasted_iota(jnp.int32, (BLOCK, BLOCK), 0)
    across = lax.broadcasted_iota(jnp.int32, (BLOCK, BLOCK), 1)
    lanes = lax.broadcasted_iota(jnp.int32, (BLOCK, width), 1) // BLOCK
    rows = lax.broadcasted_iota(jnp.int32, (width, BLOCK), 0) // BLOCK
    full_lanes = lax.broadcasted_iota(jnp.int32, (width, width), 1) // BLOCK
    steps = range(PIVOTS)
    for block in range(first_block, last_block):
        span = slice(block * BLOCK, (block + 1) * BLOCK)
        pivot = work[span, span]
        for at in range(0, BLOCK, PIVOTS):
            columns = [
                jnp.broadcast_to(pivot[:, at + i : at + i + 1], (BLOCK, BLOCK)) for i in steps
            ]
            inverse = small_inverse(
                [
                    [columns[max(i, j)][at + min(i, j) : at + min(i, j) + 1, :] for j in steps]
                    for i in steps
                ]
            )
            fresh = []
            for i in steps:
                row = inverse[i][0] * pivot[at : at + 1, :]
                for j in steps[1:]:
                    row = row + inverse[i][j] * pivot[at + j : at + j + 1, :]
                for j in steps:
                    row = jnp.where(across[:1] == at + j, inverse[i][j], row)
                fresh.append(row)
            after = jnp.where((across >= at) & (across < at + PIVOTS), 0.0, pivot)
            for i in steps:
                after = after - columns[i] * fresh[i]
            for i in steps:
                after = jnp.where(down == at + i, fresh[i], after)
            pivot = after
        panel = dot(pivot, work[span, :])
        panel = jnp.where(lanes == block, jnp.concatenate([pivot] * (width // BLOCK), axis=1), panel)
        column = jnp.where(rows == block, 0.0, work[:, span])
        kept = jnp.where(full_lanes == block, 0.0, work[...])
        work[...] = kept - dot(column, panel)
        work[span, :] = panel


def gather_kernel(
    axis_sizes, step_rows, item_factor, context_factor, items, context, gram_rows, context_gram,
    loaded, gram, scattered, summed, sum_sems, pass_sems, spread_sems, load_sems, own_sems, sibling_sems
):
    users, items_extent = axis_sizes
    user, item = lax.axis_index("user"), lax.axis_index("item")
    steps = context_factor.shape[0] // step_rows
    pairs = step_rows // PAIR

    def load(step):
        span = pl.ds(pl.multiple_of(step * step_rows, step_rows), step_rows)
        return pltpu.make_async_copy(context_factor.at[span], loaded.at[step], load_sems.at[step])

    def transform(step, carry):
        load(step).wait()
        chunk = loaded[step]
        columns = chunk.T
        for pair in range(pairs):
            context[step * pairs + pair] = columns[:, pair * PAIR : (pair + 1) * PAIR].astype(
                jnp.bfloat16
            )
        context_gram[...] += gram_of(columns)
        return carry

    for step in range(steps):
        load(step).start()
    context_gram[...] = jnp.zeros_like(context_gram)
    columns = item_factor[...].T
    for pair in range(items.shape[1]):
        items[user, pair] = columns[:, pair * PAIR : (pair + 1) * PAIR].astype(jnp.bfloat16)
    gram[...] = gram_of(columns)
    greet((("user", users), ("item", items_extent)))
    core = lax.rem(user, 2)
    sibling = user + 1 - 2 * core
    first = start_gram_sum(gram, scattered, sum_sems, items_extent)
    own = []
    for at, ahead in enumerate(range(2, users, 2)):
        peer = lax.rem(user + ahead, users)
        own.append(copy_to(items.at[user], items.at[user], own_sems.at[at], peer, item))
    forwarded = [copy_to(items.at[user], items.at[user], sibling_sems.at[0], sibling, item)]
    lax.fori_loop(0, steps // 2, transform, 0)
    for at, ahead in enumerate(range(2, users, 2)):
        own[at].wait_recv()
        block = items.at[lax.rem(user + users - ahead, users)]
        forwarded.append(copy_to(block, block, sibling_sems.at[1 + at], sibling, item))
    second = pass_gram_sum(first, scattered, summed, pass_sems, users)
    lax.fori_loop(steps // 2, steps, transform, 0)
    receive(second)
    gram_rows[...] = jnp.sum(summed[...], axis=0)
    receive(forwarded)
    for copy in first + own + forwarded + second:
        copy.wait_send()


def gather_items(item_factor, context_factor, axis_sizes):
    users, items = axis_sizes
    rows, width = item_factor.shape
    contexts = context_factor.shape[0]
    step_rows = 512
    gram, scattered, summed, sum_sems, pass_sems, spread_sems = gram_scratch(axis_sizes, width)
    return pl.pallas_call(
        functools.partial(gather_kernel, axis_sizes, step_rows),
        out_shape=(
            jax.ShapeDtypeStruct((users, rows // PAIR, width, PAIR), jnp.bfloat16),
            jax.ShapeDtypeStruct((contexts // PAIR, width, PAIR), jnp.bfloat16),
            jax.ShapeDtypeStruct((width // items, width), jnp.float32),
            jax.ShapeDtypeStruct((width, width), jnp.float32),
        ),
        in_specs=[VMEM_SPEC, pl.BlockSpec(memory_space=pl.ANY)],
        out_specs=(VMEM_SPEC,) * 4,
        scratch_shapes=[
            pltpu.VMEM((contexts // step_rows, step_rows, width), jnp.float32),
            gram, scattered, summed, sum_sems, pass_sems, spread_sems,
            pltpu.SemaphoreType.DMA((contexts // step_rows,)),
            pltpu.SemaphoreType.DMA((users // 2 - 1, 2)),
            pltpu.SemaphoreType.DMA((users // 2, 2)),
        ],
        compiler_params=pltpu.CompilerParams(
            collective_id=0, has_side_effects=True, vmem_limit_bytes=32 * 2**20
        ),
        name="gather_items",
    )(item_factor, context_factor)


def user_kernel(
    axis_sizes, side, partial, gram_rows, context_gram, raw, gathered, raw_gram, arrived, mixed, settled,
    work, gram, scattered, summed, sum_sems, pass_sems, spread_sems, far_sems, near_sems, out_sems, on_sems,
    system_sems, gram_block,
):
    users, items = axis_sizes
    user, item = lax.axis_index("user"), lax.axis_index("item")
    slow, fast = item // side, lax.rem(item, side)
    half = partial.shape[2] // 2
    hops = (2, 1, 3)
    blocks = work.shape[0] // BLOCK
    greet((("user", users), ("item", items)))
    system = spread_gram(work, gram_rows, system_sems, items)

    def at_slow(ahead):
        return lax.rem(slow + ahead, side) * side + fast

    def at_fast(ahead):
        return slow * side + lax.rem(fast + ahead, side)

    far = []
    for ahead in hops:
        far.append(
            copy_to(
                partial.at[lax.rem(slow + ahead, side), :, pl.ds(0, half)],
                arrived.at[0, ahead - 1],
                far_sems.at[0, ahead - 1],
                user,
                at_slow(ahead),
            )
        )
        far.append(
            copy_to(
                partial.at[:, lax.rem(fast + ahead, side), pl.ds(half, half)],
                arrived.at[1, ahead - 1],
                far_sems.at[1, ahead - 1],
                user,
                at_fast(ahead),
            )
        )
    receive(system)
    work[...] = work[...] * context_gram[...]
    invert(work, 0, blocks // 2)

    def combine(part, where):
        own = partial[slow, where, :half] if part == 0 else partial[where, fast, half:]
        total = own.astype(jnp.float32)
        for ahead in range(side - 1):
            total = total + arrived[part, ahead, where].astype(jnp.float32)
        return total

    near = []
    kept = []
    for part in range(2):
        receive(far[part::2])
        here = fast if part == 0 else slow
        for ahead in hops:
            where = lax.rem(here + ahead, side)
            mixed[part, ahead - 1] = combine(part, where)
            near.append(
                copy_to(
                    mixed.at[part, ahead - 1],
                    settled.at[part, ahead - 1],
                    near_sems.at[part, ahead - 1],
                    user,
                    at_fast(ahead) if part == 0 else at_slow(ahead),
                )
            )
        kept.append(combine(part, here))
    invert(work, blocks // 2, blocks)
    receive(near)
    total = jnp.concatenate(
        [kept[part] + jnp.sum(settled[part], axis=0) for part in range(2)], axis=0
    )
    raw[...] = dot(total, work[...])
    columns = raw[...].T
    for part in range(2):
        gathered[item, part] = columns[:, part * PAIR : (part + 1) * PAIR].astype(jnp.bfloat16)

    onward = []

    def pass_on(block, part, stage):
        for ahead in hops:
            onward.append(
                copy_to(
                    gathered.at[block, part],
                    gathered.at[block, part],
                    on_sems.at[part, stage, ahead - 1],
                    user,
                    at_fast(ahead) if part == 0 else at_slow(ahead),
                )
            )

    outward = []
    for ahead in hops:
        for part in range(2):
            outward.append(
                copy_to(
                    gathered.at[item, part],
                    gathered.at[item, part],
                    out_sems.at[part, ahead - 1],
                    user,
                    at_slow(ahead) if part == 0 else at_fast(ahead),
                )
            )
    gram[...] = gram_of(columns)
    first = start_gram_sum(gram, scattered, sum_sems, items)
    for part in range(2):
        pass_on(item, part, 0)
    for at, ahead in ((1, 1), (2, 3), (0, 2)):
        for part in range(2):
            outward[2 * at + part].wait_recv()
            back = side - ahead
            pass_on(at_slow(back) if part == 0 else at_fast(back), part, ahead)
    second = pass_gram_sum(first, scattered, summed, pass_sems, users)
    receive(second)
    gram_block[...] = jnp.sum(summed[...], axis=0)
    third = spread_gram(raw_gram, gram_block, spread_sems, items)
    receive(onward)
    receive(third)
    for copy in system + far + near + outward + onward + first + second + third:
        copy.wait_send()


def update_users(partial, gram_rows, context_gram, axis_sizes):
    users, items = axis_sizes
    side, _, rows, width = partial.shape
    half = rows // 2
    square = jax.ShapeDtypeStruct((width, width), jnp.float32)
    return pl.pallas_call(
        functools.partial(user_kernel, axis_sizes, side),
        out_shape=(
            jax.ShapeDtypeStruct((rows, width), jnp.float32),
            jax.ShapeDtypeStruct((items, rows // PAIR, width, PAIR), jnp.bfloat16),
            square,
        ),
        in_specs=[VMEM_SPEC] * 3,
        out_specs=(VMEM_SPEC,) * 3,
        scratch_shapes=[
            pltpu.VMEM((2, side - 1, side, half, width), jnp.bfloat16),
            pltpu.VMEM((2, side - 1, half, width), jnp.float32),
            pltpu.VMEM((2, side - 1, half, width), jnp.float32),
            pltpu.VMEM((width, width), jnp.float32),
        ]
        + gram_scratch(axis_sizes, width)
        + [
            pltpu.SemaphoreType.DMA((2, side - 1, 2)),
            pltpu.SemaphoreType.DMA((2, side - 1, 2)),
            pltpu.SemaphoreType.DMA((2, side - 1, 2)),
            pltpu.SemaphoreType.DMA((2, side, side - 1, 2)),
            pltpu.SemaphoreType.DMA((2, items - 1)),
            pltpu.VMEM((width // items, width), jnp.float32),
        ],
        compiler_params=pltpu.CompilerParams(
            collective_id=1, has_side_effects=True, vmem_limit_bytes=40 * 2**20
        ),
        name="update_users",
    )(partial, gram_rows, context_gram)


def item_kernel(
    axis_sizes, partial, raw_gram, context_gram, raw, new_items, user_factor, arrived, work,
    user_sums, item_sums, user_sems, item_sems, sems
):
    users, items = axis_sizes
    user, item = lax.axis_index("user"), lax.axis_index("item")
    greet((("user", users), ("item", items)))
    copies = send_all(
        "user",
        users,
        lambda peer, ahead: partial.at[peer],
        lambda me, ahead: arrived.at[ahead - 1],
        sems,
    )
    width = work.shape[0]
    rows_total = jnp.float32(user_factor.shape[0] * users * items)
    down = lax.broadcasted_iota(jnp.int32, (width, width), 0)
    across = lax.broadcasted_iota(jnp.int32, (width, width), 1)
    diagonal = jnp.where(down == across, raw_gram[...], 0.0)
    scale_row = jnp.sqrt(rows_total / (jnp.sum(diagonal, axis=0, keepdims=True) + 1e-06))
    scale_column = jnp.sqrt(rows_total / (jnp.sum(diagonal, axis=1, keepdims=True) + 1e-06))
    user_factor[...] = raw[...] * scale_row
    work[...] = raw_gram[...] * scale_column * scale_row * context_gram[...]
    invert(work, 0, width // BLOCK)
    total = partial[user].astype(jnp.float32)
    for ahead in range(1, users):
        copies[ahead - 1].wait_recv()
        total = total + arrived[ahead - 1].astype(jnp.float32)
    item_raw = dot(total * scale_row, work[...])
    squares = jnp.sum(item_raw * item_raw, axis=0, keepdims=True)
    user_sums[user] = jnp.broadcast_to(squares, user_sums.shape[1:])
    first = send_all(
        "user", users, lambda peer, ahead: user_sums.at[user], lambda me, ahead: user_sums.at[me], user_sems
    )
    receive(first)
    item_sums[item] = jnp.sum(user_sums[...], axis=0)
    second = send_all(
        "item", items, lambda peer, ahead: item_sums.at[item], lambda me, ahead: item_sums.at[me], item_sems
    )
    receive(second)
    squares = jnp.sum(item_sums[...], axis=0)[:1]
    new_items[...] = item_raw * jnp.sqrt(rows_total / (squares + 1e-06))
    for copy in copies + first + second:
        copy.wait_send()


def update_items(partial, raw_gram, context_gram, raw, axis_sizes):
    users, items = axis_sizes
    _, rows, width = partial.shape
    out = jax.ShapeDtypeStruct((rows, width), jnp.float32)
    return pl.pallas_call(
        functools.partial(item_kernel, axis_sizes),
        out_shape=(out, out),
        in_specs=[VMEM_SPEC] * 4,
        out_specs=(VMEM_SPEC,) * 2,
        scratch_shapes=[
            pltpu.VMEM((users - 1, rows, width), jnp.bfloat16),
            pltpu.VMEM((width, width), jnp.float32),
            pltpu.VMEM((users, 8, width), jnp.float32),
            pltpu.VMEM((items, 8, width), jnp.float32),
            pltpu.SemaphoreType.DMA((2, users - 1)),
            pltpu.SemaphoreType.DMA((2, items - 1)),
            pltpu.SemaphoreType.DMA((2, users - 1)),
        ],
        compiler_params=pltpu.CompilerParams(
            collective_id=2, has_side_effects=True, vmem_limit_bytes=32 * 2**20
        ),
        name="update_items",
    )(partial, raw_gram, context_gram, raw)


def local(
    item_factor, context_factor, tile_count, tile_rows, tile_cols, tile_ctx, nz_offsets, nz_values
):
    axis_sizes = (lax.axis_size("user"), lax.axis_size("item"))
    users, items = axis_sizes
    rows, width = item_factor.shape
    side = math.isqrt(items)
    count = tile_count.reshape(1)
    ids = (tile_rows[0, 0], tile_cols[0, 0], tile_ctx[0, 0])
    offsets = nz_offsets[0, 0]
    values = nz_values[0, 0]
    item_pairs, context_pairs, gram_rows, context_gram = gather_items(
        item_factor, context_factor, axis_sizes
    )
    partial_users = mttkrp(
        0, count, ids, offsets, values, item_pairs.reshape(-1, width, PAIR), context_pairs,
        items * rows // TILE,
    )
    raw, user_pairs, raw_gram = update_users(
        partial_users.reshape(side, side, rows, width), gram_rows, context_gram, axis_sizes
    )
    partial_items = mttkrp(
        1, count, ids, offsets, values, user_pairs.reshape(-1, width, PAIR), context_pairs,
        users * rows // TILE,
    )
    new_items, user_factor = update_items(
        partial_items.reshape(users, rows, width), raw_gram, context_gram, raw, axis_sizes
    )
    return (user_factor, new_items)


def solution(mesh):
    in_specs = (
        P(("item", "user"), None),
        P(),
        P("user", "item"),
        P("user", "item", None),
        P("user", "item", None),
        P("user", "item", None),
        P("user", "item", None, None, None),
        P("user", "item", None, None),
    )
    out_specs = (P(("user", "item"), None), P(("item", "user"), None))
    return jax.shard_map(local, mesh=mesh, in_specs=in_specs, out_specs=out_specs, check_vma=False)
```

```python
import functools
import math

import jax
import jax.numpy as jnp
from jax import lax
from jax.experimental import pallas as pl
from jax.experimental.pallas import tpu as pltpu
from jax.sharding import PartitionSpec as P

TILE = 64
UNROLL = 32
PAIR = 2 * TILE
BLOCK = 64
PIVOTS = 4
HIGHEST = lax.Precision.HIGHEST
MESH = pl.DeviceIdType.MESH
VMEM_SPEC = pl.BlockSpec(memory_space=pltpu.VMEM)
SMEM_SPEC = pl.BlockSpec(memory_space=pltpu.SMEM)


def dot(left, right):
    return jnp.dot(left, right, precision=HIGHEST, preferred_element_type=jnp.float32)


def gram_of(columns):
    return lax.dot_general(
        columns,
        columns,
        (((1,), (1,)), ((), ())),
        precision=HIGHEST,
        preferred_element_type=jnp.float32,
    )


def mttkrp_kernel(
    target_at,
    count,
    target_ids,
    source_ids,
    context_ids,
    offsets,
    values,
    source,
    context,
    out,
    totals,
):
    totals[...] = jnp.zeros_like(totals)
    rank, entries = totals.shape[2], offsets.shape[2]

    def one_hot(row, extent):
        positions = lax.broadcasted_iota(jnp.int32, (extent, entries), 0)
        return jnp.where(positions == row, 1.0, 0.0).astype(jnp.bfloat16)

    def lanes_of(pair, row):
        wide = pair.astype(jnp.float32)
        picked = [
            jnp.take_along_axis(
                wide,
                jnp.broadcast_to(row[:, at : at + PAIR], (rank, PAIR)),
                axis=1,
                mode="promise_in_bounds",
            )
            for at in range(0, entries, PAIR)
        ]
        return jnp.concatenate(picked, axis=1)

    def group(step, carry):
        first = pl.multiple_of(step * UNROLL, UNROLL)
        targets = offsets[target_at, pl.ds(first, UNROLL), :]
        sources = offsets[1 - target_at, pl.ds(first, UNROLL), :]
        contexts = offsets[2, pl.ds(first, UNROLL), :]
        weights = values[pl.ds(first, UNROLL), :]
        for at in range(UNROLL):
            row = slice(at, at + 1)
            source_id, context_id = source_ids[first + at], context_ids[first + at]
            source_row = sources[row] + TILE * lax.rem(source_id, 2)
            context_row = contexts[row] + TILE * lax.rem(context_id, 2)
            source_part = jnp.dot(
                source[lax.div(source_id, 2)],
                one_hot(source_row, PAIR),
                preferred_element_type=jnp.float32,
            )
            context_part = lanes_of(context[lax.div(context_id, 2)], context_row)
            weight = jnp.where(first + at < count[0], weights[row], 0.0)
            terms = (weight * source_part * context_part).astype(jnp.bfloat16)
            totals[target_ids[first + at]] += lax.dot_general(
                one_hot(targets[row], TILE),
                terms,
                (((1,), (1,)), ((), ())),
                preferred_element_type=jnp.float32,
            )
        return carry

    lax.fori_loop(0, (count[0] + UNROLL - 1) // UNROLL, group, 0)
    out[...] = totals[...].astype(out.dtype)


def mttkrp(target_at, count, ids, offsets, values, source_pairs, context_pairs, tiles):
    shape = (tiles, TILE, source_pairs.shape[1])
    return pl.pallas_call(
        functools.partial(mttkrp_kernel, target_at),
        out_shape=jax.ShapeDtypeStruct(shape, jnp.bfloat16),
        in_specs=[SMEM_SPEC] * 4 + [VMEM_SPEC] * 4,
        out_specs=VMEM_SPEC,
        scratch_shapes=[pltpu.VMEM(shape, jnp.float32)],
        compiler_params=pltpu.CompilerParams(vmem_limit_bytes=24 * 2**20),
        name="mttkrp",
    )(
        count,
        ids[target_at],
        ids[1 - target_at],
        ids[2],
        offsets,
        values,
        source_pairs,
        context_pairs,
    )


def greet(groups):
    barrier = pltpu.get_barrier_semaphore()
    for axis, size in groups:
        me = lax.axis_index(axis)
        for ahead in range(1, size):
            pl.semaphore_signal(
                barrier, inc=1, device_id={axis: lax.rem(me + ahead, size)}, device_id_type=MESH
            )


def await_greetings(groups):
    pl.semaphore_wait(pltpu.get_barrier_semaphore(), sum(size - 1 for _, size in groups))


def send_all(axis, size, source, target, sems):
    me = lax.axis_index(axis)
    copies = []
    for ahead in range(1, size):
        peer = lax.rem(me + ahead, size)
        copy = pltpu.make_async_remote_copy(
            src_ref=source(peer, ahead),
            dst_ref=target(me, ahead),
            send_sem=sems.at[0, ahead - 1],
            recv_sem=sems.at[1, ahead - 1],
            device_id={axis: peer},
            device_id_type=MESH,
        )
        copy.start()
        copies.append(copy)
    return copies


def copy_to(source, target, sems, user, item):
    copy = pltpu.make_async_remote_copy(
        src_ref=source,
        dst_ref=target,
        send_sem=sems.at[0],
        recv_sem=sems.at[1],
        device_id=(user, item),
        device_id_type=MESH,
    )
    copy.start()
    return copy


def receive(copies):
    for copy in copies:
        copy.wait_recv()


def rows_of(item, rows):
    return pl.ds(pl.multiple_of(item * rows, rows), rows)


def gram_to_users(gram, by_user, sems, users):
    rows = by_user.shape[1]
    user = lax.axis_index("user")
    by_user[user] = gram[rows_of(user, rows), :]
    return send_all(
        "user",
        users,
        lambda peer, ahead: gram.at[rows_of(peer, rows)],
        lambda me, ahead: by_user.at[me],
        sems,
    )


def gram_to_items(first, by_user, pieces, by_item, sems, items):
    receive(first)
    block = jnp.sum(by_user[...], axis=0)
    count = pieces.shape[0]
    for piece in range(count):
        pieces[piece] = piece_of(block, piece)
    item = lax.axis_index("item")
    by_item[item] = pieces[lax.rem(item, count)]
    return send_all(
        "item",
        items,
        lambda peer, ahead: pieces.at[lax.rem(peer, count)],
        lambda me, ahead: by_item.at[me],
        sems,
    )


def piece_of(block, piece):
    down, across = 8 * (piece // 2), 128 * (piece % 2)
    return block[down : down + 8, across : across + 128]


def pieces_back(own, finished, sems):
    count = finished.shape[0]
    user, item = lax.axis_index("user"), lax.axis_index("item")
    at = lax.rem(item, count)
    finished[at] = own[...]
    return [
        copy_to(
            own,
            finished.at[at],
            sems.at[ahead - 1],
            user,
            item - at + lax.rem(at + ahead, count),
        )
        for ahead in range(1, count)
    ]


def blocks_back(third, finished, block, result, sems, users):
    receive(third)
    for piece in range(finished.shape[0]):
        down, across = 8 * (piece // 2), 128 * (piece % 2)
        block[down : down + 8, across : across + 128] = finished[piece]
    rows = block.shape[0]
    span = rows_of(lax.axis_index("user"), rows)
    result[span, :] = block[...]
    return send_all("user", users, lambda peer, ahead: block, lambda me, ahead: result.at[span], sems)


def gram_sum_scratch(axis_sizes, width):
    users, items = axis_sizes
    rows = width // users
    return [
        pltpu.VMEM((width, width), jnp.float32),
        pltpu.VMEM((users, rows, width), jnp.float32),
        pltpu.VMEM((rows * width // 1024, 8, 128), jnp.float32),
        pltpu.VMEM((items, 8, 128), jnp.float32),
        pltpu.SemaphoreType.DMA((2, users - 1)),
        pltpu.SemaphoreType.DMA((2, items - 1)),
    ]


def gram_spread_scratch(axis_sizes, width):
    users, items = axis_sizes
    rows = width // users
    count = rows * width // 1024
    return [
        pltpu.VMEM((count, 8, 128), jnp.float32),
        pltpu.VMEM((rows, width), jnp.float32),
        pltpu.SemaphoreType.DMA((count - 1, 2)),
        pltpu.SemaphoreType.DMA((2, users - 1)),
    ]


def small_inverse(matrix):
    size = len(matrix)
    if size == 2:
        (first, off), (_, last) = matrix
        scale = 1.0 / (first * last - off * off)
        cross = -off * scale
        return [[last * scale, cross], [cross, first * scale]]
    half = size // 2

    def product(left, right):
        return [
            [sum(left[i][k] * right[k][j] for k in range(1, half)) + left[i][0] * right[0][j] for j in range(half)]
            for i in range(half)
        ]

    corner = small_inverse([row[:half] for row in matrix[:half]])
    side = [row[half:] for row in matrix[:half]]
    solved = product(corner, side)
    lowered = product([list(column) for column in zip(*side)], solved)
    rest = small_inverse(
        [[matrix[half + i][half + j] - lowered[i][j] for j in range(half)] for i in range(half)]
    )
    spread = product(solved, rest)
    update = product(spread, [list(column) for column in zip(*solved)])
    top = [
        [corner[i][j] + update[i][j] for j in range(half)] + [-spread[i][j] for j in range(half)]
        for i in range(half)
    ]
    bottom = [[-spread[j][i] for j in range(half)] + rest[i] for i in range(half)]
    return top + bottom


def invert(work, first_block, last_block):
    width = work.shape[0]
    down = lax.broadcasted_iota(jnp.int32, (BLOCK, BLOCK), 0)
    across = lax.broadcasted_iota(jnp.int32, (BLOCK, BLOCK), 1)
    lanes = lax.broadcasted_iota(jnp.int32, (BLOCK, width), 1) // BLOCK
    rows = lax.broadcasted_iota(jnp.int32, (width, BLOCK), 0) // BLOCK
    full_lanes = lax.broadcasted_iota(jnp.int32, (width, width), 1) // BLOCK
    steps = range(PIVOTS)
    for block in range(first_block, last_block):
        span = slice(block * BLOCK, (block + 1) * BLOCK)
        pivot = work[span, span]
        for at in range(0, BLOCK, PIVOTS):
            columns = [
                jnp.broadcast_to(pivot[:, at + i : at + i + 1], (BLOCK, BLOCK)) for i in steps
            ]
            inverse = small_inverse(
                [
                    [columns[max(i, j)][at + min(i, j) : at + min(i, j) + 1, :] for j in steps]
                    for i in steps
                ]
            )
            fresh = []
            for i in steps:
                row = inverse[i][0] * pivot[at : at + 1, :]
                for j in steps[1:]:
                    row = row + inverse[i][j] * pivot[at + j : at + j + 1, :]
                for j in steps:
                    row = jnp.where(across[:1] == at + j, inverse[i][j], row)
                fresh.append(row)
            after = jnp.where((across >= at) & (across < at + PIVOTS), 0.0, pivot)
            for i in steps:
                after = after - columns[i] * fresh[i]
            for i in steps:
                after = jnp.where(down == at + i, fresh[i], after)
            pivot = after
        panel = dot(pivot, work[span, :])
        panel = jnp.where(lanes == block, jnp.concatenate([pivot] * (width // BLOCK), axis=1), panel)
        column = jnp.where(rows == block, 0.0, work[:, span])
        kept = jnp.where(full_lanes == block, 0.0, work[...])
        work[...] = kept - dot(column, panel)
        work[span, :] = panel


def gather_kernel(
    axis_sizes, step_rows, item_factor, context_factor, items, context, gram_piece, context_gram,
    loaded, load_sems, own_sems, sibling_sems, gram, by_user, pieces, by_item, user_sems, item_sems,
):
    users, items_extent = axis_sizes
    everyone = (("user", users), ("item", items_extent))
    user, item = lax.axis_index("user"), lax.axis_index("item")
    steps = context_factor.shape[0] // step_rows
    pairs = step_rows // PAIR
    greet(everyone)

    def load(step):
        span = pl.ds(pl.multiple_of(step * step_rows, step_rows), step_rows)
        return pltpu.make_async_copy(context_factor.at[span], loaded.at[step], load_sems.at[step])

    def transform(step, carry):
        load(step).wait()
        chunk = loaded[step]
        columns = chunk.T
        for pair in range(pairs):
            context[step * pairs + pair] = columns[:, pair * PAIR : (pair + 1) * PAIR].astype(
                jnp.bfloat16
            )
        context_gram[...] += gram_of(columns)
        return carry

    for step in range(steps):
        load(step).start()
    context_gram[...] = jnp.zeros_like(context_gram)
    columns = item_factor[...].T
    for pair in range(items.shape[1]):
        items[user, pair] = columns[:, pair * PAIR : (pair + 1) * PAIR].astype(jnp.bfloat16)
    gram[...] = gram_of(columns)
    await_greetings(everyone)
    core = lax.rem(user, 2)
    sibling = user + 1 - 2 * core
    own = []
    for at, ahead in enumerate(range(2, users, 2)):
        peer = lax.rem(user + ahead, users)
        own.append(copy_to(items.at[user], items.at[user], own_sems.at[at], peer, item))
    forwarded = [copy_to(items.at[user], items.at[user], sibling_sems.at[0], sibling, item)]
    first = gram_to_users(gram, by_user, user_sems, users)
    lax.fori_loop(0, steps // 4, transform, 0)
    for at, ahead in enumerate(range(2, users, 2)):
        own[at].wait_recv()
        block = items.at[lax.rem(user + users - ahead, users)]
        forwarded.append(copy_to(block, block, sibling_sems.at[1 + at], sibling, item))
    second = gram_to_items(first, by_user, pieces, by_item, item_sems, items_extent)
    lax.fori_loop(steps // 4, steps, transform, 0)
    receive(second)
    gram_piece[...] = jnp.sum(by_item[...], axis=0)
    receive(forwarded)
    for copy in first + own + forwarded + second:
        copy.wait_send()


def gather_items(item_factor, context_factor, axis_sizes):
    users, items = axis_sizes
    rows, width = item_factor.shape
    contexts = context_factor.shape[0]
    step_rows = 512
    return pl.pallas_call(
        functools.partial(gather_kernel, axis_sizes, step_rows),
        out_shape=(
            jax.ShapeDtypeStruct((users, rows // PAIR, width, PAIR), jnp.bfloat16),
            jax.ShapeDtypeStruct((contexts // PAIR, width, PAIR), jnp.bfloat16),
            jax.ShapeDtypeStruct((8, 128), jnp.float32),
            jax.ShapeDtypeStruct((width, width), jnp.float32),
        ),
        in_specs=[VMEM_SPEC, pl.BlockSpec(memory_space=pltpu.HBM)],
        out_specs=(VMEM_SPEC,) * 4,
        scratch_shapes=[
            pltpu.VMEM((contexts // step_rows, step_rows, width), jnp.float32),
            pltpu.SemaphoreType.DMA((contexts // step_rows,)),
            pltpu.SemaphoreType.DMA((users // 2 - 1, 2)),
            pltpu.SemaphoreType.DMA((users // 2, 2)),
        ]
        + gram_sum_scratch(axis_sizes, width),
        compiler_params=pltpu.CompilerParams(
            collective_id=0, has_side_effects=True, vmem_limit_bytes=16 * 2**20
        ),
        name="gather_items",
    )(item_factor, context_factor)


def user_kernel(
    axis_sizes, side, partial, gram_piece, context_gram, raw, gathered, raw_gram, arrived, mixed, settled,
    work, raw_piece, far_sems, near_sems, out_sems, on_sems,
    gram, by_user, pieces, by_item, user_sems, item_sems,
    finished, gram_block, piece_sems, block_sems, raw_finished, raw_block, raw_piece_sems, raw_block_sems,
):
    users, items = axis_sizes
    user, item = lax.axis_index("user"), lax.axis_index("item")
    slow, fast = item // side, lax.rem(item, side)
    half = partial.shape[2] // 2
    hops = (2, 1, 3)
    blocks = work.shape[0] // BLOCK
    everyone = (("user", users), ("item", items))
    greet(everyone)
    await_greetings(everyone)
    third = pieces_back(gram_piece, finished, piece_sems)

    def at_slow(ahead):
        return lax.rem(slow + ahead, side) * side + fast

    def at_fast(ahead):
        return slow * side + lax.rem(fast + ahead, side)

    far = []
    for ahead in hops:
        far.append(
            copy_to(
                partial.at[lax.rem(slow + ahead, side), :, pl.ds(0, half)],
                arrived.at[0, ahead - 1],
                far_sems.at[0, ahead - 1],
                user,
                at_slow(ahead),
            )
        )
        far.append(
            copy_to(
                partial.at[:, lax.rem(fast + ahead, side), pl.ds(half, half)],
                arrived.at[1, ahead - 1],
                far_sems.at[1, ahead - 1],
                user,
                at_fast(ahead),
            )
        )
    fourth = blocks_back(third, finished, gram_block, work, block_sems, users)
    receive(fourth)
    work[...] = work[...] * context_gram[...]
    invert(work, 0, blocks // 2)

    def combine(part, where):
        own = partial[slow, where, :half] if part == 0 else partial[where, fast, half:]
        total = own.astype(jnp.float32)
        for ahead in range(side - 1):
            total = total + arrived[part, ahead, where].astype(jnp.float32)
        return total

    near = []
    kept = []
    for part in range(2):
        receive(far[part::2])
        here = fast if part == 0 else slow
        for ahead in hops:
            where = lax.rem(here + ahead, side)
            mixed[part, ahead - 1] = combine(part, where).astype(mixed.dtype)
            near.append(
                copy_to(
                    mixed.at[part, ahead - 1],
                    settled.at[part, ahead - 1],
                    near_sems.at[part, ahead - 1],
                    user,
                    at_fast(ahead) if part == 0 else at_slow(ahead),
                )
            )
        kept.append(combine(part, here))
    invert(work, blocks // 2, blocks)
    receive(near)
    total = jnp.concatenate(
        [
            kept[part] + sum(settled[part, at].astype(jnp.float32) for at in range(side - 1))
            for part in range(2)
        ],
        axis=0,
    )
    raw[...] = dot(total, work[...])
    columns = raw[...].T
    for part in range(2):
        gathered[item, part] = columns[:, part * PAIR : (part + 1) * PAIR].astype(jnp.bfloat16)

    onward = []

    def pass_on(block, part, stage):
        for ahead in hops:
            onward.append(
                copy_to(
                    gathered.at[block, part],
                    gathered.at[block, part],
                    on_sems.at[part, stage, ahead - 1],
                    user,
                    at_fast(ahead) if part == 0 else at_slow(ahead),
                )
            )

    outward = []
    for ahead in hops:
        for part in range(2):
            outward.append(
                copy_to(
                    gathered.at[item, part],
                    gathered.at[item, part],
                    out_sems.at[part, ahead - 1],
                    user,
                    at_slow(ahead) if part == 0 else at_fast(ahead),
                )
            )
    gram[...] = gram_of(columns)
    first = gram_to_users(gram, by_user, user_sems, users)
    for part in range(2):
        pass_on(item, part, 0)
    for at, ahead in ((1, 1), (2, 3), (0, 2)):
        for part in range(2):
            outward[2 * at + part].wait_recv()
            back = side - ahead
            pass_on(at_slow(back) if part == 0 else at_fast(back), part, ahead)
    second = gram_to_items(first, by_user, pieces, by_item, item_sems, items)
    receive(second)
    raw_piece[...] = jnp.sum(by_item[...], axis=0)
    fifth = pieces_back(raw_piece, raw_finished, raw_piece_sems)
    sixth = blocks_back(fifth, raw_finished, raw_block, raw_gram, raw_block_sems, users)
    receive(onward)
    receive(sixth)
    for copy in third + fourth + far + near + outward + onward + first + second + fifth + sixth:
        copy.wait_send()


def update_users(partial, gram_piece, context_gram, axis_sizes):
    users, items = axis_sizes
    side, _, rows, width = partial.shape
    half = rows // 2
    square = jax.ShapeDtypeStruct((width, width), jnp.float32)
    return pl.pallas_call(
        functools.partial(user_kernel, axis_sizes, side),
        out_shape=(
            jax.ShapeDtypeStruct((rows, width), jnp.float32),
            jax.ShapeDtypeStruct((items, rows // PAIR, width, PAIR), jnp.bfloat16),
            square,
        ),
        in_specs=[VMEM_SPEC] * 3,
        out_specs=(VMEM_SPEC,) * 3,
        scratch_shapes=[
            pltpu.VMEM((2, side - 1, side, half, width), jnp.bfloat16),
            pltpu.VMEM((2, side - 1, half, width), jnp.bfloat16),
            pltpu.VMEM((2, side - 1, half, width), jnp.bfloat16),
            pltpu.VMEM((width, width), jnp.float32),
            pltpu.VMEM((8, 128), jnp.float32),
            pltpu.SemaphoreType.DMA((2, side - 1, 2)),
            pltpu.SemaphoreType.DMA((2, side - 1, 2)),
            pltpu.SemaphoreType.DMA((2, side - 1, 2)),
            pltpu.SemaphoreType.DMA((2, side, side - 1, 2)),
        ]
        + gram_sum_scratch(axis_sizes, width)
        + gram_spread_scratch(axis_sizes, width)
        + gram_spread_scratch(axis_sizes, width),
        compiler_params=pltpu.CompilerParams(
            collective_id=1, has_side_effects=True, vmem_limit_bytes=24 * 2**20
        ),
        name="update_users",
    )(partial, gram_piece, context_gram)


def item_kernel(
    axis_sizes, partial, raw_gram, context_gram, raw, new_items, user_factor, arrived, work,
    user_sums, item_sums, user_sems, item_sems, sems
):
    users, items = axis_sizes
    user, item = lax.axis_index("user"), lax.axis_index("item")
    everyone = (("user", users), ("item", items))
    greet(everyone)
    await_greetings(everyone)
    copies = send_all(
        "user",
        users,
        lambda peer, ahead: partial.at[peer],
        lambda me, ahead: arrived.at[ahead - 1],
        sems,
    )
    width = work.shape[0]
    rows_total = jnp.float32(user_factor.shape[0] * users * items)
    down = lax.broadcasted_iota(jnp.int32, (width, width), 0)
    across = lax.broadcasted_iota(jnp.int32, (width, width), 1)
    diagonal = jnp.where(down == across, raw_gram[...], 0.0)
    scale_row = jnp.sqrt(rows_total / (jnp.sum(diagonal, axis=0, keepdims=True) + 1e-06))
    scale_column = jnp.sqrt(rows_total / (jnp.sum(diagonal, axis=1, keepdims=True) + 1e-06))
    user_factor[...] = raw[...] * scale_row
    work[...] = raw_gram[...] * scale_column * scale_row * context_gram[...]
    invert(work, 0, width // BLOCK)
    total = partial[user].astype(jnp.float32)
    for ahead in range(1, users):
        copies[ahead - 1].wait_recv()
        total = total + arrived[ahead - 1].astype(jnp.float32)
    item_raw = dot(total * scale_row, work[...])
    squares = jnp.sum(item_raw * item_raw, axis=0, keepdims=True)
    user_sums[user] = jnp.broadcast_to(squares, user_sums.shape[1:])
    first = send_all(
        "user", users, lambda peer, ahead: user_sums.at[user], lambda me, ahead: user_sums.at[me], user_sems
    )
    receive(first)
    item_sums[item] = jnp.sum(user_sums[...], axis=0)
    second = send_all(
        "item", items, lambda peer, ahead: item_sums.at[item], lambda me, ahead: item_sums.at[me], item_sems
    )
    receive(second)
    squares = jnp.sum(item_sums[...], axis=0)[:1]
    new_items[...] = item_raw * jnp.sqrt(rows_total / (squares + 1e-06))
    for copy in copies + first + second:
        copy.wait_send()


def update_items(partial, raw_gram, context_gram, raw, axis_sizes):
    users, items = axis_sizes
    _, rows, width = partial.shape
    out = jax.ShapeDtypeStruct((rows, width), jnp.float32)
    return pl.pallas_call(
        functools.partial(item_kernel, axis_sizes),
        out_shape=(out, out),
        in_specs=[VMEM_SPEC] * 4,
        out_specs=(VMEM_SPEC,) * 2,
        scratch_shapes=[
            pltpu.VMEM((users - 1, rows, width), jnp.bfloat16),
            pltpu.VMEM((width, width), jnp.float32),
            pltpu.VMEM((users, 8, width), jnp.float32),
            pltpu.VMEM((items, 8, width), jnp.float32),
            pltpu.SemaphoreType.DMA((2, users - 1)),
            pltpu.SemaphoreType.DMA((2, items - 1)),
            pltpu.SemaphoreType.DMA((2, users - 1)),
        ],
        compiler_params=pltpu.CompilerParams(
            collective_id=2, has_side_effects=True, vmem_limit_bytes=16 * 2**20
        ),
        name="update_items",
    )(partial, raw_gram, context_gram, raw)


def local(
    item_factor, context_factor, tile_count, tile_rows, tile_cols, tile_ctx, nz_offsets, nz_values
):
    axis_sizes = (lax.axis_size("user"), lax.axis_size("item"))
    users, items = axis_sizes
    rows, width = item_factor.shape
    side = math.isqrt(items)
    count = tile_count.reshape(1)
    ids = (tile_rows[0, 0], tile_cols[0, 0], tile_ctx[0, 0])
    offsets = nz_offsets[0, 0]
    values = nz_values[0, 0]
    item_pairs, context_pairs, gram_piece, context_gram = gather_items(
        item_factor, context_factor, axis_sizes
    )
    partial_users = mttkrp(
        0, count, ids, offsets, values, item_pairs.reshape(-1, width, PAIR), context_pairs,
        items * rows // TILE,
    )
    raw, user_pairs, raw_gram = update_users(
        partial_users.reshape(side, side, rows, width), gram_piece, context_gram, axis_sizes
    )
    partial_items = mttkrp(
        1, count, ids, offsets, values, user_pairs.reshape(-1, width, PAIR), context_pairs,
        users * rows // TILE,
    )
    new_items, user_factor = update_items(
        partial_items.reshape(users, rows, width), raw_gram, context_gram, raw, axis_sizes
    )
    return (user_factor, new_items)


def solution(mesh):
    in_specs = (
        P(("item", "user"), None),
        P(),
        P("user", "item"),
        P("user", "item", None),
        P("user", "item", None),
        P("user", "item", None),
        P("user", "item", None, None, None),
        P("user", "item", None, None),
    )
    out_specs = (P(("user", "item"), None), P(("item", "user"), None))
    return jax.shard_map(local, mesh=mesh, in_specs=in_specs, out_specs=out_specs, check_vma=False)
```

```python
import functools
import math

import jax
import jax.numpy as jnp
from jax import lax
from jax.experimental import pallas as pl
from jax.experimental.pallas import tpu as pltpu
from jax.sharding import PartitionSpec as P

TILE = 64
UNROLL = 64
PAIR = 2 * TILE
BLOCK = 64
SPLIT = 2
HOPS = (1, 3, 2)
PIVOTS = 4
HIGHEST = lax.Precision.HIGHEST
MESH = pl.DeviceIdType.MESH
VMEM_SPEC = pl.BlockSpec(memory_space=pltpu.VMEM)
SMEM_SPEC = pl.BlockSpec(memory_space=pltpu.SMEM)


def dot(left, right):
    return jnp.dot(left, right, precision=HIGHEST, preferred_element_type=jnp.float32)


def gram_of(columns):
    return lax.dot_general(
        columns,
        columns,
        (((1,), (1,)), ((), ())),
        precision=HIGHEST,
        preferred_element_type=jnp.float32,
    )


def mttkrp_kernel(
    target_at,
    count,
    target_ids,
    source_ids,
    context_ids,
    offsets,
    values,
    source,
    context,
    out,
    totals,
):
    totals[...] = jnp.zeros_like(totals)
    rank, entries = totals.shape[2], offsets.shape[2]

    def one_hot(row, extent):
        positions = lax.broadcasted_iota(jnp.int32, (extent, entries), 0)
        return jnp.where(positions == row, 1.0, 0.0).astype(jnp.bfloat16)

    def lanes_of(pair, row):
        wide = pair.astype(jnp.float32)
        picked = [
            jnp.take_along_axis(
                wide,
                jnp.broadcast_to(row[:, at : at + PAIR], (rank, PAIR)),
                axis=1,
                mode="promise_in_bounds",
            )
            for at in range(0, entries, PAIR)
        ]
        return jnp.concatenate(picked, axis=1)

    def group(step, carry):
        first = pl.multiple_of(step * UNROLL, UNROLL)
        targets = offsets[target_at, pl.ds(first, UNROLL), :]
        sources = offsets[1 - target_at, pl.ds(first, UNROLL), :]
        contexts = offsets[2, pl.ds(first, UNROLL), :]
        weights = values[pl.ds(first, UNROLL), :]
        for at in range(UNROLL):
            row = slice(at, at + 1)
            source_id, context_id = source_ids[first + at], context_ids[first + at]
            source_row = sources[row] + TILE * lax.rem(source_id, 2)
            context_row = contexts[row] + TILE * lax.rem(context_id, 2)
            source_part = jnp.dot(
                source[lax.div(source_id, 2)],
                one_hot(source_row, PAIR),
                preferred_element_type=jnp.float32,
            )
            context_part = lanes_of(context[lax.div(context_id, 2)], context_row)
            weight = jnp.where(first + at < count[0], weights[row], 0.0)
            terms = (weight * source_part * context_part).astype(jnp.bfloat16)
            totals[target_ids[first + at]] += lax.dot_general(
                one_hot(targets[row], TILE),
                terms,
                (((1,), (1,)), ((), ())),
                preferred_element_type=jnp.float32,
            )
        return carry

    lax.fori_loop(0, (count[0] + UNROLL - 1) // UNROLL, group, 0)
    out[...] = totals[...].astype(out.dtype)


def mttkrp(target_at, count, ids, offsets, values, source_pairs, context_pairs, tiles):
    shape = (tiles, TILE, source_pairs.shape[1])
    return pl.pallas_call(
        functools.partial(mttkrp_kernel, target_at),
        out_shape=jax.ShapeDtypeStruct(shape, jnp.bfloat16),
        in_specs=[SMEM_SPEC] * 4 + [VMEM_SPEC] * 4,
        out_specs=VMEM_SPEC,
        scratch_shapes=[pltpu.VMEM(shape, jnp.float32)],
        compiler_params=pltpu.CompilerParams(vmem_limit_bytes=24 * 2**20),
        name="mttkrp",
    )(
        count,
        ids[target_at],
        ids[1 - target_at],
        ids[2],
        offsets,
        values,
        source_pairs,
        context_pairs,
    )


def greet(groups):
    barrier = pltpu.get_barrier_semaphore()
    for axis, size in groups:
        me = lax.axis_index(axis)
        for ahead in range(1, size):
            pl.semaphore_signal(
                barrier, inc=1, device_id={axis: lax.rem(me + ahead, size)}, device_id_type=MESH
            )


def await_greetings(groups):
    pl.semaphore_wait(pltpu.get_barrier_semaphore(), sum(size - 1 for _, size in groups))


def send_all(axis, size, source, target, sems):
    me = lax.axis_index(axis)
    copies = []
    for ahead in range(1, size):
        peer = lax.rem(me + ahead, size)
        copy = pltpu.make_async_remote_copy(
            src_ref=source(peer, ahead),
            dst_ref=target(me, ahead),
            send_sem=sems.at[0, ahead - 1],
            recv_sem=sems.at[1, ahead - 1],
            device_id={axis: peer},
            device_id_type=MESH,
        )
        copy.start()
        copies.append(copy)
    return copies


def copy_to(source, target, sems, user, item):
    copy = pltpu.make_async_remote_copy(
        src_ref=source,
        dst_ref=target,
        send_sem=sems.at[0],
        recv_sem=sems.at[1],
        device_id=(user, item),
        device_id_type=MESH,
    )
    copy.start()
    return copy


def receive(copies):
    for copy in copies:
        copy.wait_recv()


def rows_of(item, rows):
    return pl.ds(pl.multiple_of(item * rows, rows), rows)


def gram_to_users(gram, by_user, sems, users):
    rows = by_user.shape[1]
    user = lax.axis_index("user")
    by_user[user] = gram[rows_of(user, rows), :]
    return send_all(
        "user",
        users,
        lambda peer, ahead: gram.at[rows_of(peer, rows)],
        lambda me, ahead: by_user.at[me],
        sems,
    )


def torus(side):
    item = lax.axis_index("item")
    slow, fast = item // side, lax.rem(item, side)

    def at_slow(ahead):
        return lax.rem(slow + ahead, side) * side + fast

    def at_fast(ahead):
        return slow * side + lax.rem(fast + ahead, side)

    return slow, fast, at_slow, at_fast


def exchange(before, terms, place, along, spread, sems):
    receive(before)
    spread[place] = jnp.sum(terms[...], axis=0)
    user = lax.axis_index("user")
    return [
        copy_to(spread.at[place], spread.at[place], sems.at[ahead - 1], user, along(ahead))
        for ahead in HOPS
    ]


def blocks_back(block, result, sems, users):
    rows = block.shape[0]
    span = rows_of(lax.axis_index("user"), rows)
    result[span, :] = block[...]
    return send_all("user", users, lambda peer, ahead: block, lambda me, ahead: result.at[span], sems)


def gram_scratch(users, side, width):
    rows = width // users
    return [
        pltpu.VMEM((width, width), jnp.float32),
        pltpu.VMEM((users, rows, width), jnp.float32),
        pltpu.VMEM((side, rows, width), jnp.float32),
        pltpu.VMEM((side, rows, width), jnp.float32),
        pltpu.SemaphoreType.DMA((2, users - 1)),
        pltpu.SemaphoreType.DMA((side - 1, 2)),
        pltpu.SemaphoreType.DMA((side - 1, 2)),
    ]


def small_inverse(matrix):
    size = len(matrix)
    if size == 2:
        (first, off), (_, last) = matrix
        scale = 1.0 / (first * last - off * off)
        cross = -off * scale
        return [[last * scale, cross], [cross, first * scale]]
    half = size // 2

    def product(left, right):
        return [
            [sum(left[i][k] * right[k][j] for k in range(1, half)) + left[i][0] * right[0][j] for j in range(half)]
            for i in range(half)
        ]

    corner = small_inverse([row[:half] for row in matrix[:half]])
    side = [row[half:] for row in matrix[:half]]
    solved = product(corner, side)
    lowered = product([list(column) for column in zip(*side)], solved)
    rest = small_inverse(
        [[matrix[half + i][half + j] - lowered[i][j] for j in range(half)] for i in range(half)]
    )
    spread = product(solved, rest)
    update = product(spread, [list(column) for column in zip(*solved)])
    top = [
        [corner[i][j] + update[i][j] for j in range(half)] + [-spread[i][j] for j in range(half)]
        for i in range(half)
    ]
    bottom = [[-spread[j][i] for j in range(half)] + rest[i] for i in range(half)]
    return top + bottom


def invert(work, first_block, last_block):
    width = work.shape[0]
    down = lax.broadcasted_iota(jnp.int32, (BLOCK, BLOCK), 0)
    across = lax.broadcasted_iota(jnp.int32, (BLOCK, BLOCK), 1)
    lanes = lax.broadcasted_iota(jnp.int32, (BLOCK, width), 1) // BLOCK
    rows = lax.broadcasted_iota(jnp.int32, (width, BLOCK), 0) // BLOCK
    full_lanes = lax.broadcasted_iota(jnp.int32, (width, width), 1) // BLOCK
    steps = range(PIVOTS)
    for block in range(first_block, last_block):
        span = slice(block * BLOCK, (block + 1) * BLOCK)
        pivot = work[span, span]
        for at in range(0, BLOCK, PIVOTS):
            columns = [
                jnp.broadcast_to(pivot[:, at + i : at + i + 1], (BLOCK, BLOCK)) for i in steps
            ]
            inverse = small_inverse(
                [
                    [columns[max(i, j)][at + min(i, j) : at + min(i, j) + 1, :] for j in steps]
                    for i in steps
                ]
            )
            fresh = []
            for i in steps:
                row = inverse[i][0] * pivot[at : at + 1, :]
                for j in steps[1:]:
                    row = row + inverse[i][j] * pivot[at + j : at + j + 1, :]
                for j in steps:
                    row = jnp.where(across[:1] == at + j, inverse[i][j], row)
                fresh.append(row)
            after = jnp.where((across >= at) & (across < at + PIVOTS), 0.0, pivot)
            for i in steps:
                after = after - columns[i] * fresh[i]
            for i in steps:
                after = jnp.where(down == at + i, fresh[i], after)
            pivot = after
        panel = dot(pivot, work[span, :])
        panel = jnp.where(lanes == block, jnp.concatenate([pivot] * (width // BLOCK), axis=1), panel)
        column = jnp.where(rows == block, 0.0, work[:, span])
        kept = jnp.where(full_lanes == block, 0.0, work[...])
        work[...] = kept - dot(column, panel)
        work[span, :] = panel


def gather_kernel(
    axis_sizes, side, step_rows, item_factor, context_factor, items, context, gram_rows, context_gram,
    own_rows, loaded, load_sems, own_sems, sibling_sems,
    gram, by_user, by_slow, by_fast, user_sems, slow_sems, fast_sems,
):
    users, items_extent = axis_sizes
    everyone = (("user", users), ("item", items_extent))
    user, item = lax.axis_index("user"), lax.axis_index("item")
    slow, fast, at_slow, at_fast = torus(side)
    steps = context_factor.shape[0] // step_rows
    pairs = step_rows // PAIR
    greet(everyone)

    def load(step):
        span = pl.ds(pl.multiple_of(step * step_rows, step_rows), step_rows)
        return pltpu.make_async_copy(context_factor.at[span], loaded.at[step], load_sems.at[step])

    def transform(step, carry):
        load(step).wait()
        chunk = loaded[step]
        columns = chunk.T
        for pair in range(pairs):
            context[step * pairs + pair] = columns[:, pair * PAIR : (pair + 1) * PAIR].astype(
                jnp.bfloat16
            )
        context_gram[...] += gram_of(columns)
        return carry

    fetch = pltpu.make_async_copy(item_factor, own_rows, load_sems.at[steps])
    fetch.start()
    for step in range(steps):
        load(step).start()
    context_gram[...] = jnp.zeros_like(context_gram)
    fetch.wait()
    columns = own_rows[...].T
    for pair in range(items.shape[1]):
        items[user, pair] = columns[:, pair * PAIR : (pair + 1) * PAIR].astype(jnp.bfloat16)
    gram[...] = gram_of(columns)
    await_greetings(everyone)
    core = lax.rem(user, 2)
    sibling = user + 1 - 2 * core
    own = []
    for ahead in HOPS:
        peer = lax.rem(user + 2 * ahead, users)
        own.append(copy_to(items.at[user], items.at[user], own_sems.at[ahead - 1], peer, item))
    forwarded = [copy_to(items.at[user], items.at[user], sibling_sems.at[0], sibling, item)]

    def forward(at):
        own[at].wait_recv()
        block = items.at[lax.rem(user + users - 2 * HOPS[at], users)]
        forwarded.append(copy_to(block, block, sibling_sems.at[1 + at], sibling, item))

    first = gram_to_users(gram, by_user, user_sems, users)
    lax.fori_loop(0, steps // 2, transform, 0)
    second = exchange(first, by_user, slow, at_slow, by_slow, slow_sems)
    forward(0)
    forward(1)
    lax.fori_loop(steps // 2, 3 * steps // 4, transform, 0)
    third = exchange(second, by_slow, fast, at_fast, by_fast, fast_sems)
    forward(2)
    lax.fori_loop(3 * steps // 4, steps, transform, 0)
    receive(third)
    gram_rows[...] = jnp.sum(by_fast[...], axis=0)
    receive(forwarded)
    for copy in first + own + forwarded + second + third:
        copy.wait_send()


def gather_items(item_factor, context_factor, axis_sizes, side):
    users, items = axis_sizes
    rows, width = item_factor.shape
    contexts = context_factor.shape[0]
    step_rows = 512
    return pl.pallas_call(
        functools.partial(gather_kernel, axis_sizes, side, step_rows),
        out_shape=(
            jax.ShapeDtypeStruct((users, rows // PAIR, width, PAIR), jnp.bfloat16),
            jax.ShapeDtypeStruct((contexts // PAIR, width, PAIR), jnp.bfloat16),
            jax.ShapeDtypeStruct((width // users, width), jnp.float32),
            jax.ShapeDtypeStruct((width, width), jnp.float32),
        ),
        in_specs=[pl.BlockSpec(memory_space=pltpu.HBM)] * 2,
        out_specs=(VMEM_SPEC,) * 4,
        scratch_shapes=[
            pltpu.VMEM((rows, width), jnp.float32),
            pltpu.VMEM((contexts // step_rows, step_rows, width), jnp.float32),
            pltpu.SemaphoreType.DMA((contexts // step_rows + 1,)),
            pltpu.SemaphoreType.DMA((users // 2 - 1, 2)),
            pltpu.SemaphoreType.DMA((users // 2, 2)),
        ]
        + gram_scratch(users, side, width),
        compiler_params=pltpu.CompilerParams(
            collective_id=0, has_side_effects=True, vmem_limit_bytes=16 * 2**20
        ),
        name="gather_items",
    )(
        pltpu.with_memory_space_constraint(item_factor, pltpu.HBM),
        pltpu.with_memory_space_constraint(context_factor, pltpu.HBM),
    )


def user_kernel(
    axis_sizes, side, partial, gram_rows, context_gram, raw, gathered, raw_gram, arrived, mixed, settled,
    work, far_sems, near_sems, out_sems, on_sems, system_sems, raw_block, raw_sems,
    gram, by_user, by_slow, by_fast, user_sems, slow_sems, fast_sems,
):
    users, items = axis_sizes
    user, item = lax.axis_index("user"), lax.axis_index("item")
    slow, fast, at_slow, at_fast = torus(side)
    half = partial.shape[2] // 2
    blocks = work.shape[0] // BLOCK
    everyone = (("user", users), ("item", items))
    greet(everyone)
    await_greetings(everyone)
    system = blocks_back(gram_rows, work, system_sems, users)

    far = []
    for ahead in HOPS:
        far.append(
            copy_to(
                partial.at[lax.rem(slow + ahead, side), :, pl.ds(0, half)],
                arrived.at[0, ahead - 1],
                far_sems.at[0, ahead - 1],
                user,
                at_slow(ahead),
            )
        )
        far.append(
            copy_to(
                partial.at[:, lax.rem(fast + ahead, side), pl.ds(half, half)],
                arrived.at[1, ahead - 1],
                far_sems.at[1, ahead - 1],
                user,
                at_fast(ahead),
            )
        )
    receive(system)
    work[...] = work[...] * context_gram[...]
    invert(work, 0, SPLIT)

    def combine(part, where):
        own = partial[slow, where, :half] if part == 0 else partial[where, fast, half:]
        total = own.astype(jnp.float32)
        for ahead in range(side - 1):
            total = total + arrived[part, ahead, where].astype(jnp.float32)
        return total

    near = []
    kept = []
    for part in range(2):
        receive(far[part::2])
        here = fast if part == 0 else slow
        for ahead in HOPS:
            where = lax.rem(here + ahead, side)
            mixed[part, ahead - 1] = combine(part, where).astype(mixed.dtype)
            near.append(
                copy_to(
                    mixed.at[part, ahead - 1],
                    settled.at[part, ahead - 1],
                    near_sems.at[part, ahead - 1],
                    user,
                    at_fast(ahead) if part == 0 else at_slow(ahead),
                )
            )
        kept.append(combine(part, here))
    invert(work, SPLIT, blocks)
    receive(near)
    total = jnp.concatenate(
        [
            kept[part] + sum(settled[part, at].astype(jnp.float32) for at in range(side - 1))
            for part in range(2)
        ],
        axis=0,
    )
    raw[...] = dot(total, work[...])
    columns = raw[...].T
    for part in range(2):
        gathered[item, part] = columns[:, part * PAIR : (part + 1) * PAIR].astype(jnp.bfloat16)

    onward = []

    def pass_on(block, part, stage):
        for ahead in HOPS:
            onward.append(
                copy_to(
                    gathered.at[block, part],
                    gathered.at[block, part],
                    on_sems.at[part, stage, ahead - 1],
                    user,
                    at_fast(ahead) if part == 0 else at_slow(ahead),
                )
            )

    outward = []
    for ahead in HOPS:
        for part in range(2):
            outward.append(
                copy_to(
                    gathered.at[item, part],
                    gathered.at[item, part],
                    out_sems.at[part, ahead - 1],
                    user,
                    at_slow(ahead) if part == 0 else at_fast(ahead),
                )
            )
    gram[...] = gram_of(columns)
    first = gram_to_users(gram, by_user, user_sems, users)
    for part in range(2):
        pass_on(item, part, 0)

    def forward(at):
        for part in range(2):
            outward[2 * at + part].wait_recv()
            back = side - HOPS[at]
            pass_on(at_slow(back) if part == 0 else at_fast(back), part, HOPS[at])

    second = exchange(first, by_user, slow, at_slow, by_slow, slow_sems)
    forward(0)
    third = exchange(second, by_slow, fast, at_fast, by_fast, fast_sems)
    forward(1)
    forward(2)
    receive(third)
    raw_block[...] = jnp.sum(by_fast[...], axis=0)
    fourth = blocks_back(raw_block, raw_gram, raw_sems, users)
    receive(onward)
    receive(fourth)
    for copy in system + far + near + outward + onward + first + second + third + fourth:
        copy.wait_send()


def update_users(partial, gram_rows, context_gram, axis_sizes):
    users, items = axis_sizes
    side, _, rows, width = partial.shape
    half = rows // 2
    square = jax.ShapeDtypeStruct((width, width), jnp.float32)
    return pl.pallas_call(
        functools.partial(user_kernel, axis_sizes, side),
        out_shape=(
            jax.ShapeDtypeStruct((rows, width), jnp.float32),
            jax.ShapeDtypeStruct((items, rows // PAIR, width, PAIR), jnp.bfloat16),
            square,
        ),
        in_specs=[VMEM_SPEC] * 3,
        out_specs=(VMEM_SPEC,) * 3,
        scratch_shapes=[
            pltpu.VMEM((2, side - 1, side, half, width), jnp.bfloat16),
            pltpu.VMEM((2, side - 1, half, width), jnp.bfloat16),
            pltpu.VMEM((2, side - 1, half, width), jnp.bfloat16),
            pltpu.VMEM((width, width), jnp.float32),
            pltpu.SemaphoreType.DMA((2, side - 1, 2)),
            pltpu.SemaphoreType.DMA((2, side - 1, 2)),
            pltpu.SemaphoreType.DMA((2, side - 1, 2)),
            pltpu.SemaphoreType.DMA((2, side, side - 1, 2)),
            pltpu.SemaphoreType.DMA((2, users - 1)),
            pltpu.VMEM((width // users, width), jnp.float32),
            pltpu.SemaphoreType.DMA((2, users - 1)),
        ]
        + gram_scratch(users, side, width),
        compiler_params=pltpu.CompilerParams(
            collective_id=1, has_side_effects=True, vmem_limit_bytes=24 * 2**20
        ),
        name="update_users",
    )(partial, gram_rows, context_gram)


def item_kernel(
    axis_sizes, partial, raw_gram, context_gram, raw, new_items, user_factor, arrived, work,
    user_sums, item_sums, user_sems, item_sems, sems
):
    users, items = axis_sizes
    user, item = lax.axis_index("user"), lax.axis_index("item")
    everyone = (("user", users), ("item", items))
    greet(everyone)
    await_greetings(everyone)
    copies = send_all(
        "user",
        users,
        lambda peer, ahead: partial.at[peer],
        lambda me, ahead: arrived.at[ahead - 1],
        sems,
    )
    width = work.shape[0]
    rows_total = jnp.float32(user_factor.shape[0] * users * items)
    down = lax.broadcasted_iota(jnp.int32, (width, width), 0)
    across = lax.broadcasted_iota(jnp.int32, (width, width), 1)
    diagonal = jnp.where(down == across, raw_gram[...], 0.0)
    scale_row = jnp.sqrt(rows_total / (jnp.sum(diagonal, axis=0, keepdims=True) + 1e-06))
    scale_column = jnp.sqrt(rows_total / (jnp.sum(diagonal, axis=1, keepdims=True) + 1e-06))
    user_factor[...] = raw[...] * scale_row
    work[...] = raw_gram[...] * scale_column * scale_row * context_gram[...]
    invert(work, 0, width // BLOCK)
    total = partial[user].astype(jnp.float32)
    for ahead in range(1, users):
        copies[ahead - 1].wait_recv()
        total = total + arrived[ahead - 1].astype(jnp.float32)
    item_raw = dot(total * scale_row, work[...])
    squares = jnp.sum(item_raw * item_raw, axis=0, keepdims=True)
    user_sums[user] = jnp.broadcast_to(squares, user_sums.shape[1:])
    first = send_all(
        "user", users, lambda peer, ahead: user_sums.at[user], lambda me, ahead: user_sums.at[me], user_sems
    )
    receive(first)
    item_sums[item] = jnp.sum(user_sums[...], axis=0)
    second = send_all(
        "item", items, lambda peer, ahead: item_sums.at[item], lambda me, ahead: item_sums.at[me], item_sems
    )
    receive(second)
    squares = jnp.sum(item_sums[...], axis=0)[:1]
    new_items[...] = item_raw * jnp.sqrt(rows_total / (squares + 1e-06))
    for copy in copies + first + second:
        copy.wait_send()


def update_items(partial, raw_gram, context_gram, raw, axis_sizes):
    users, items = axis_sizes
    _, rows, width = partial.shape
    out = jax.ShapeDtypeStruct((rows, width), jnp.float32)
    return pl.pallas_call(
        functools.partial(item_kernel, axis_sizes),
        out_shape=(out, out),
        in_specs=[VMEM_SPEC] * 4,
        out_specs=(VMEM_SPEC,) * 2,
        scratch_shapes=[
            pltpu.VMEM((users - 1, rows, width), jnp.bfloat16),
            pltpu.VMEM((width, width), jnp.float32),
            pltpu.VMEM((users, 8, width), jnp.float32),
            pltpu.VMEM((items, 8, width), jnp.float32),
            pltpu.SemaphoreType.DMA((2, users - 1)),
            pltpu.SemaphoreType.DMA((2, items - 1)),
            pltpu.SemaphoreType.DMA((2, users - 1)),
        ],
        compiler_params=pltpu.CompilerParams(
            collective_id=2, has_side_effects=True, vmem_limit_bytes=16 * 2**20
        ),
        name="update_items",
    )(partial, raw_gram, context_gram, raw)


def local(
    item_factor, context_factor, tile_count, tile_rows, tile_cols, tile_ctx, nz_offsets, nz_values
):
    axis_sizes = (lax.axis_size("user"), lax.axis_size("item"))
    users, items = axis_sizes
    rows, width = item_factor.shape
    side = math.isqrt(items)
    count = tile_count.reshape(1)
    ids = (tile_rows[0, 0], tile_cols[0, 0], tile_ctx[0, 0])
    offsets = nz_offsets[0, 0]
    values = nz_values[0, 0]
    item_pairs, context_pairs, gram_rows, context_gram = gather_items(
        item_factor, context_factor, axis_sizes, side
    )
    partial_users = mttkrp(
        0, count, ids, offsets, values, item_pairs.reshape(-1, width, PAIR), context_pairs,
        items * rows // TILE,
    )
    raw, user_pairs, raw_gram = update_users(
        partial_users.reshape(side, side, rows, width), gram_rows, context_gram, axis_sizes
    )
    partial_items = mttkrp(
        1, count, ids, offsets, values, user_pairs.reshape(-1, width, PAIR), context_pairs,
        users * rows // TILE,
    )
    new_items, user_factor = update_items(
        partial_items.reshape(users, rows, width), raw_gram, context_gram, raw, axis_sizes
    )
    return (user_factor, new_items)


def solution(mesh):
    in_specs = (
        P(("item", "user"), None),
        P(),
        P("user", "item"),
        P("user", "item", None),
        P("user", "item", None),
        P("user", "item", None),
        P("user", "item", None, None, None),
        P("user", "item", None, None),
    )
    out_specs = (P(("user", "item"), None), P(("item", "user"), None))
    return jax.shard_map(local, mesh=mesh, in_specs=in_specs, out_specs=out_specs, check_vma=False)
```

```python
import functools
import math

import jax
import jax.numpy as jnp
from jax import lax
from jax.experimental import pallas as pl
from jax.experimental.pallas import tpu as pltpu
from jax.sharding import PartitionSpec as P

TILE = 64
UNROLL = 32
PLAN = (3, 2)
PAIR = 2 * TILE
BLOCK = 64
SPLIT = 2
HOPS = (1, 3, 2)
PIVOTS = 4
HIGHEST = lax.Precision.HIGHEST
MESH = pl.DeviceIdType.MESH
VMEM_SPEC = pl.BlockSpec(memory_space=pltpu.VMEM)
SMEM_SPEC = pl.BlockSpec(memory_space=pltpu.SMEM)


def dot(left, right):
    return jnp.dot(left, right, precision=HIGHEST, preferred_element_type=jnp.float32)


def gram_of(columns):
    return lax.dot_general(
        columns,
        columns,
        (((1,), (1,)), ((), ())),
        precision=HIGHEST,
        preferred_element_type=jnp.float32,
    )


def mttkrp_kernel(
    target_at,
    count,
    target_ids,
    source_ids,
    context_ids,
    offsets,
    values,
    source,
    context,
    out,
    totals,
):
    totals[...] = jnp.zeros_like(totals)
    rank, entries = totals.shape[2], offsets.shape[2]

    def one_hot(row, extent):
        positions = lax.broadcasted_iota(jnp.int32, (extent, entries), 0)
        return jnp.where(positions == row, 1.0, 0.0).astype(jnp.bfloat16)

    def lanes_of(pair, row):
        wide = pair.astype(jnp.float32)
        picked = [
            jnp.take_along_axis(
                wide,
                jnp.broadcast_to(row[:, at : at + PAIR], (rank, PAIR)),
                axis=1,
                mode="promise_in_bounds",
            )
            for at in range(0, entries, PAIR)
        ]
        return jnp.concatenate(picked, axis=1)

    def group(step, carry):
        first = pl.multiple_of(step * UNROLL, UNROLL)
        targets = offsets[target_at, pl.ds(first, UNROLL), :]
        sources = offsets[1 - target_at, pl.ds(first, UNROLL), :]
        contexts = offsets[2, pl.ds(first, UNROLL), :]
        weights = values[pl.ds(first, UNROLL), :]
        for at in range(UNROLL):
            row = slice(at, at + 1)
            source_id, context_id = source_ids[first + at], context_ids[first + at]
            source_row = sources[row] + TILE * lax.rem(source_id, 2)
            context_row = contexts[row] + TILE * lax.rem(context_id, 2)
            source_part = jnp.dot(
                source[lax.div(source_id, 2)],
                one_hot(source_row, PAIR),
                preferred_element_type=jnp.float32,
            )
            context_part = lanes_of(context[lax.div(context_id, 2)], context_row)
            weight = jnp.where(first + at < count[0], weights[row], 0.0)
            terms = (weight * source_part * context_part).astype(jnp.bfloat16)
            totals[target_ids[first + at]] += lax.dot_general(
                one_hot(targets[row], TILE),
                terms,
                (((1,), (1,)), ((), ())),
                preferred_element_type=jnp.float32,
            )
        return carry

    lax.fori_loop(0, (count[0] + UNROLL - 1) // UNROLL, group, 0)
    out[...] = totals[...].astype(out.dtype)


def mttkrp(target_at, count, ids, offsets, values, source_pairs, context_pairs, tiles):
    shape = (tiles, TILE, source_pairs.shape[1])
    return pl.pallas_call(
        functools.partial(mttkrp_kernel, target_at),
        out_shape=jax.ShapeDtypeStruct(shape, jnp.bfloat16),
        in_specs=[SMEM_SPEC] * 4 + [VMEM_SPEC] * 4,
        out_specs=VMEM_SPEC,
        scratch_shapes=[pltpu.VMEM(shape, jnp.float32)],
        compiler_params=pltpu.CompilerParams(vmem_limit_bytes=24 * 2**20),
        name="mttkrp",
    )(
        count,
        ids[target_at],
        ids[1 - target_at],
        ids[2],
        offsets,
        values,
        source_pairs,
        context_pairs,
    )


def greet(groups):
    barrier = pltpu.get_barrier_semaphore()
    for axis, size in groups:
        me = lax.axis_index(axis)
        for ahead in range(1, size):
            pl.semaphore_signal(
                barrier, inc=1, device_id={axis: lax.rem(me + ahead, size)}, device_id_type=MESH
            )


def await_greetings(groups):
    pl.semaphore_wait(pltpu.get_barrier_semaphore(), sum(size - 1 for _, size in groups))


def send_all(axis, size, source, target, sems):
    me = lax.axis_index(axis)
    copies = []
    for ahead in range(1, size):
        peer = lax.rem(me + ahead, size)
        copy = pltpu.make_async_remote_copy(
            src_ref=source(peer, ahead),
            dst_ref=target(me, ahead),
            send_sem=sems.at[0, ahead - 1],
            recv_sem=sems.at[1, ahead - 1],
            device_id={axis: peer},
            device_id_type=MESH,
        )
        copy.start()
        copies.append(copy)
    return copies


def copy_to(source, target, sems, user, item):
    copy = pltpu.make_async_remote_copy(
        src_ref=source,
        dst_ref=target,
        send_sem=sems.at[0],
        recv_sem=sems.at[1],
        device_id=(user, item),
        device_id_type=MESH,
    )
    copy.start()
    return copy


def receive(copies):
    for copy in copies:
        copy.wait_recv()


def rows_of(item, rows):
    return pl.ds(pl.multiple_of(item * rows, rows), rows)


def gram_to_users(gram, by_user, sems, users):
    rows = by_user.shape[1]
    user = lax.axis_index("user")
    by_user[user] = gram[rows_of(user, rows), :]
    return send_all(
        "user",
        users,
        lambda peer, ahead: gram.at[rows_of(peer, rows)],
        lambda me, ahead: by_user.at[me],
        sems,
    )


def torus(side):
    item = lax.axis_index("item")
    slow, fast = item // side, lax.rem(item, side)

    def at_slow(ahead):
        return lax.rem(slow + ahead, side) * side + fast

    def at_fast(ahead):
        return slow * side + lax.rem(fast + ahead, side)

    return slow, fast, at_slow, at_fast


def exchange(before, terms, place, along, spread, sems):
    receive(before)
    spread[place] = jnp.sum(terms[...], axis=0)
    user = lax.axis_index("user")
    return [
        copy_to(spread.at[place], spread.at[place], sems.at[ahead - 1], user, along(ahead))
        for ahead in HOPS
    ]


def blocks_back(block, result, sems, users):
    rows = block.shape[0]
    span = rows_of(lax.axis_index("user"), rows)
    result[span, :] = block[...]
    return send_all("user", users, lambda peer, ahead: block, lambda me, ahead: result.at[span], sems)


def gram_scratch(users, side, width):
    rows = width // users
    return [
        pltpu.VMEM((width, width), jnp.float32),
        pltpu.VMEM((users, rows, width), jnp.float32),
        pltpu.VMEM((side, rows, width), jnp.float32),
        pltpu.VMEM((side, rows, width), jnp.float32),
        pltpu.SemaphoreType.DMA((2, users - 1)),
        pltpu.SemaphoreType.DMA((side - 1, 2)),
        pltpu.SemaphoreType.DMA((side - 1, 2)),
    ]


def small_inverse(matrix):
    size = len(matrix)
    if size == 2:
        (first, off), (_, last) = matrix
        scale = 1.0 / (first * last - off * off)
        cross = -off * scale
        return [[last * scale, cross], [cross, first * scale]]
    half = size // 2

    def product(left, right):
        return [
            [sum(left[i][k] * right[k][j] for k in range(1, half)) + left[i][0] * right[0][j] for j in range(half)]
            for i in range(half)
        ]

    corner = small_inverse([row[:half] for row in matrix[:half]])
    side = [row[half:] for row in matrix[:half]]
    solved = product(corner, side)
    lowered = product([list(column) for column in zip(*side)], solved)
    rest = small_inverse(
        [[matrix[half + i][half + j] - lowered[i][j] for j in range(half)] for i in range(half)]
    )
    spread = product(solved, rest)
    update = product(spread, [list(column) for column in zip(*solved)])
    top = [
        [corner[i][j] + update[i][j] for j in range(half)] + [-spread[i][j] for j in range(half)]
        for i in range(half)
    ]
    bottom = [[-spread[j][i] for j in range(half)] + rest[i] for i in range(half)]
    return top + bottom


def invert(work, first_block, last_block):
    width = work.shape[0]
    down = lax.broadcasted_iota(jnp.int32, (BLOCK, BLOCK), 0)
    across = lax.broadcasted_iota(jnp.int32, (BLOCK, BLOCK), 1)
    lanes = lax.broadcasted_iota(jnp.int32, (BLOCK, width), 1) // BLOCK
    rows = lax.broadcasted_iota(jnp.int32, (width, BLOCK), 0) // BLOCK
    full_lanes = lax.broadcasted_iota(jnp.int32, (width, width), 1) // BLOCK
    steps = range(PIVOTS)
    for block in range(first_block, last_block):
        span = slice(block * BLOCK, (block + 1) * BLOCK)
        pivot = work[span, span]
        for at in range(0, BLOCK, PIVOTS):
            columns = [
                jnp.broadcast_to(pivot[:, at + i : at + i + 1], (BLOCK, BLOCK)) for i in steps
            ]
            inverse = small_inverse(
                [
                    [columns[max(i, j)][at + min(i, j) : at + min(i, j) + 1, :] for j in steps]
                    for i in steps
                ]
            )
            fresh = []
            for i in steps:
                row = inverse[i][0] * pivot[at : at + 1, :]
                for j in steps[1:]:
                    row = row + inverse[i][j] * pivot[at + j : at + j + 1, :]
                for j in steps:
                    row = jnp.where(across[:1] == at + j, inverse[i][j], row)
                fresh.append(row)
            after = jnp.where((across >= at) & (across < at + PIVOTS), 0.0, pivot)
            for i in steps:
                after = after - columns[i] * fresh[i]
            for i in steps:
                after = jnp.where(down == at + i, fresh[i], after)
            pivot = after
        panel = dot(pivot, work[span, :])
        panel = jnp.where(lanes == block, jnp.concatenate([pivot] * (width // BLOCK), axis=1), panel)
        column = jnp.where(rows == block, 0.0, work[:, span])
        kept = jnp.where(full_lanes == block, 0.0, work[...])
        work[...] = kept - dot(column, panel)
        work[span, :] = panel


def gather_kernel(
    axis_sizes, side, step_rows, item_factor, context_factor, items, context, gram_rows, context_gram,
    own_rows, loaded, load_sems, own_sems, sibling_sems,
    gram, by_user, by_slow, by_fast, user_sems, slow_sems, fast_sems,
):
    users, items_extent = axis_sizes
    everyone = (("user", users), ("item", items_extent))
    user, item = lax.axis_index("user"), lax.axis_index("item")
    slow, fast, at_slow, at_fast = torus(side)
    steps = context_factor.shape[0] // step_rows
    pairs = step_rows // PAIR
    greet(everyone)

    def load(step):
        span = pl.ds(pl.multiple_of(step * step_rows, step_rows), step_rows)
        return pltpu.make_async_copy(context_factor.at[span], loaded.at[step], load_sems.at[step])

    def transform(step, carry):
        load(step).wait()
        chunk = loaded[step]
        columns = chunk.T
        for pair in range(pairs):
            context[step * pairs + pair] = columns[:, pair * PAIR : (pair + 1) * PAIR].astype(
                jnp.bfloat16
            )
        context_gram[...] += gram_of(columns)
        return carry

    fetch = pltpu.make_async_copy(item_factor, own_rows, load_sems.at[steps])
    fetch.start()
    for step in range(steps):
        load(step).start()
    context_gram[...] = jnp.zeros_like(context_gram)
    fetch.wait()
    columns = own_rows[...].T
    for pair in range(items.shape[1]):
        items[user, pair] = columns[:, pair * PAIR : (pair + 1) * PAIR].astype(jnp.bfloat16)
    gram[...] = gram_of(columns)
    await_greetings(everyone)
    first = gram_to_users(gram, by_user, user_sems, users)
    core = lax.rem(user, 2)
    sibling = user + 1 - 2 * core
    own = []
    for ahead in HOPS:
        peer = lax.rem(user + 2 * ahead, users)
        own.append(copy_to(items.at[user], items.at[user], own_sems.at[ahead - 1], peer, item))
    forwarded = [copy_to(items.at[user], items.at[user], sibling_sems.at[0], sibling, item)]

    def forward(at):
        own[at].wait_recv()
        block = items.at[lax.rem(user + users - 2 * HOPS[at], users)]
        forwarded.append(copy_to(block, block, sibling_sems.at[1 + at], sibling, item))

    lax.fori_loop(0, PLAN[0], transform, 0)
    second = exchange(first, by_user, slow, at_slow, by_slow, slow_sems)
    forward(0)
    forward(1)
    lax.fori_loop(PLAN[0], PLAN[0] + PLAN[1], transform, 0)
    third = exchange(second, by_slow, fast, at_fast, by_fast, fast_sems)
    forward(2)
    lax.fori_loop(PLAN[0] + PLAN[1], steps, transform, 0)
    receive(third)
    gram_rows[...] = jnp.sum(by_fast[...], axis=0)
    receive(forwarded)
    for copy in first + own + forwarded + second + third:
        copy.wait_send()


def gather_items(item_factor, context_factor, axis_sizes, side):
    users, items = axis_sizes
    rows, width = item_factor.shape
    contexts = context_factor.shape[0]
    step_rows = 512
    return pl.pallas_call(
        functools.partial(gather_kernel, axis_sizes, side, step_rows),
        out_shape=(
            jax.ShapeDtypeStruct((users, rows // PAIR, width, PAIR), jnp.bfloat16),
            jax.ShapeDtypeStruct((contexts // PAIR, width, PAIR), jnp.bfloat16),
            jax.ShapeDtypeStruct((width // users, width), jnp.float32),
            jax.ShapeDtypeStruct((width, width), jnp.float32),
        ),
        in_specs=[pl.BlockSpec(memory_space=pltpu.HBM)] * 2,
        out_specs=(VMEM_SPEC,) * 4,
        scratch_shapes=[
            pltpu.VMEM((rows, width), jnp.float32),
            pltpu.VMEM((contexts // step_rows, step_rows, width), jnp.float32),
            pltpu.SemaphoreType.DMA((contexts // step_rows + 1,)),
            pltpu.SemaphoreType.DMA((users // 2 - 1, 2)),
            pltpu.SemaphoreType.DMA((users // 2, 2)),
        ]
        + gram_scratch(users, side, width),
        compiler_params=pltpu.CompilerParams(
            collective_id=0, has_side_effects=True, vmem_limit_bytes=16 * 2**20
        ),
        name="gather_items",
    )(
        pltpu.with_memory_space_constraint(item_factor, pltpu.HBM),
        pltpu.with_memory_space_constraint(context_factor, pltpu.HBM),
    )


def user_kernel(
    axis_sizes, side, partial, gram_rows, context_gram, raw, gathered, raw_gram, arrived, mixed, settled,
    work, far_sems, near_sems, out_sems, on_sems, system_sems, raw_block, raw_sems,
    gram, by_user, by_slow, by_fast, user_sems, slow_sems, fast_sems,
):
    users, items = axis_sizes
    user, item = lax.axis_index("user"), lax.axis_index("item")
    slow, fast, at_slow, at_fast = torus(side)
    half = partial.shape[2] // 2
    blocks = work.shape[0] // BLOCK
    everyone = (("user", users), ("item", items))
    greet(everyone)
    await_greetings(everyone)
    system = blocks_back(gram_rows, work, system_sems, users)

    far = []
    for ahead in HOPS:
        far.append(
            copy_to(
                partial.at[lax.rem(slow + ahead, side), :, pl.ds(0, half)],
                arrived.at[0, ahead - 1],
                far_sems.at[0, ahead - 1],
                user,
                at_slow(ahead),
            )
        )
        far.append(
            copy_to(
                partial.at[:, lax.rem(fast + ahead, side), pl.ds(half, half)],
                arrived.at[1, ahead - 1],
                far_sems.at[1, ahead - 1],
                user,
                at_fast(ahead),
            )
        )
    receive(system)
    work[...] = work[...] * context_gram[...]
    invert(work, 0, SPLIT)

    def combine(part, where):
        own = partial[slow, where, :half] if part == 0 else partial[where, fast, half:]
        total = own.astype(jnp.float32)
        for ahead in range(side - 1):
            total = total + arrived[part, ahead, where].astype(jnp.float32)
        return total

    near = []
    kept = []
    for part in range(2):
        receive(far[part::2])
        here = fast if part == 0 else slow
        for ahead in HOPS:
            where = lax.rem(here + ahead, side)
            mixed[part, ahead - 1] = combine(part, where).astype(mixed.dtype)
            near.append(
                copy_to(
                    mixed.at[part, ahead - 1],
                    settled.at[part, ahead - 1],
                    near_sems.at[part, ahead - 1],
                    user,
                    at_fast(ahead) if part == 0 else at_slow(ahead),
                )
            )
        kept.append(combine(part, here))
    invert(work, SPLIT, blocks)
    receive(near)
    total = jnp.concatenate(
        [
            kept[part] + sum(settled[part, at].astype(jnp.float32) for at in range(side - 1))
            for part in range(2)
        ],
        axis=0,
    )
    raw[...] = dot(total, work[...])
    columns = raw[...].T
    for part in range(2):
        gathered[item, part] = columns[:, part * PAIR : (part + 1) * PAIR].astype(jnp.bfloat16)

    onward = []

    def pass_on(block, part, stage):
        for ahead in HOPS:
            onward.append(
                copy_to(
                    gathered.at[block, part],
                    gathered.at[block, part],
                    on_sems.at[part, stage, ahead - 1],
                    user,
                    at_fast(ahead) if part == 0 else at_slow(ahead),
                )
            )

    outward = []
    for ahead in HOPS:
        for part in range(2):
            outward.append(
                copy_to(
                    gathered.at[item, part],
                    gathered.at[item, part],
                    out_sems.at[part, ahead - 1],
                    user,
                    at_slow(ahead) if part == 0 else at_fast(ahead),
                )
            )
    gram[...] = gram_of(columns)
    first = gram_to_users(gram, by_user, user_sems, users)
    for part in range(2):
        pass_on(item, part, 0)

    def forward(at):
        for part in range(2):
            outward[2 * at + part].wait_recv()
            back = side - HOPS[at]
            pass_on(at_slow(back) if part == 0 else at_fast(back), part, HOPS[at])

    second = exchange(first, by_user, slow, at_slow, by_slow, slow_sems)
    forward(0)
    third = exchange(second, by_slow, fast, at_fast, by_fast, fast_sems)
    forward(1)
    forward(2)
    receive(third)
    raw_block[...] = jnp.sum(by_fast[...], axis=0)
    fourth = blocks_back(raw_block, raw_gram, raw_sems, users)
    receive(onward)
    receive(fourth)
    for copy in system + far + near + outward + onward + first + second + third + fourth:
        copy.wait_send()


def update_users(partial, gram_rows, context_gram, axis_sizes):
    users, items = axis_sizes
    side, _, rows, width = partial.shape
    half = rows // 2
    square = jax.ShapeDtypeStruct((width, width), jnp.float32)
    return pl.pallas_call(
        functools.partial(user_kernel, axis_sizes, side),
        out_shape=(
            jax.ShapeDtypeStruct((rows, width), jnp.float32),
            jax.ShapeDtypeStruct((items, rows // PAIR, width, PAIR), jnp.bfloat16),
            square,
        ),
        in_specs=[VMEM_SPEC] * 3,
        out_specs=(VMEM_SPEC,) * 3,
        scratch_shapes=[
            pltpu.VMEM((2, side - 1, side, half, width), jnp.bfloat16),
            pltpu.VMEM((2, side - 1, half, width), jnp.bfloat16),
            pltpu.VMEM((2, side - 1, half, width), jnp.bfloat16),
            pltpu.VMEM((width, width), jnp.float32),
            pltpu.SemaphoreType.DMA((2, side - 1, 2)),
            pltpu.SemaphoreType.DMA((2, side - 1, 2)),
            pltpu.SemaphoreType.DMA((2, side - 1, 2)),
            pltpu.SemaphoreType.DMA((2, side, side - 1, 2)),
            pltpu.SemaphoreType.DMA((2, users - 1)),
            pltpu.VMEM((width // users, width), jnp.float32),
            pltpu.SemaphoreType.DMA((2, users - 1)),
        ]
        + gram_scratch(users, side, width),
        compiler_params=pltpu.CompilerParams(
            collective_id=1, has_side_effects=True, vmem_limit_bytes=24 * 2**20
        ),
        name="update_users",
    )(partial, gram_rows, context_gram)


def item_kernel(
    axis_sizes, partial, raw_gram, context_gram, raw, new_items, user_factor, arrived, work,
    user_sums, item_sums, user_sems, item_sems, sems
):
    users, items = axis_sizes
    user, item = lax.axis_index("user"), lax.axis_index("item")
    everyone = (("user", users), ("item", items))
    greet(everyone)
    await_greetings(everyone)
    copies = send_all(
        "user",
        users,
        lambda peer, ahead: partial.at[peer],
        lambda me, ahead: arrived.at[ahead - 1],
        sems,
    )
    width = work.shape[0]
    rows_total = jnp.float32(user_factor.shape[0] * users * items)
    down = lax.broadcasted_iota(jnp.int32, (width, width), 0)
    across = lax.broadcasted_iota(jnp.int32, (width, width), 1)
    diagonal = jnp.where(down == across, raw_gram[...], 0.0)
    scale_row = jnp.sqrt(rows_total / (jnp.sum(diagonal, axis=0, keepdims=True) + 1e-06))
    scale_column = jnp.sqrt(rows_total / (jnp.sum(diagonal, axis=1, keepdims=True) + 1e-06))
    user_factor[...] = raw[...] * scale_row
    work[...] = raw_gram[...] * scale_column * scale_row * context_gram[...]
    invert(work, 0, width // BLOCK)
    total = partial[user].astype(jnp.float32)
    for ahead in range(1, users):
        copies[ahead - 1].wait_recv()
        total = total + arrived[ahead - 1].astype(jnp.float32)
    item_raw = dot(total * scale_row, work[...])
    squares = jnp.sum(item_raw * item_raw, axis=0, keepdims=True)
    user_sums[user] = jnp.broadcast_to(squares, user_sums.shape[1:])
    first = send_all(
        "user", users, lambda peer, ahead: user_sums.at[user], lambda me, ahead: user_sums.at[me], user_sems
    )
    receive(first)
    item_sums[item] = jnp.sum(user_sums[...], axis=0)
    second = send_all(
        "item", items, lambda peer, ahead: item_sums.at[item], lambda me, ahead: item_sums.at[me], item_sems
    )
    receive(second)
    squares = jnp.sum(item_sums[...], axis=0)[:1]
    new_items[...] = item_raw * jnp.sqrt(rows_total / (squares + 1e-06))
    for copy in copies + first + second:
        copy.wait_send()


def update_items(partial, raw_gram, context_gram, raw, axis_sizes):
    users, items = axis_sizes
    _, rows, width = partial.shape
    out = jax.ShapeDtypeStruct((rows, width), jnp.float32)
    return pl.pallas_call(
        functools.partial(item_kernel, axis_sizes),
        out_shape=(out, out),
        in_specs=[VMEM_SPEC] * 4,
        out_specs=(VMEM_SPEC,) * 2,
        scratch_shapes=[
            pltpu.VMEM((users - 1, rows, width), jnp.bfloat16),
            pltpu.VMEM((width, width), jnp.float32),
            pltpu.VMEM((users, 8, width), jnp.float32),
            pltpu.VMEM((items, 8, width), jnp.float32),
            pltpu.SemaphoreType.DMA((2, users - 1)),
            pltpu.SemaphoreType.DMA((2, items - 1)),
            pltpu.SemaphoreType.DMA((2, users - 1)),
        ],
        compiler_params=pltpu.CompilerParams(
            collective_id=2, has_side_effects=True, vmem_limit_bytes=16 * 2**20
        ),
        name="update_items",
    )(partial, raw_gram, context_gram, raw)


def local(
    item_factor, context_factor, tile_count, tile_rows, tile_cols, tile_ctx, nz_offsets, nz_values
):
    axis_sizes = (lax.axis_size("user"), lax.axis_size("item"))
    users, items = axis_sizes
    rows, width = item_factor.shape
    side = math.isqrt(items)
    count = tile_count.reshape(1)
    ids = (tile_rows[0, 0], tile_cols[0, 0], tile_ctx[0, 0])
    offsets = nz_offsets[0, 0]
    values = nz_values[0, 0]
    item_pairs, context_pairs, gram_rows, context_gram = gather_items(
        item_factor, context_factor, axis_sizes, side
    )
    partial_users = mttkrp(
        0, count, ids, offsets, values, item_pairs.reshape(-1, width, PAIR), context_pairs,
        items * rows // TILE,
    )
    raw, user_pairs, raw_gram = update_users(
        partial_users.reshape(side, side, rows, width), gram_rows, context_gram, axis_sizes
    )
    partial_items = mttkrp(
        1, count, ids, offsets, values, user_pairs.reshape(-1, width, PAIR), context_pairs,
        users * rows // TILE,
    )
    new_items, user_factor = update_items(
        partial_items.reshape(users, rows, width), raw_gram, context_gram, raw, axis_sizes
    )
    return (user_factor, new_items)


def solution(mesh):
    in_specs = (
        P(("item", "user"), None),
        P(),
        P("user", "item"),
        P("user", "item", None),
        P("user", "item", None),
        P("user", "item", None),
        P("user", "item", None, None, None),
        P("user", "item", None, None),
    )
    out_specs = (P(("user", "item"), None), P(("item", "user"), None))
    return jax.shard_map(local, mesh=mesh, in_specs=in_specs, out_specs=out_specs, check_vma=False)
```

```python
import functools
import math

import jax
import jax.numpy as jnp
from jax import lax
from jax.experimental import pallas as pl
from jax.experimental.pallas import tpu as pltpu
from jax.sharding import PartitionSpec as P

TILE = 64
UNROLL = 32
CONTEXT_STEPS = (3, 2)
PAIR = 2 * TILE
BLOCK = 64
SPLIT = 2
HOPS = (1, 3, 2)
PIVOTS = 4
HIGHEST = lax.Precision.HIGHEST
MESH = pl.DeviceIdType.MESH
VMEM_SPEC = pl.BlockSpec(memory_space=pltpu.VMEM)
SMEM_SPEC = pl.BlockSpec(memory_space=pltpu.SMEM)


def dot(left, right):
    return jnp.dot(left, right, precision=HIGHEST, preferred_element_type=jnp.float32)


def gram_of(columns):
    return lax.dot_general(
        columns,
        columns,
        (((1,), (1,)), ((), ())),
        precision=HIGHEST,
        preferred_element_type=jnp.float32,
    )


def mttkrp_kernel(
    target_at,
    count,
    target_ids,
    source_ids,
    context_ids,
    offsets,
    values,
    source,
    context,
    out,
    totals,
    tiles,
):
    totals[...] = jnp.zeros_like(totals)

    def unpack(pair, carry):
        for half in range(2):
            tiles[2 * pair + half] = source[pair][:, half * TILE : (half + 1) * TILE]
        return carry

    lax.fori_loop(0, source.shape[0], unpack, 0)
    rank, entries = totals.shape[2], offsets.shape[2]

    def one_hot(row, extent):
        positions = lax.broadcasted_iota(jnp.int32, (extent, entries), 0)
        return jnp.where(positions == row, 1.0, 0.0).astype(jnp.bfloat16)

    def lanes_of(pair, row):
        wide = pair.astype(jnp.float32)
        picked = [
            jnp.take_along_axis(
                wide,
                jnp.broadcast_to(row[:, at : at + PAIR], (rank, PAIR)),
                axis=1,
                mode="promise_in_bounds",
            )
            for at in range(0, entries, PAIR)
        ]
        return jnp.concatenate(picked, axis=1)

    def group(step, carry):
        first = pl.multiple_of(step * UNROLL, UNROLL)
        targets = offsets[target_at, pl.ds(first, UNROLL), :]
        sources = offsets[1 - target_at, pl.ds(first, UNROLL), :]
        contexts = offsets[2, pl.ds(first, UNROLL), :]
        weights = values[pl.ds(first, UNROLL), :]
        for at in range(UNROLL):
            row = slice(at, at + 1)
            source_id, context_id = source_ids[first + at], context_ids[first + at]
            context_row = contexts[row] + TILE * lax.rem(context_id, 2)
            source_part = jnp.dot(
                tiles[source_id],
                one_hot(sources[row], TILE),
                preferred_element_type=jnp.float32,
            )
            context_part = lanes_of(context[lax.div(context_id, 2)], context_row)
            weight = jnp.where(first + at < count[0], weights[row], 0.0)
            terms = (weight * source_part * context_part).astype(jnp.bfloat16)
            totals[target_ids[first + at]] += lax.dot_general(
                one_hot(targets[row], TILE),
                terms,
                (((1,), (1,)), ((), ())),
                preferred_element_type=jnp.float32,
            )
        return carry

    lax.fori_loop(0, (count[0] + UNROLL - 1) // UNROLL, group, 0)
    out[...] = totals[...].astype(out.dtype)


def mttkrp(target_at, count, ids, offsets, values, source_pairs, context_pairs, tiles):
    shape = (tiles, TILE, source_pairs.shape[1])
    return pl.pallas_call(
        functools.partial(mttkrp_kernel, target_at),
        out_shape=jax.ShapeDtypeStruct(shape, jnp.bfloat16),
        in_specs=[SMEM_SPEC] * 4 + [VMEM_SPEC] * 4,
        out_specs=VMEM_SPEC,
        scratch_shapes=[
            pltpu.VMEM(shape, jnp.float32),
            pltpu.VMEM((2 * source_pairs.shape[0], shape[2], TILE), jnp.bfloat16),
        ],
        compiler_params=pltpu.CompilerParams(vmem_limit_bytes=24 * 2**20),
        name="mttkrp",
    )(
        count,
        ids[target_at],
        ids[1 - target_at],
        ids[2],
        offsets,
        values,
        source_pairs,
        context_pairs,
    )


def greet(groups):
    barrier = pltpu.get_barrier_semaphore()
    for axis, size in groups:
        me = lax.axis_index(axis)
        for ahead in range(1, size):
            pl.semaphore_signal(
                barrier, inc=1, device_id={axis: lax.rem(me + ahead, size)}, device_id_type=MESH
            )


def await_greetings(groups):
    pl.semaphore_wait(pltpu.get_barrier_semaphore(), sum(size - 1 for _, size in groups))


def send_all(axis, size, source, target, sems):
    me = lax.axis_index(axis)
    copies = []
    for ahead in range(1, size):
        peer = lax.rem(me + ahead, size)
        copy = pltpu.make_async_remote_copy(
            src_ref=source(peer, ahead),
            dst_ref=target(me, ahead),
            send_sem=sems.at[0, ahead - 1],
            recv_sem=sems.at[1, ahead - 1],
            device_id={axis: peer},
            device_id_type=MESH,
        )
        copy.start()
        copies.append(copy)
    return copies


def copy_to(source, target, sems, user, item):
    copy = pltpu.make_async_remote_copy(
        src_ref=source,
        dst_ref=target,
        send_sem=sems.at[0],
        recv_sem=sems.at[1],
        device_id=(user, item),
        device_id_type=MESH,
    )
    copy.start()
    return copy


def receive(copies):
    for copy in copies:
        copy.wait_recv()


def rows_of(item, rows):
    return pl.ds(pl.multiple_of(item * rows, rows), rows)


def gram_to_users(gram, by_user, sems, users):
    rows = by_user.shape[1]
    user = lax.axis_index("user")
    by_user[user] = gram[rows_of(user, rows), :]
    return send_all(
        "user",
        users,
        lambda peer, ahead: gram.at[rows_of(peer, rows)],
        lambda me, ahead: by_user.at[me],
        sems,
    )


def torus(side):
    item = lax.axis_index("item")
    slow, fast = item // side, lax.rem(item, side)

    def at_slow(ahead):
        return lax.rem(slow + ahead, side) * side + fast

    def at_fast(ahead):
        return slow * side + lax.rem(fast + ahead, side)

    return slow, fast, at_slow, at_fast


def exchange(before, terms, place, along, spread, sems):
    receive(before)
    spread[place] = jnp.sum(terms[...], axis=0)
    user = lax.axis_index("user")
    return [
        copy_to(spread.at[place], spread.at[place], sems.at[ahead - 1], user, along(ahead))
        for ahead in HOPS
    ]


def blocks_back(block, result, sems, users):
    rows = block.shape[0]
    span = rows_of(lax.axis_index("user"), rows)
    result[span, :] = block[...]
    return send_all("user", users, lambda peer, ahead: block, lambda me, ahead: result.at[span], sems)


def gram_scratch(users, side, width):
    rows = width // users
    return [
        pltpu.VMEM((width, width), jnp.float32),
        pltpu.VMEM((users, rows, width), jnp.float32),
        pltpu.VMEM((side, rows, width), jnp.float32),
        pltpu.VMEM((side, rows, width), jnp.float32),
        pltpu.SemaphoreType.DMA((2, users - 1)),
        pltpu.SemaphoreType.DMA((side - 1, 2)),
        pltpu.SemaphoreType.DMA((side - 1, 2)),
    ]


def small_inverse(matrix):
    size = len(matrix)
    if size == 2:
        (first, off), (_, last) = matrix
        scale = 1.0 / (first * last - off * off)
        cross = -off * scale
        return [[last * scale, cross], [cross, first * scale]]
    half = size // 2

    def product(left, right):
        return [
            [sum(left[i][k] * right[k][j] for k in range(1, half)) + left[i][0] * right[0][j] for j in range(half)]
            for i in range(half)
        ]

    corner = small_inverse([row[:half] for row in matrix[:half]])
    side = [row[half:] for row in matrix[:half]]
    solved = product(corner, side)
    lowered = product([list(column) for column in zip(*side)], solved)
    rest = small_inverse(
        [[matrix[half + i][half + j] - lowered[i][j] for j in range(half)] for i in range(half)]
    )
    spread = product(solved, rest)
    update = product(spread, [list(column) for column in zip(*solved)])
    top = [
        [corner[i][j] + update[i][j] for j in range(half)] + [-spread[i][j] for j in range(half)]
        for i in range(half)
    ]
    bottom = [[-spread[j][i] for j in range(half)] + rest[i] for i in range(half)]
    return top + bottom


def invert(work, first_block, last_block):
    width = work.shape[0]
    down = lax.broadcasted_iota(jnp.int32, (BLOCK, BLOCK), 0)
    across = lax.broadcasted_iota(jnp.int32, (BLOCK, BLOCK), 1)
    lanes = lax.broadcasted_iota(jnp.int32, (BLOCK, width), 1) // BLOCK
    rows = lax.broadcasted_iota(jnp.int32, (width, BLOCK), 0) // BLOCK
    full_lanes = lax.broadcasted_iota(jnp.int32, (width, width), 1) // BLOCK
    steps = range(PIVOTS)
    for block in range(first_block, last_block):
        span = slice(block * BLOCK, (block + 1) * BLOCK)
        pivot = work[span, span]
        for at in range(0, BLOCK, PIVOTS):
            columns = [
                jnp.broadcast_to(pivot[:, at + i : at + i + 1], (BLOCK, BLOCK)) for i in steps
            ]
            inverse = small_inverse(
                [
                    [columns[max(i, j)][at + min(i, j) : at + min(i, j) + 1, :] for j in steps]
                    for i in steps
                ]
            )
            fresh = []
            for i in steps:
                row = inverse[i][0] * pivot[at : at + 1, :]
                for j in steps[1:]:
                    row = row + inverse[i][j] * pivot[at + j : at + j + 1, :]
                for j in steps:
                    row = jnp.where(across[:1] == at + j, inverse[i][j], row)
                fresh.append(row)
            after = jnp.where((across >= at) & (across < at + PIVOTS), 0.0, pivot)
            for i in steps:
                after = after - columns[i] * fresh[i]
            for i in steps:
                after = jnp.where(down == at + i, fresh[i], after)
            pivot = after
        panel = dot(pivot, work[span, :])
        panel = jnp.where(lanes == block, jnp.concatenate([pivot] * (width // BLOCK), axis=1), panel)
        column = jnp.where(rows == block, 0.0, work[:, span])
        kept = jnp.where(full_lanes == block, 0.0, work[...])
        work[...] = kept - dot(column, panel)
        work[span, :] = panel


def gather_kernel(
    axis_sizes, side, step_rows, item_factor, context_factor, items, context, gram_rows, context_gram,
    own_rows, loaded, load_sems, own_sems, sibling_sems,
    gram, by_user, by_slow, by_fast, user_sems, slow_sems, fast_sems,
):
    users, items_extent = axis_sizes
    everyone = (("user", users), ("item", items_extent))
    user, item = lax.axis_index("user"), lax.axis_index("item")
    slow, fast, at_slow, at_fast = torus(side)
    steps = context_factor.shape[0] // step_rows
    pairs = step_rows // PAIR
    greet(everyone)

    def load(step):
        span = pl.ds(pl.multiple_of(step * step_rows, step_rows), step_rows)
        return pltpu.make_async_copy(context_factor.at[span], loaded.at[step], load_sems.at[step])

    def transform(step, carry):
        load(step).wait()
        chunk = loaded[step]
        columns = chunk.T
        for pair in range(pairs):
            context[step * pairs + pair] = columns[:, pair * PAIR : (pair + 1) * PAIR].astype(
                jnp.bfloat16
            )
        context_gram[...] += gram_of(columns)
        return carry

    fetch = pltpu.make_async_copy(item_factor, own_rows, load_sems.at[steps])
    fetch.start()
    for step in range(steps):
        load(step).start()
    context_gram[...] = jnp.zeros_like(context_gram)
    fetch.wait()
    columns = own_rows[...].T
    for pair in range(items.shape[1]):
        items[user, pair] = columns[:, pair * PAIR : (pair + 1) * PAIR].astype(jnp.bfloat16)
    gram[...] = gram_of(columns)
    await_greetings(everyone)
    first = gram_to_users(gram, by_user, user_sems, users)
    core = lax.rem(user, 2)
    sibling = user + 1 - 2 * core
    own = []
    for ahead in HOPS:
        peer = lax.rem(user + 2 * ahead, users)
        own.append(copy_to(items.at[user], items.at[user], own_sems.at[ahead - 1], peer, item))
    forwarded = [copy_to(items.at[user], items.at[user], sibling_sems.at[0], sibling, item)]

    def forward(at):
        own[at].wait_recv()
        block = items.at[lax.rem(user + users - 2 * HOPS[at], users)]
        forwarded.append(copy_to(block, block, sibling_sems.at[1 + at], sibling, item))

    lax.fori_loop(0, CONTEXT_STEPS[0], transform, 0)
    second = exchange(first, by_user, slow, at_slow, by_slow, slow_sems)
    forward(0)
    forward(1)
    lax.fori_loop(CONTEXT_STEPS[0], CONTEXT_STEPS[0] + CONTEXT_STEPS[1], transform, 0)
    third = exchange(second, by_slow, fast, at_fast, by_fast, fast_sems)
    forward(2)
    lax.fori_loop(CONTEXT_STEPS[0] + CONTEXT_STEPS[1], steps, transform, 0)
    receive(third)
    gram_rows[...] = jnp.sum(by_fast[...], axis=0)
    receive(forwarded)
    for copy in first + own + forwarded + second + third:
        copy.wait_send()


def gather_items(item_factor, context_factor, axis_sizes, side):
    users, items = axis_sizes
    rows, width = item_factor.shape
    contexts = context_factor.shape[0]
    step_rows = 512
    return pl.pallas_call(
        functools.partial(gather_kernel, axis_sizes, side, step_rows),
        out_shape=(
            jax.ShapeDtypeStruct((users, rows // PAIR, width, PAIR), jnp.bfloat16),
            jax.ShapeDtypeStruct((contexts // PAIR, width, PAIR), jnp.bfloat16),
            jax.ShapeDtypeStruct((width // users, width), jnp.float32),
            jax.ShapeDtypeStruct((width, width), jnp.float32),
        ),
        in_specs=[pl.BlockSpec(memory_space=pltpu.HBM)] * 2,
        out_specs=(VMEM_SPEC,) * 4,
        scratch_shapes=[
            pltpu.VMEM((rows, width), jnp.float32),
            pltpu.VMEM((contexts // step_rows, step_rows, width), jnp.float32),
            pltpu.SemaphoreType.DMA((contexts // step_rows + 1,)),
            pltpu.SemaphoreType.DMA((users // 2 - 1, 2)),
            pltpu.SemaphoreType.DMA((users // 2, 2)),
        ]
        + gram_scratch(users, side, width),
        compiler_params=pltpu.CompilerParams(
            collective_id=0, has_side_effects=True, vmem_limit_bytes=16 * 2**20
        ),
        name="gather_items",
    )(
        pltpu.with_memory_space_constraint(item_factor, pltpu.HBM),
        pltpu.with_memory_space_constraint(context_factor, pltpu.HBM),
    )


def user_kernel(
    axis_sizes, side, partial, gram_rows, context_gram, raw, gathered, raw_gram, arrived, mixed, settled,
    work, far_sems, near_sems, out_sems, on_sems, system_sems, raw_block, raw_sems,
    gram, by_user, by_slow, by_fast, user_sems, slow_sems, fast_sems,
):
    users, items = axis_sizes
    user, item = lax.axis_index("user"), lax.axis_index("item")
    slow, fast, at_slow, at_fast = torus(side)
    half = partial.shape[2] // 2
    blocks = work.shape[0] // BLOCK
    everyone = (("user", users), ("item", items))
    greet(everyone)
    await_greetings(everyone)
    system = blocks_back(gram_rows, work, system_sems, users)

    far = []
    for ahead in HOPS:
        far.append(
            copy_to(
                partial.at[lax.rem(slow + ahead, side), :, pl.ds(0, half)],
                arrived.at[0, ahead - 1],
                far_sems.at[0, ahead - 1],
                user,
                at_slow(ahead),
            )
        )
        far.append(
            copy_to(
                partial.at[:, lax.rem(fast + ahead, side), pl.ds(half, half)],
                arrived.at[1, ahead - 1],
                far_sems.at[1, ahead - 1],
                user,
                at_fast(ahead),
            )
        )
    receive(system)
    work[...] = work[...] * context_gram[...]
    invert(work, 0, SPLIT)

    def combine(part, where):
        own = partial[slow, where, :half] if part == 0 else partial[where, fast, half:]
        total = own.astype(jnp.float32)
        for ahead in range(side - 1):
            total = total + arrived[part, ahead, where].astype(jnp.float32)
        return total

    near = []
    kept = []
    for part in range(2):
        receive(far[part::2])
        here = fast if part == 0 else slow
        for ahead in HOPS:
            where = lax.rem(here + ahead, side)
            mixed[part, ahead - 1] = combine(part, where).astype(mixed.dtype)
            near.append(
                copy_to(
                    mixed.at[part, ahead - 1],
                    settled.at[part, ahead - 1],
                    near_sems.at[part, ahead - 1],
                    user,
                    at_fast(ahead) if part == 0 else at_slow(ahead),
                )
            )
        kept.append(combine(part, here))
    invert(work, SPLIT, blocks)
    receive(near)
    total = jnp.concatenate(
        [
            kept[part] + sum(settled[part, at].astype(jnp.float32) for at in range(side - 1))
            for part in range(2)
        ],
        axis=0,
    )
    raw[...] = dot(total, work[...])
    columns = raw[...].T
    for part in range(2):
        gathered[item, part] = columns[:, part * PAIR : (part + 1) * PAIR].astype(jnp.bfloat16)

    onward = []

    def pass_on(block, part, stage):
        for ahead in HOPS:
            onward.append(
                copy_to(
                    gathered.at[block, part],
                    gathered.at[block, part],
                    on_sems.at[part, stage, ahead - 1],
                    user,
                    at_fast(ahead) if part == 0 else at_slow(ahead),
                )
            )

    outward = []
    for ahead in HOPS:
        for part in range(2):
            outward.append(
                copy_to(
                    gathered.at[item, part],
                    gathered.at[item, part],
                    out_sems.at[part, ahead - 1],
                    user,
                    at_slow(ahead) if part == 0 else at_fast(ahead),
                )
            )
    gram[...] = gram_of(columns)
    first = gram_to_users(gram, by_user, user_sems, users)
    for part in range(2):
        pass_on(item, part, 0)

    def forward(at):
        for part in range(2):
            outward[2 * at + part].wait_recv()
            back = side - HOPS[at]
            pass_on(at_slow(back) if part == 0 else at_fast(back), part, HOPS[at])

    second = exchange(first, by_user, slow, at_slow, by_slow, slow_sems)
    forward(0)
    third = exchange(second, by_slow, fast, at_fast, by_fast, fast_sems)
    forward(1)
    forward(2)
    receive(third)
    raw_block[...] = jnp.sum(by_fast[...], axis=0)
    fourth = blocks_back(raw_block, raw_gram, raw_sems, users)
    receive(onward)
    receive(fourth)
    for copy in system + far + near + outward + onward + first + second + third + fourth:
        copy.wait_send()


def update_users(partial, gram_rows, context_gram, axis_sizes):
    users, items = axis_sizes
    side, _, rows, width = partial.shape
    half = rows // 2
    square = jax.ShapeDtypeStruct((width, width), jnp.float32)
    return pl.pallas_call(
        functools.partial(user_kernel, axis_sizes, side),
        out_shape=(
            jax.ShapeDtypeStruct((rows, width), jnp.float32),
            jax.ShapeDtypeStruct((items, rows // PAIR, width, PAIR), jnp.bfloat16),
            square,
        ),
        in_specs=[VMEM_SPEC] * 3,
        out_specs=(VMEM_SPEC,) * 3,
        scratch_shapes=[
            pltpu.VMEM((2, side - 1, side, half, width), jnp.bfloat16),
            pltpu.VMEM((2, side - 1, half, width), jnp.bfloat16),
            pltpu.VMEM((2, side - 1, half, width), jnp.bfloat16),
            pltpu.VMEM((width, width), jnp.float32),
            pltpu.SemaphoreType.DMA((2, side - 1, 2)),
            pltpu.SemaphoreType.DMA((2, side - 1, 2)),
            pltpu.SemaphoreType.DMA((2, side - 1, 2)),
            pltpu.SemaphoreType.DMA((2, side, side - 1, 2)),
            pltpu.SemaphoreType.DMA((2, users - 1)),
            pltpu.VMEM((width // users, width), jnp.float32),
            pltpu.SemaphoreType.DMA((2, users - 1)),
        ]
        + gram_scratch(users, side, width),
        compiler_params=pltpu.CompilerParams(
            collective_id=1, has_side_effects=True, vmem_limit_bytes=24 * 2**20
        ),
        name="update_users",
    )(partial, gram_rows, context_gram)


def item_kernel(
    axis_sizes, partial, raw_gram, context_gram, raw, new_items, user_factor, arrived, work,
    user_sums, item_sums, user_sems, item_sems, sems
):
    users, items = axis_sizes
    user, item = lax.axis_index("user"), lax.axis_index("item")
    everyone = (("user", users), ("item", items))
    greet(everyone)
    await_greetings(everyone)
    copies = send_all(
        "user",
        users,
        lambda peer, ahead: partial.at[peer],
        lambda me, ahead: arrived.at[ahead - 1],
        sems,
    )
    width = work.shape[0]
    rows_total = jnp.float32(user_factor.shape[0] * users * items)
    down = lax.broadcasted_iota(jnp.int32, (width, width), 0)
    across = lax.broadcasted_iota(jnp.int32, (width, width), 1)
    diagonal = jnp.where(down == across, raw_gram[...], 0.0)
    scale_row = jnp.sqrt(rows_total / (jnp.sum(diagonal, axis=0, keepdims=True) + 1e-06))
    scale_column = jnp.sqrt(rows_total / (jnp.sum(diagonal, axis=1, keepdims=True) + 1e-06))
    user_factor[...] = raw[...] * scale_row
    work[...] = raw_gram[...] * scale_column * scale_row * context_gram[...]
    invert(work, 0, width // BLOCK)
    total = partial[user].astype(jnp.float32)
    for ahead in range(1, users):
        copies[ahead - 1].wait_recv()
        total = total + arrived[ahead - 1].astype(jnp.float32)
    item_raw = dot(total * scale_row, work[...])
    squares = jnp.sum(item_raw * item_raw, axis=0, keepdims=True)
    user_sums[user] = jnp.broadcast_to(squares, user_sums.shape[1:])
    first = send_all(
        "user", users, lambda peer, ahead: user_sums.at[user], lambda me, ahead: user_sums.at[me], user_sems
    )
    receive(first)
    item_sums[item] = jnp.sum(user_sums[...], axis=0)
    second = send_all(
        "item", items, lambda peer, ahead: item_sums.at[item], lambda me, ahead: item_sums.at[me], item_sems
    )
    receive(second)
    squares = jnp.sum(item_sums[...], axis=0)[:1]
    new_items[...] = item_raw * jnp.sqrt(rows_total / (squares + 1e-06))
    for copy in copies + first + second:
        copy.wait_send()


def update_items(partial, raw_gram, context_gram, raw, axis_sizes):
    users, items = axis_sizes
    _, rows, width = partial.shape
    out = jax.ShapeDtypeStruct((rows, width), jnp.float32)
    return pl.pallas_call(
        functools.partial(item_kernel, axis_sizes),
        out_shape=(out, out),
        in_specs=[VMEM_SPEC] * 4,
        out_specs=(VMEM_SPEC,) * 2,
        scratch_shapes=[
            pltpu.VMEM((users - 1, rows, width), jnp.bfloat16),
            pltpu.VMEM((width, width), jnp.float32),
            pltpu.VMEM((users, 8, width), jnp.float32),
            pltpu.VMEM((items, 8, width), jnp.float32),
            pltpu.SemaphoreType.DMA((2, users - 1)),
            pltpu.SemaphoreType.DMA((2, items - 1)),
            pltpu.SemaphoreType.DMA((2, users - 1)),
        ],
        compiler_params=pltpu.CompilerParams(
            collective_id=2, has_side_effects=True, vmem_limit_bytes=16 * 2**20
        ),
        name="update_items",
    )(partial, raw_gram, context_gram, raw)


def local(
    item_factor, context_factor, tile_count, tile_rows, tile_cols, tile_ctx, nz_offsets, nz_values
):
    axis_sizes = (lax.axis_size("user"), lax.axis_size("item"))
    users, items = axis_sizes
    rows, width = item_factor.shape
    side = math.isqrt(items)
    count = tile_count.reshape(1)
    ids = (tile_rows[0, 0], tile_cols[0, 0], tile_ctx[0, 0])
    offsets = nz_offsets[0, 0]
    values = nz_values[0, 0]
    item_pairs, context_pairs, gram_rows, context_gram = gather_items(
        item_factor, context_factor, axis_sizes, side
    )
    partial_users = mttkrp(
        0, count, ids, offsets, values, item_pairs.reshape(-1, width, PAIR), context_pairs,
        items * rows // TILE,
    )
    raw, user_pairs, raw_gram = update_users(
        partial_users.reshape(side, side, rows, width), gram_rows, context_gram, axis_sizes
    )
    partial_items = mttkrp(
        1, count, ids, offsets, values, user_pairs.reshape(-1, width, PAIR), context_pairs,
        users * rows // TILE,
    )
    new_items, user_factor = update_items(
        partial_items.reshape(users, rows, width), raw_gram, context_gram, raw, axis_sizes
    )
    return (user_factor, new_items)


def solution(mesh):
    in_specs = (
        P(("item", "user"), None),
        P(),
        P("user", "item"),
        P("user", "item", None),
        P("user", "item", None),
        P("user", "item", None),
        P("user", "item", None, None, None),
        P("user", "item", None, None),
    )
    out_specs = (P(("user", "item"), None), P(("item", "user"), None))
    return jax.shard_map(local, mesh=mesh, in_specs=in_specs, out_specs=out_specs, check_vma=False)
```

```python
import functools
import math

import jax
import jax.numpy as jnp
from jax import lax
from jax.experimental import pallas as pl
from jax.experimental.pallas import tpu as pltpu
from jax.sharding import PartitionSpec as P

TILE = 64
UNROLL = 32
CONTEXT_STEPS = (3, 2)
PAIR = 2 * TILE
BLOCK = 64
SPLIT = 2
HOPS = (1, 3, 2)
PIVOTS = 4
HIGHEST = lax.Precision.HIGHEST
MESH = pl.DeviceIdType.MESH
VMEM_SPEC = pl.BlockSpec(memory_space=pltpu.VMEM)
SMEM_SPEC = pl.BlockSpec(memory_space=pltpu.SMEM)


def dot(left, right):
    return jnp.dot(left, right, precision=HIGHEST, preferred_element_type=jnp.float32)


def gram_of(columns):
    return lax.dot_general(
        columns,
        columns,
        (((1,), (1,)), ((), ())),
        precision=HIGHEST,
        preferred_element_type=jnp.float32,
    )


def mttkrp_kernel(
    target_at,
    count,
    target_ids,
    source_ids,
    context_ids,
    offsets,
    values,
    source,
    context,
    out,
    totals,
):
    totals[...] = jnp.zeros_like(totals)
    rank, entries = totals.shape[2], offsets.shape[2]

    def one_hot(row, extent):
        positions = lax.broadcasted_iota(jnp.int32, (extent, entries), 0)
        return jnp.where(positions == row, 1.0, 0.0).astype(jnp.bfloat16)

    def lanes_of(pair, row):
        wide = pair.astype(jnp.float32)
        picked = [
            jnp.take_along_axis(
                wide,
                jnp.broadcast_to(row[:, at : at + PAIR], (rank, PAIR)),
                axis=1,
                mode="promise_in_bounds",
            )
            for at in range(0, entries, PAIR)
        ]
        return jnp.concatenate(picked, axis=1)

    def group(step, carry):
        first = pl.multiple_of(step * UNROLL, UNROLL)
        targets = offsets[target_at, pl.ds(first, UNROLL), :]
        sources = offsets[1 - target_at, pl.ds(first, UNROLL), :]
        contexts = offsets[2, pl.ds(first, UNROLL), :]
        weights = values[pl.ds(first, UNROLL), :]
        for at in range(UNROLL):
            row = slice(at, at + 1)
            source_id, context_id = source_ids[first + at], context_ids[first + at]
            context_row = contexts[row] + TILE * lax.rem(context_id, 2)
            source_part = jnp.dot(
                source[source_id],
                one_hot(sources[row], TILE),
                preferred_element_type=jnp.float32,
            )
            context_part = lanes_of(context[lax.div(context_id, 2)], context_row)
            weight = jnp.where(first + at < count[0], weights[row], 0.0)
            terms = (weight * source_part * context_part).astype(jnp.bfloat16)
            totals[target_ids[first + at]] += lax.dot_general(
                one_hot(targets[row], TILE),
                terms,
                (((1,), (1,)), ((), ())),
                preferred_element_type=jnp.float32,
            )
        return carry

    lax.fori_loop(0, (count[0] + UNROLL - 1) // UNROLL, group, 0)
    out[...] = totals[...].astype(out.dtype)


def unpack_kernel(pairs, tiles):
    def step(at, carry):
        for pair in range(8):
            for half in range(2):
                tiles[16 * at + 2 * pair + half] = pairs[8 * at + pair][
                    :, half * TILE : (half + 1) * TILE
                ]
        return carry

    lax.fori_loop(0, pairs.shape[0] // 8, step, 0)


def unpack(pairs):
    count, rank, _ = pairs.shape
    return pl.pallas_call(
        unpack_kernel,
        out_shape=jax.ShapeDtypeStruct((2 * count, rank, TILE), pairs.dtype),
        in_specs=[VMEM_SPEC],
        out_specs=VMEM_SPEC,
        compiler_params=pltpu.CompilerParams(vmem_limit_bytes=16 * 2**20),
        name="unpack",
    )(pairs)


def mttkrp(target_at, count, ids, offsets, values, source_pairs, context_pairs, tiles):
    shape = (tiles, TILE, source_pairs.shape[1])
    source_tiles = unpack(source_pairs)
    return pl.pallas_call(
        functools.partial(mttkrp_kernel, target_at),
        out_shape=jax.ShapeDtypeStruct(shape, jnp.bfloat16),
        in_specs=[SMEM_SPEC] * 4 + [VMEM_SPEC] * 4,
        out_specs=VMEM_SPEC,
        scratch_shapes=[pltpu.VMEM(shape, jnp.float32)],
        compiler_params=pltpu.CompilerParams(vmem_limit_bytes=24 * 2**20),
        name="mttkrp",
    )(
        count,
        ids[target_at],
        ids[1 - target_at],
        ids[2],
        offsets,
        values,
        source_tiles,
        context_pairs,
    )


def greet(groups):
    barrier = pltpu.get_barrier_semaphore()
    for axis, size in groups:
        me = lax.axis_index(axis)
        for ahead in range(1, size):
            pl.semaphore_signal(
                barrier, inc=1, device_id={axis: lax.rem(me + ahead, size)}, device_id_type=MESH
            )


def await_greetings(groups):
    pl.semaphore_wait(pltpu.get_barrier_semaphore(), sum(size - 1 for _, size in groups))


def send_all(axis, size, source, target, sems):
    me = lax.axis_index(axis)
    copies = []
    for ahead in range(1, size):
        peer = lax.rem(me + ahead, size)
        copy = pltpu.make_async_remote_copy(
            src_ref=source(peer, ahead),
            dst_ref=target(me, ahead),
            send_sem=sems.at[0, ahead - 1],
            recv_sem=sems.at[1, ahead - 1],
            device_id={axis: peer},
            device_id_type=MESH,
        )
        copy.start()
        copies.append(copy)
    return copies


def copy_to(source, target, sems, user, item):
    copy = pltpu.make_async_remote_copy(
        src_ref=source,
        dst_ref=target,
        send_sem=sems.at[0],
        recv_sem=sems.at[1],
        device_id=(user, item),
        device_id_type=MESH,
    )
    copy.start()
    return copy


def receive(copies):
    for copy in copies:
        copy.wait_recv()


def rows_of(item, rows):
    return pl.ds(pl.multiple_of(item * rows, rows), rows)


def gram_to_users(gram, by_user, sems, users):
    rows = by_user.shape[1]
    user = lax.axis_index("user")
    by_user[user] = gram[rows_of(user, rows), :]
    return send_all(
        "user",
        users,
        lambda peer, ahead: gram.at[rows_of(peer, rows)],
        lambda me, ahead: by_user.at[me],
        sems,
    )


def torus(side):
    item = lax.axis_index("item")
    slow, fast = item // side, lax.rem(item, side)

    def at_slow(ahead):
        return lax.rem(slow + ahead, side) * side + fast

    def at_fast(ahead):
        return slow * side + lax.rem(fast + ahead, side)

    return slow, fast, at_slow, at_fast


def exchange(before, terms, place, along, spread, sems):
    receive(before)
    spread[place] = jnp.sum(terms[...], axis=0)
    user = lax.axis_index("user")
    return [
        copy_to(spread.at[place], spread.at[place], sems.at[ahead - 1], user, along(ahead))
        for ahead in HOPS
    ]


def blocks_back(block, result, sems, users):
    rows = block.shape[0]
    span = rows_of(lax.axis_index("user"), rows)
    result[span, :] = block[...]
    return send_all("user", users, lambda peer, ahead: block, lambda me, ahead: result.at[span], sems)


def gram_scratch(users, side, width):
    rows = width // users
    return [
        pltpu.VMEM((width, width), jnp.float32),
        pltpu.VMEM((users, rows, width), jnp.float32),
        pltpu.VMEM((side, rows, width), jnp.float32),
        pltpu.VMEM((side, rows, width), jnp.float32),
        pltpu.SemaphoreType.DMA((2, users - 1)),
        pltpu.SemaphoreType.DMA((side - 1, 2)),
        pltpu.SemaphoreType.DMA((side - 1, 2)),
    ]


def small_inverse(matrix):
    size = len(matrix)
    if size == 2:
        (first, off), (_, last) = matrix
        scale = 1.0 / (first * last - off * off)
        cross = -off * scale
        return [[last * scale, cross], [cross, first * scale]]
    half = size // 2

    def product(left, right):
        return [
            [sum(left[i][k] * right[k][j] for k in range(1, half)) + left[i][0] * right[0][j] for j in range(half)]
            for i in range(half)
        ]

    corner = small_inverse([row[:half] for row in matrix[:half]])
    side = [row[half:] for row in matrix[:half]]
    solved = product(corner, side)
    lowered = product([list(column) for column in zip(*side)], solved)
    rest = small_inverse(
        [[matrix[half + i][half + j] - lowered[i][j] for j in range(half)] for i in range(half)]
    )
    spread = product(solved, rest)
    update = product(spread, [list(column) for column in zip(*solved)])
    top = [
        [corner[i][j] + update[i][j] for j in range(half)] + [-spread[i][j] for j in range(half)]
        for i in range(half)
    ]
    bottom = [[-spread[j][i] for j in range(half)] + rest[i] for i in range(half)]
    return top + bottom


def invert(work, first_block, last_block):
    width = work.shape[0]
    down = lax.broadcasted_iota(jnp.int32, (BLOCK, BLOCK), 0)
    across = lax.broadcasted_iota(jnp.int32, (BLOCK, BLOCK), 1)
    lanes = lax.broadcasted_iota(jnp.int32, (BLOCK, width), 1) // BLOCK
    rows = lax.broadcasted_iota(jnp.int32, (width, BLOCK), 0) // BLOCK
    full_lanes = lax.broadcasted_iota(jnp.int32, (width, width), 1) // BLOCK
    steps = range(PIVOTS)
    for block in range(first_block, last_block):
        span = slice(block * BLOCK, (block + 1) * BLOCK)
        pivot = work[span, span]
        for at in range(0, BLOCK, PIVOTS):
            columns = [
                jnp.broadcast_to(pivot[:, at + i : at + i + 1], (BLOCK, BLOCK)) for i in steps
            ]
            inverse = small_inverse(
                [
                    [columns[max(i, j)][at + min(i, j) : at + min(i, j) + 1, :] for j in steps]
                    for i in steps
                ]
            )
            fresh = []
            for i in steps:
                row = inverse[i][0] * pivot[at : at + 1, :]
                for j in steps[1:]:
                    row = row + inverse[i][j] * pivot[at + j : at + j + 1, :]
                for j in steps:
                    row = jnp.where(across[:1] == at + j, inverse[i][j], row)
                fresh.append(row)
            after = jnp.where((across >= at) & (across < at + PIVOTS), 0.0, pivot)
            for i in steps:
                after = after - columns[i] * fresh[i]
            for i in steps:
                after = jnp.where(down == at + i, fresh[i], after)
            pivot = after
        panel = dot(pivot, work[span, :])
        panel = jnp.where(lanes == block, jnp.concatenate([pivot] * (width // BLOCK), axis=1), panel)
        column = jnp.where(rows == block, 0.0, work[:, span])
        kept = jnp.where(full_lanes == block, 0.0, work[...])
        work[...] = kept - dot(column, panel)
        work[span, :] = panel


def gather_kernel(
    axis_sizes, side, step_rows, item_factor, context_factor, items, context, gram_rows, context_gram,
    own_rows, loaded, load_sems, own_sems, sibling_sems,
    gram, by_user, by_slow, by_fast, user_sems, slow_sems, fast_sems,
):
    users, items_extent = axis_sizes
    everyone = (("user", users), ("item", items_extent))
    user, item = lax.axis_index("user"), lax.axis_index("item")
    slow, fast, at_slow, at_fast = torus(side)
    steps = context_factor.shape[0] // step_rows
    pairs = step_rows // PAIR
    greet(everyone)

    def load(step):
        span = pl.ds(pl.multiple_of(step * step_rows, step_rows), step_rows)
        return pltpu.make_async_copy(context_factor.at[span], loaded.at[step], load_sems.at[step])

    def transform(step, carry):
        load(step).wait()
        chunk = loaded[step]
        columns = chunk.T
        for pair in range(pairs):
            context[step * pairs + pair] = columns[:, pair * PAIR : (pair + 1) * PAIR].astype(
                jnp.bfloat16
            )
        context_gram[...] += gram_of(columns)
        return carry

    fetch = pltpu.make_async_copy(item_factor, own_rows, load_sems.at[steps])
    fetch.start()
    for step in range(steps):
        load(step).start()
    context_gram[...] = jnp.zeros_like(context_gram)
    fetch.wait()
    columns = own_rows[...].T
    for pair in range(items.shape[1]):
        items[user, pair] = columns[:, pair * PAIR : (pair + 1) * PAIR].astype(jnp.bfloat16)
    gram[...] = gram_of(columns)
    await_greetings(everyone)
    first = gram_to_users(gram, by_user, user_sems, users)
    core = lax.rem(user, 2)
    sibling = user + 1 - 2 * core
    own = []
    for ahead in HOPS:
        peer = lax.rem(user + 2 * ahead, users)
        own.append(copy_to(items.at[user], items.at[user], own_sems.at[ahead - 1], peer, item))
    forwarded = [copy_to(items.at[user], items.at[user], sibling_sems.at[0], sibling, item)]

    def forward(at):
        own[at].wait_recv()
        block = items.at[lax.rem(user + users - 2 * HOPS[at], users)]
        forwarded.append(copy_to(block, block, sibling_sems.at[1 + at], sibling, item))

    lax.fori_loop(0, CONTEXT_STEPS[0], transform, 0)
    second = exchange(first, by_user, slow, at_slow, by_slow, slow_sems)
    forward(0)
    forward(1)
    lax.fori_loop(CONTEXT_STEPS[0], CONTEXT_STEPS[0] + CONTEXT_STEPS[1], transform, 0)
    third = exchange(second, by_slow, fast, at_fast, by_fast, fast_sems)
    forward(2)
    lax.fori_loop(CONTEXT_STEPS[0] + CONTEXT_STEPS[1], steps, transform, 0)
    receive(third)
    gram_rows[...] = jnp.sum(by_fast[...], axis=0)
    receive(forwarded)
    for copy in first + own + forwarded + second + third:
        copy.wait_send()


def gather_items(item_factor, context_factor, axis_sizes, side):
    users, items = axis_sizes
    rows, width = item_factor.shape
    contexts = context_factor.shape[0]
    step_rows = 512
    return pl.pallas_call(
        functools.partial(gather_kernel, axis_sizes, side, step_rows),
        out_shape=(
            jax.ShapeDtypeStruct((users, rows // PAIR, width, PAIR), jnp.bfloat16),
            jax.ShapeDtypeStruct((contexts // PAIR, width, PAIR), jnp.bfloat16),
            jax.ShapeDtypeStruct((width // users, width), jnp.float32),
            jax.ShapeDtypeStruct((width, width), jnp.float32),
        ),
        in_specs=[pl.BlockSpec(memory_space=pltpu.HBM)] * 2,
        out_specs=(VMEM_SPEC,) * 4,
        scratch_shapes=[
            pltpu.VMEM((rows, width), jnp.float32),
            pltpu.VMEM((contexts // step_rows, step_rows, width), jnp.float32),
            pltpu.SemaphoreType.DMA((contexts // step_rows + 1,)),
            pltpu.SemaphoreType.DMA((users // 2 - 1, 2)),
            pltpu.SemaphoreType.DMA((users // 2, 2)),
        ]
        + gram_scratch(users, side, width),
        compiler_params=pltpu.CompilerParams(
            collective_id=0, has_side_effects=True, vmem_limit_bytes=16 * 2**20
        ),
        name="gather_items",
    )(
        pltpu.with_memory_space_constraint(item_factor, pltpu.HBM),
        pltpu.with_memory_space_constraint(context_factor, pltpu.HBM),
    )


def user_kernel(
    axis_sizes, side, partial, gram_rows, context_gram, raw, gathered, raw_gram, arrived, mixed, settled,
    work, far_sems, near_sems, out_sems, on_sems, system_sems, raw_block, raw_sems,
    gram, by_user, by_slow, by_fast, user_sems, slow_sems, fast_sems,
):
    users, items = axis_sizes
    user, item = lax.axis_index("user"), lax.axis_index("item")
    slow, fast, at_slow, at_fast = torus(side)
    half = partial.shape[2] // 2
    blocks = work.shape[0] // BLOCK
    everyone = (("user", users), ("item", items))
    greet(everyone)
    await_greetings(everyone)
    system = blocks_back(gram_rows, work, system_sems, users)

    far = []
    for ahead in HOPS:
        far.append(
            copy_to(
                partial.at[lax.rem(slow + ahead, side), :, pl.ds(0, half)],
                arrived.at[0, ahead - 1],
                far_sems.at[0, ahead - 1],
                user,
                at_slow(ahead),
            )
        )
        far.append(
            copy_to(
                partial.at[:, lax.rem(fast + ahead, side), pl.ds(half, half)],
                arrived.at[1, ahead - 1],
                far_sems.at[1, ahead - 1],
                user,
                at_fast(ahead),
            )
        )
    receive(system)
    work[...] = work[...] * context_gram[...]
    invert(work, 0, SPLIT)

    def combine(part, where):
        own = partial[slow, where, :half] if part == 0 else partial[where, fast, half:]
        total = own.astype(jnp.float32)
        for ahead in range(side - 1):
            total = total + arrived[part, ahead, where].astype(jnp.float32)
        return total

    near = []
    kept = []
    for part in range(2):
        receive(far[part::2])
        here = fast if part == 0 else slow
        for ahead in HOPS:
            where = lax.rem(here + ahead, side)
            mixed[part, ahead - 1] = combine(part, where).astype(mixed.dtype)
            near.append(
                copy_to(
                    mixed.at[part, ahead - 1],
                    settled.at[part, ahead - 1],
                    near_sems.at[part, ahead - 1],
                    user,
                    at_fast(ahead) if part == 0 else at_slow(ahead),
                )
            )
        kept.append(combine(part, here))
    invert(work, SPLIT, blocks)
    receive(near)
    total = jnp.concatenate(
        [
            kept[part] + sum(settled[part, at].astype(jnp.float32) for at in range(side - 1))
            for part in range(2)
        ],
        axis=0,
    )
    raw[...] = dot(total, work[...])
    columns = raw[...].T
    for part in range(2):
        gathered[item, part] = columns[:, part * PAIR : (part + 1) * PAIR].astype(jnp.bfloat16)

    onward = []

    def pass_on(block, part, stage):
        for ahead in HOPS:
            onward.append(
                copy_to(
                    gathered.at[block, part],
                    gathered.at[block, part],
                    on_sems.at[part, stage, ahead - 1],
                    user,
                    at_fast(ahead) if part == 0 else at_slow(ahead),
                )
            )

    outward = []
    for ahead in HOPS:
        for part in range(2):
            outward.append(
                copy_to(
                    gathered.at[item, part],
                    gathered.at[item, part],
                    out_sems.at[part, ahead - 1],
                    user,
                    at_slow(ahead) if part == 0 else at_fast(ahead),
                )
            )
    gram[...] = gram_of(columns)
    first = gram_to_users(gram, by_user, user_sems, users)
    for part in range(2):
        pass_on(item, part, 0)

    def forward(at):
        for part in range(2):
            outward[2 * at + part].wait_recv()
            back = side - HOPS[at]
            pass_on(at_slow(back) if part == 0 else at_fast(back), part, HOPS[at])

    second = exchange(first, by_user, slow, at_slow, by_slow, slow_sems)
    forward(0)
    third = exchange(second, by_slow, fast, at_fast, by_fast, fast_sems)
    forward(1)
    forward(2)
    receive(third)
    raw_block[...] = jnp.sum(by_fast[...], axis=0)
    fourth = blocks_back(raw_block, raw_gram, raw_sems, users)
    receive(onward)
    receive(fourth)
    for copy in system + far + near + outward + onward + first + second + third + fourth:
        copy.wait_send()


def update_users(partial, gram_rows, context_gram, axis_sizes):
    users, items = axis_sizes
    side, _, rows, width = partial.shape
    half = rows // 2
    square = jax.ShapeDtypeStruct((width, width), jnp.float32)
    return pl.pallas_call(
        functools.partial(user_kernel, axis_sizes, side),
        out_shape=(
            jax.ShapeDtypeStruct((rows, width), jnp.float32),
            jax.ShapeDtypeStruct((items, rows // PAIR, width, PAIR), jnp.bfloat16),
            square,
        ),
        in_specs=[VMEM_SPEC] * 3,
        out_specs=(VMEM_SPEC,) * 3,
        scratch_shapes=[
            pltpu.VMEM((2, side - 1, side, half, width), jnp.bfloat16),
            pltpu.VMEM((2, side - 1, half, width), jnp.bfloat16),
            pltpu.VMEM((2, side - 1, half, width), jnp.bfloat16),
            pltpu.VMEM((width, width), jnp.float32),
            pltpu.SemaphoreType.DMA((2, side - 1, 2)),
            pltpu.SemaphoreType.DMA((2, side - 1, 2)),
            pltpu.SemaphoreType.DMA((2, side - 1, 2)),
            pltpu.SemaphoreType.DMA((2, side, side - 1, 2)),
            pltpu.SemaphoreType.DMA((2, users - 1)),
            pltpu.VMEM((width // users, width), jnp.float32),
            pltpu.SemaphoreType.DMA((2, users - 1)),
        ]
        + gram_scratch(users, side, width),
        compiler_params=pltpu.CompilerParams(
            collective_id=1, has_side_effects=True, vmem_limit_bytes=24 * 2**20
        ),
        name="update_users",
    )(partial, gram_rows, context_gram)


def item_kernel(
    axis_sizes, partial, raw_gram, context_gram, raw, new_items, user_factor, arrived, work,
    user_sums, item_sums, user_sems, item_sems, sems
):
    users, items = axis_sizes
    user, item = lax.axis_index("user"), lax.axis_index("item")
    everyone = (("user", users), ("item", items))
    greet(everyone)
    await_greetings(everyone)
    copies = send_all(
        "user",
        users,
        lambda peer, ahead: partial.at[peer],
        lambda me, ahead: arrived.at[ahead - 1],
        sems,
    )
    width = work.shape[0]
    rows_total = jnp.float32(user_factor.shape[0] * users * items)
    down = lax.broadcasted_iota(jnp.int32, (width, width), 0)
    across = lax.broadcasted_iota(jnp.int32, (width, width), 1)
    diagonal = jnp.where(down == across, raw_gram[...], 0.0)
    scale_row = jnp.sqrt(rows_total / (jnp.sum(diagonal, axis=0, keepdims=True) + 1e-06))
    scale_column = jnp.sqrt(rows_total / (jnp.sum(diagonal, axis=1, keepdims=True) + 1e-06))
    user_factor[...] = raw[...] * scale_row
    work[...] = raw_gram[...] * scale_column * scale_row * context_gram[...]
    invert(work, 0, width // BLOCK)
    total = partial[user].astype(jnp.float32)
    for ahead in range(1, users):
        copies[ahead - 1].wait_recv()
        total = total + arrived[ahead - 1].astype(jnp.float32)
    item_raw = dot(total * scale_row, work[...])
    squares = jnp.sum(item_raw * item_raw, axis=0, keepdims=True)
    user_sums[user] = jnp.broadcast_to(squares, user_sums.shape[1:])
    first = send_all(
        "user", users, lambda peer, ahead: user_sums.at[user], lambda me, ahead: user_sums.at[me], user_sems
    )
    receive(first)
    item_sums[item] = jnp.sum(user_sums[...], axis=0)
    second = send_all(
        "item", items, lambda peer, ahead: item_sums.at[item], lambda me, ahead: item_sums.at[me], item_sems
    )
    receive(second)
    squares = jnp.sum(item_sums[...], axis=0)[:1]
    new_items[...] = item_raw * jnp.sqrt(rows_total / (squares + 1e-06))
    for copy in copies + first + second:
        copy.wait_send()


def update_items(partial, raw_gram, context_gram, raw, axis_sizes):
    users, items = axis_sizes
    _, rows, width = partial.shape
    out = jax.ShapeDtypeStruct((rows, width), jnp.float32)
    return pl.pallas_call(
        functools.partial(item_kernel, axis_sizes),
        out_shape=(out, out),
        in_specs=[VMEM_SPEC] * 4,
        out_specs=(VMEM_SPEC,) * 2,
        scratch_shapes=[
            pltpu.VMEM((users - 1, rows, width), jnp.bfloat16),
            pltpu.VMEM((width, width), jnp.float32),
            pltpu.VMEM((users, 8, width), jnp.float32),
            pltpu.VMEM((items, 8, width), jnp.float32),
            pltpu.SemaphoreType.DMA((2, users - 1)),
            pltpu.SemaphoreType.DMA((2, items - 1)),
            pltpu.SemaphoreType.DMA((2, users - 1)),
        ],
        compiler_params=pltpu.CompilerParams(
            collective_id=2, has_side_effects=True, vmem_limit_bytes=16 * 2**20
        ),
        name="update_items",
    )(partial, raw_gram, context_gram, raw)


def local(
    item_factor, context_factor, tile_count, tile_rows, tile_cols, tile_ctx, nz_offsets, nz_values
):
    axis_sizes = (lax.axis_size("user"), lax.axis_size("item"))
    users, items = axis_sizes
    rows, width = item_factor.shape
    side = math.isqrt(items)
    count = tile_count.reshape(1)
    ids = (tile_rows[0, 0], tile_cols[0, 0], tile_ctx[0, 0])
    offsets = nz_offsets[0, 0]
    values = nz_values[0, 0]
    item_pairs, context_pairs, gram_rows, context_gram = gather_items(
        item_factor, context_factor, axis_sizes, side
    )
    partial_users = mttkrp(
        0, count, ids, offsets, values, item_pairs.reshape(-1, width, PAIR), context_pairs,
        items * rows // TILE,
    )
    raw, user_pairs, raw_gram = update_users(
        partial_users.reshape(side, side, rows, width), gram_rows, context_gram, axis_sizes
    )
    partial_items = mttkrp(
        1, count, ids, offsets, values, user_pairs.reshape(-1, width, PAIR), context_pairs,
        users * rows // TILE,
    )
    new_items, user_factor = update_items(
        partial_items.reshape(users, rows, width), raw_gram, context_gram, raw, axis_sizes
    )
    return (user_factor, new_items)


def solution(mesh):
    in_specs = (
        P(("item", "user"), None),
        P(),
        P("user", "item"),
        P("user", "item", None),
        P("user", "item", None),
        P("user", "item", None),
        P("user", "item", None, None, None),
        P("user", "item", None, None),
    )
    out_specs = (P(("user", "item"), None), P(("item", "user"), None))
    return jax.shard_map(local, mesh=mesh, in_specs=in_specs, out_specs=out_specs, check_vma=False)
```

```python
import functools
import math

import jax
import jax.numpy as jnp
from jax import lax
from jax.experimental import pallas as pl
from jax.experimental.pallas import tpu as pltpu
from jax.sharding import PartitionSpec as P

TILE = 64
UNROLL = 32
CONTEXT_STEPS = (3, 2)
PAIR = 2 * TILE
BLOCK = 64
SPLIT = 2
HOPS = (1, 3, 2)
PIVOTS = 4
HIGHEST = lax.Precision.HIGHEST
MESH = pl.DeviceIdType.MESH
VMEM_SPEC = pl.BlockSpec(memory_space=pltpu.VMEM)
SMEM_SPEC = pl.BlockSpec(memory_space=pltpu.SMEM)


def dot(left, right):
    return jnp.dot(left, right, precision=HIGHEST, preferred_element_type=jnp.float32)


def gram_of(columns):
    return lax.dot_general(
        columns,
        columns,
        (((1,), (1,)), ((), ())),
        precision=HIGHEST,
        preferred_element_type=jnp.float32,
    )


def mttkrp_kernel(
    target_at,
    count,
    target_ids,
    source_ids,
    context_ids,
    offsets,
    values,
    source,
    context,
    out,
    totals,
):
    totals[...] = jnp.zeros_like(totals)
    rank, entries = totals.shape[2], offsets.shape[2]

    def one_hot(row, extent):
        positions = lax.broadcasted_iota(jnp.int32, (extent, entries), 0)
        return jnp.where(positions == row, 1.0, 0.0).astype(jnp.bfloat16)

    def lanes_of(pair, row):
        wide = pair.astype(jnp.float32)
        picked = [
            jnp.take_along_axis(
                wide,
                jnp.broadcast_to(row[:, at : at + PAIR], (rank, PAIR)),
                axis=1,
                mode="promise_in_bounds",
            )
            for at in range(0, entries, PAIR)
        ]
        return jnp.concatenate(picked, axis=1)

    def group(step, carry):
        first = pl.multiple_of(step * UNROLL, UNROLL)
        targets = offsets[target_at, pl.ds(first, UNROLL), :]
        sources = offsets[1 - target_at, pl.ds(first, UNROLL), :]
        contexts = offsets[2, pl.ds(first, UNROLL), :]
        weights = values[pl.ds(first, UNROLL), :]
        for at in range(UNROLL):
            row = slice(at, at + 1)
            source_id, context_id = source_ids[first + at], context_ids[first + at]
            source_row = sources[row] + TILE * lax.rem(source_id, 2)
            context_row = contexts[row] + TILE * lax.rem(context_id, 2)
            source_part = jnp.dot(
                source[lax.div(source_id, 2)],
                one_hot(source_row, PAIR),
                preferred_element_type=jnp.float32,
            )
            context_part = lanes_of(context[lax.div(context_id, 2)], context_row)
            weight = jnp.where(first + at < count[0], weights[row], 0.0)
            terms = (weight * source_part * context_part).astype(jnp.bfloat16)
            totals[target_ids[first + at]] += lax.dot_general(
                one_hot(targets[row], TILE),
                terms,
                (((1,), (1,)), ((), ())),
                preferred_element_type=jnp.float32,
            )
        return carry

    lax.fori_loop(0, (count[0] + UNROLL - 1) // UNROLL, group, 0)
    out[...] = totals[...].astype(out.dtype)


def mttkrp(target_at, count, ids, offsets, values, source_pairs, context_pairs, tiles):
    shape = (tiles, TILE, source_pairs.shape[1])
    return pl.pallas_call(
        functools.partial(mttkrp_kernel, target_at),
        out_shape=jax.ShapeDtypeStruct(shape, jnp.bfloat16),
        in_specs=[SMEM_SPEC] * 4 + [VMEM_SPEC] * 4,
        out_specs=VMEM_SPEC,
        scratch_shapes=[pltpu.VMEM(shape, jnp.float32)],
        compiler_params=pltpu.CompilerParams(vmem_limit_bytes=24 * 2**20),
        name="mttkrp",
    )(
        count,
        ids[target_at],
        ids[1 - target_at],
        ids[2],
        offsets,
        values,
        source_pairs,
        context_pairs,
    )


def greet(groups):
    barrier = pltpu.get_barrier_semaphore()
    for axis, size in groups:
        me = lax.axis_index(axis)
        for ahead in range(1, size):
            pl.semaphore_signal(
                barrier, inc=1, device_id={axis: lax.rem(me + ahead, size)}, device_id_type=MESH
            )


def await_greetings(groups):
    pl.semaphore_wait(pltpu.get_barrier_semaphore(), sum(size - 1 for _, size in groups))


def send_all(axis, size, source, target, sems):
    me = lax.axis_index(axis)
    copies = []
    for ahead in range(1, size):
        peer = lax.rem(me + ahead, size)
        copy = pltpu.make_async_remote_copy(
            src_ref=source(peer, ahead),
            dst_ref=target(me, ahead),
            send_sem=sems.at[0, ahead - 1],
            recv_sem=sems.at[1, ahead - 1],
            device_id={axis: peer},
            device_id_type=MESH,
        )
        copy.start()
        copies.append(copy)
    return copies


def copy_to(source, target, sems, user, item):
    copy = pltpu.make_async_remote_copy(
        src_ref=source,
        dst_ref=target,
        send_sem=sems.at[0],
        recv_sem=sems.at[1],
        device_id=(user, item),
        device_id_type=MESH,
    )
    copy.start()
    return copy


def receive(copies):
    for copy in copies:
        copy.wait_recv()


def rows_of(item, rows):
    return pl.ds(pl.multiple_of(item * rows, rows), rows)


def gram_to_users(gram, by_user, sems, users):
    rows = by_user.shape[1]
    user = lax.axis_index("user")
    by_user[user] = gram[rows_of(user, rows), :]
    return send_all(
        "user",
        users,
        lambda peer, ahead: gram.at[rows_of(peer, rows)],
        lambda me, ahead: by_user.at[me],
        sems,
    )


def torus(side):
    item = lax.axis_index("item")
    slow, fast = item // side, lax.rem(item, side)

    def at_slow(ahead):
        return lax.rem(slow + ahead, side) * side + fast

    def at_fast(ahead):
        return slow * side + lax.rem(fast + ahead, side)

    return slow, fast, at_slow, at_fast


def exchange(before, terms, place, along, spread, sems):
    receive(before)
    spread[place] = jnp.sum(terms[...], axis=0)
    user = lax.axis_index("user")
    return [
        copy_to(spread.at[place], spread.at[place], sems.at[ahead - 1], user, along(ahead))
        for ahead in HOPS
    ]


def blocks_back(block, result, sems, users):
    rows = block.shape[0]
    span = rows_of(lax.axis_index("user"), rows)
    result[span, :] = block[...]
    return send_all("user", users, lambda peer, ahead: block, lambda me, ahead: result.at[span], sems)


def gram_scratch(users, side, width):
    rows = width // users
    return [
        pltpu.VMEM((width, width), jnp.float32),
        pltpu.VMEM((users, rows, width), jnp.float32),
        pltpu.VMEM((side, rows, width), jnp.float32),
        pltpu.VMEM((side, rows, width), jnp.float32),
        pltpu.SemaphoreType.DMA((2, users - 1)),
        pltpu.SemaphoreType.DMA((side - 1, 2)),
        pltpu.SemaphoreType.DMA((side - 1, 2)),
    ]


def small_inverse(matrix):
    size = len(matrix)
    if size == 2:
        (first, off), (_, last) = matrix
        scale = 1.0 / (first * last - off * off)
        cross = -off * scale
        return [[last * scale, cross], [cross, first * scale]]
    half = size // 2

    def product(left, right):
        return [
            [sum(left[i][k] * right[k][j] for k in range(1, half)) + left[i][0] * right[0][j] for j in range(half)]
            for i in range(half)
        ]

    corner = small_inverse([row[:half] for row in matrix[:half]])
    side = [row[half:] for row in matrix[:half]]
    solved = product(corner, side)
    lowered = product([list(column) for column in zip(*side)], solved)
    rest = small_inverse(
        [[matrix[half + i][half + j] - lowered[i][j] for j in range(half)] for i in range(half)]
    )
    spread = product(solved, rest)
    update = product(spread, [list(column) for column in zip(*solved)])
    top = [
        [corner[i][j] + update[i][j] for j in range(half)] + [-spread[i][j] for j in range(half)]
        for i in range(half)
    ]
    bottom = [[-spread[j][i] for j in range(half)] + rest[i] for i in range(half)]
    return top + bottom


def invert(work, first_block, last_block):
    width = work.shape[0]
    down = lax.broadcasted_iota(jnp.int32, (BLOCK, BLOCK), 0)
    across = lax.broadcasted_iota(jnp.int32, (BLOCK, BLOCK), 1)
    lanes = lax.broadcasted_iota(jnp.int32, (BLOCK, width), 1) // BLOCK
    rows = lax.broadcasted_iota(jnp.int32, (width, BLOCK), 0) // BLOCK
    full_lanes = lax.broadcasted_iota(jnp.int32, (width, width), 1) // BLOCK
    steps = range(PIVOTS)
    for block in range(first_block, last_block):
        span = slice(block * BLOCK, (block + 1) * BLOCK)
        pivot = work[span, span]
        for at in range(0, BLOCK, PIVOTS):
            columns = [
                jnp.broadcast_to(pivot[:, at + i : at + i + 1], (BLOCK, BLOCK)) for i in steps
            ]
            inverse = small_inverse(
                [
                    [columns[max(i, j)][at + min(i, j) : at + min(i, j) + 1, :] for j in steps]
                    for i in steps
                ]
            )
            fresh = []
            for i in steps:
                row = inverse[i][0] * pivot[at : at + 1, :]
                for j in steps[1:]:
                    row = row + inverse[i][j] * pivot[at + j : at + j + 1, :]
                for j in steps:
                    row = jnp.where(across[:1] == at + j, inverse[i][j], row)
                fresh.append(row)
            after = jnp.where((across >= at) & (across < at + PIVOTS), 0.0, pivot)
            for i in steps:
                after = after - columns[i] * fresh[i]
            for i in steps:
                after = jnp.where(down == at + i, fresh[i], after)
            pivot = after
        panel = dot(pivot, work[span, :])
        panel = jnp.where(lanes == block, jnp.concatenate([pivot] * (width // BLOCK), axis=1), panel)
        column = jnp.where(rows == block, 0.0, work[:, span])
        kept = jnp.where(full_lanes == block, 0.0, work[...])
        work[...] = kept - dot(column, panel)
        work[span, :] = panel


def gather_kernel(
    axis_sizes, side, step_rows, item_factor, context_factor, items, context, gram_rows, context_gram,
    own_rows, loaded, load_sems, own_sems, sibling_sems,
    gram, by_user, by_slow, by_fast, user_sems, slow_sems, fast_sems,
):
    users, items_extent = axis_sizes
    everyone = (("user", users), ("item", items_extent))
    user, item = lax.axis_index("user"), lax.axis_index("item")
    slow, fast, at_slow, at_fast = torus(side)
    steps = context_factor.shape[0] // step_rows
    pairs = step_rows // PAIR
    greet(everyone)

    def load(step):
        span = pl.ds(pl.multiple_of(step * step_rows, step_rows), step_rows)
        return pltpu.make_async_copy(context_factor.at[span], loaded.at[step], load_sems.at[step])

    def transform(step, carry):
        load(step).wait()
        chunk = loaded[step]
        columns = chunk.T
        for pair in range(pairs):
            context[step * pairs + pair] = columns[:, pair * PAIR : (pair + 1) * PAIR].astype(
                jnp.bfloat16
            )
        context_gram[...] += gram_of(columns)
        return carry

    fetch = pltpu.make_async_copy(item_factor, own_rows, load_sems.at[steps])
    fetch.start()
    for step in range(steps):
        load(step).start()
    context_gram[...] = jnp.zeros_like(context_gram)
    fetch.wait()
    columns = own_rows[...].T
    for pair in range(items.shape[1]):
        items[user, pair] = columns[:, pair * PAIR : (pair + 1) * PAIR].astype(jnp.bfloat16)
    gram[...] = gram_of(columns)
    await_greetings(everyone)
    first = gram_to_users(gram, by_user, user_sems, users)
    core = lax.rem(user, 2)
    sibling = user + 1 - 2 * core
    own = []
    for ahead in HOPS:
        peer = lax.rem(user + 2 * ahead, users)
        own.append(copy_to(items.at[user], items.at[user], own_sems.at[ahead - 1], peer, item))
    forwarded = [copy_to(items.at[user], items.at[user], sibling_sems.at[0], sibling, item)]

    def forward(at):
        own[at].wait_recv()
        block = items.at[lax.rem(user + users - 2 * HOPS[at], users)]
        forwarded.append(copy_to(block, block, sibling_sems.at[1 + at], sibling, item))

    lax.fori_loop(0, CONTEXT_STEPS[0], transform, 0)
    second = exchange(first, by_user, slow, at_slow, by_slow, slow_sems)
    forward(0)
    forward(1)
    lax.fori_loop(CONTEXT_STEPS[0], CONTEXT_STEPS[0] + CONTEXT_STEPS[1], transform, 0)
    third = exchange(second, by_slow, fast, at_fast, by_fast, fast_sems)
    forward(2)
    lax.fori_loop(CONTEXT_STEPS[0] + CONTEXT_STEPS[1], steps, transform, 0)
    receive(third)
    gram_rows[...] = jnp.sum(by_fast[...], axis=0)
    receive(forwarded)
    for copy in first + own + forwarded + second + third:
        copy.wait_send()


def gather_items(item_factor, context_factor, axis_sizes, side):
    users, items = axis_sizes
    rows, width = item_factor.shape
    contexts = context_factor.shape[0]
    step_rows = 512
    return pl.pallas_call(
        functools.partial(gather_kernel, axis_sizes, side, step_rows),
        out_shape=(
            jax.ShapeDtypeStruct((users, rows // PAIR, width, PAIR), jnp.bfloat16),
            jax.ShapeDtypeStruct((contexts // PAIR, width, PAIR), jnp.bfloat16),
            jax.ShapeDtypeStruct((width // users, width), jnp.float32),
            jax.ShapeDtypeStruct((width, width), jnp.float32),
        ),
        in_specs=[pl.BlockSpec(memory_space=pltpu.HBM)] * 2,
        out_specs=(VMEM_SPEC,) * 4,
        scratch_shapes=[
            pltpu.VMEM((rows, width), jnp.float32),
            pltpu.VMEM((contexts // step_rows, step_rows, width), jnp.float32),
            pltpu.SemaphoreType.DMA((contexts // step_rows + 1,)),
            pltpu.SemaphoreType.DMA((users // 2 - 1, 2)),
            pltpu.SemaphoreType.DMA((users // 2, 2)),
        ]
        + gram_scratch(users, side, width),
        compiler_params=pltpu.CompilerParams(
            collective_id=0, has_side_effects=True, vmem_limit_bytes=16 * 2**20
        ),
        name="gather_items",
    )(
        pltpu.with_memory_space_constraint(item_factor, pltpu.HBM),
        pltpu.with_memory_space_constraint(context_factor, pltpu.HBM),
    )


def user_kernel(
    axis_sizes, side, partial, gram_rows, context_gram, raw, gathered, raw_gram, arrived, mixed, settled,
    work, far_sems, near_sems, out_sems, on_sems, system_sems, raw_block, raw_sems,
    gram, by_user, by_slow, by_fast, user_sems, slow_sems, fast_sems,
):
    users, items = axis_sizes
    user, item = lax.axis_index("user"), lax.axis_index("item")
    slow, fast, at_slow, at_fast = torus(side)
    half = partial.shape[2] // 2
    blocks = work.shape[0] // BLOCK
    everyone = (("user", users), ("item", items))
    greet(everyone)
    await_greetings(everyone)
    system = blocks_back(gram_rows, work, system_sems, users)

    far = []
    for ahead in HOPS:
        far.append(
            copy_to(
                partial.at[lax.rem(slow + ahead, side), :, pl.ds(0, half)],
                arrived.at[0, ahead - 1],
                far_sems.at[0, ahead - 1],
                user,
                at_slow(ahead),
            )
        )
        far.append(
            copy_to(
                partial.at[:, lax.rem(fast + ahead, side), pl.ds(half, half)],
                arrived.at[1, ahead - 1],
                far_sems.at[1, ahead - 1],
                user,
                at_fast(ahead),
            )
        )
    receive(system)
    work[...] = work[...] * context_gram[...]
    invert(work, 0, SPLIT)

    def combine(part, where):
        own = partial[slow, where, :half] if part == 0 else partial[where, fast, half:]
        total = own.astype(jnp.float32)
        for ahead in range(side - 1):
            total = total + arrived[part, ahead, where].astype(jnp.float32)
        return total

    near = []
    kept = []
    for part in range(2):
        receive(far[part::2])
        here = fast if part == 0 else slow
        for ahead in HOPS:
            where = lax.rem(here + ahead, side)
            mixed[part, ahead - 1] = combine(part, where).astype(mixed.dtype)
            near.append(
                copy_to(
                    mixed.at[part, ahead - 1],
                    settled.at[part, ahead - 1],
                    near_sems.at[part, ahead - 1],
                    user,
                    at_fast(ahead) if part == 0 else at_slow(ahead),
                )
            )
        kept.append(combine(part, here))
    invert(work, SPLIT, blocks)
    outward = {}
    for part in range(2):
        receive(near[part * len(HOPS) : (part + 1) * len(HOPS)])
        total = kept[part]
        for at in range(side - 1):
            total = total + settled[part, at].astype(jnp.float32)
        rows = dot(total, work[...])
        raw[part * half : (part + 1) * half, :] = rows
        gathered[item, part] = rows.T.astype(jnp.bfloat16)
        for ahead in HOPS:
            outward[part, ahead] = copy_to(
                gathered.at[item, part],
                gathered.at[item, part],
                out_sems.at[part, ahead - 1],
                user,
                at_slow(ahead) if part == 0 else at_fast(ahead),
            )
    gram[...] = gram_of(raw[...].T)
    onward = []

    def pass_on(block, part, stage):
        for ahead in HOPS:
            onward.append(
                copy_to(
                    gathered.at[block, part],
                    gathered.at[block, part],
                    on_sems.at[part, stage, ahead - 1],
                    user,
                    at_fast(ahead) if part == 0 else at_slow(ahead),
                )
            )

    first = gram_to_users(gram, by_user, user_sems, users)
    for part in range(2):
        pass_on(item, part, 0)

    def forward(at):
        for part in range(2):
            outward[part, HOPS[at]].wait_recv()
            back = side - HOPS[at]
            pass_on(at_slow(back) if part == 0 else at_fast(back), part, HOPS[at])

    second = exchange(first, by_user, slow, at_slow, by_slow, slow_sems)
    forward(0)
    third = exchange(second, by_slow, fast, at_fast, by_fast, fast_sems)
    forward(1)
    forward(2)
    receive(third)
    raw_block[...] = jnp.sum(by_fast[...], axis=0)
    fourth = blocks_back(raw_block, raw_gram, raw_sems, users)
    receive(onward)
    receive(fourth)
    for copy in system + far + near + list(outward.values()) + onward + first + second + third + fourth:
        copy.wait_send()


def update_users(partial, gram_rows, context_gram, axis_sizes):
    users, items = axis_sizes
    side, _, rows, width = partial.shape
    half = rows // 2
    square = jax.ShapeDtypeStruct((width, width), jnp.float32)
    return pl.pallas_call(
        functools.partial(user_kernel, axis_sizes, side),
        out_shape=(
            jax.ShapeDtypeStruct((rows, width), jnp.float32),
            jax.ShapeDtypeStruct((items, rows // PAIR, width, PAIR), jnp.bfloat16),
            square,
        ),
        in_specs=[VMEM_SPEC] * 3,
        out_specs=(VMEM_SPEC,) * 3,
        scratch_shapes=[
            pltpu.VMEM((2, side - 1, side, half, width), jnp.bfloat16),
            pltpu.VMEM((2, side - 1, half, width), jnp.bfloat16),
            pltpu.VMEM((2, side - 1, half, width), jnp.bfloat16),
            pltpu.VMEM((width, width), jnp.float32),
            pltpu.SemaphoreType.DMA((2, side - 1, 2)),
            pltpu.SemaphoreType.DMA((2, side - 1, 2)),
            pltpu.SemaphoreType.DMA((2, side - 1, 2)),
            pltpu.SemaphoreType.DMA((2, side, side - 1, 2)),
            pltpu.SemaphoreType.DMA((2, users - 1)),
            pltpu.VMEM((width // users, width), jnp.float32),
            pltpu.SemaphoreType.DMA((2, users - 1)),
        ]
        + gram_scratch(users, side, width),
        compiler_params=pltpu.CompilerParams(
            collective_id=1, has_side_effects=True, vmem_limit_bytes=24 * 2**20
        ),
        name="update_users",
    )(partial, gram_rows, context_gram)


def item_kernel(
    axis_sizes, partial, raw_gram, context_gram, raw, new_items, user_factor, arrived, work,
    user_sums, item_sums, user_sems, item_sems, sems
):
    users, items = axis_sizes
    user, item = lax.axis_index("user"), lax.axis_index("item")
    everyone = (("user", users), ("item", items))
    greet(everyone)
    await_greetings(everyone)
    copies = send_all(
        "user",
        users,
        lambda peer, ahead: partial.at[peer],
        lambda me, ahead: arrived.at[ahead - 1],
        sems,
    )
    width = work.shape[0]
    rows_total = jnp.float32(user_factor.shape[0] * users * items)
    down = lax.broadcasted_iota(jnp.int32, (width, width), 0)
    across = lax.broadcasted_iota(jnp.int32, (width, width), 1)
    diagonal = jnp.where(down == across, raw_gram[...], 0.0)
    scale_row = jnp.sqrt(rows_total / (jnp.sum(diagonal, axis=0, keepdims=True) + 1e-06))
    scale_column = jnp.sqrt(rows_total / (jnp.sum(diagonal, axis=1, keepdims=True) + 1e-06))
    user_factor[...] = raw[...] * scale_row
    work[...] = raw_gram[...] * scale_column * scale_row * context_gram[...]
    invert(work, 0, width // BLOCK)
    total = partial[user].astype(jnp.float32)
    for ahead in range(1, users):
        copies[ahead - 1].wait_recv()
        total = total + arrived[ahead - 1].astype(jnp.float32)
    item_raw = dot(total * scale_row, work[...])
    squares = jnp.sum(item_raw * item_raw, axis=0, keepdims=True)
    user_sums[user] = jnp.broadcast_to(squares, user_sums.shape[1:])
    first = send_all(
        "user", users, lambda peer, ahead: user_sums.at[user], lambda me, ahead: user_sums.at[me], user_sems
    )
    receive(first)
    item_sums[item] = jnp.sum(user_sums[...], axis=0)
    second = send_all(
        "item", items, lambda peer, ahead: item_sums.at[item], lambda me, ahead: item_sums.at[me], item_sems
    )
    receive(second)
    squares = jnp.sum(item_sums[...], axis=0)[:1]
    new_items[...] = item_raw * jnp.sqrt(rows_total / (squares + 1e-06))
    for copy in copies + first + second:
        copy.wait_send()


def update_items(partial, raw_gram, context_gram, raw, axis_sizes):
    users, items = axis_sizes
    _, rows, width = partial.shape
    out = jax.ShapeDtypeStruct((rows, width), jnp.float32)
    return pl.pallas_call(
        functools.partial(item_kernel, axis_sizes),
        out_shape=(out, out),
        in_specs=[VMEM_SPEC] * 4,
        out_specs=(VMEM_SPEC,) * 2,
        scratch_shapes=[
            pltpu.VMEM((users - 1, rows, width), jnp.bfloat16),
            pltpu.VMEM((width, width), jnp.float32),
            pltpu.VMEM((users, 8, width), jnp.float32),
            pltpu.VMEM((items, 8, width), jnp.float32),
            pltpu.SemaphoreType.DMA((2, users - 1)),
            pltpu.SemaphoreType.DMA((2, items - 1)),
            pltpu.SemaphoreType.DMA((2, users - 1)),
        ],
        compiler_params=pltpu.CompilerParams(
            collective_id=2, has_side_effects=True, vmem_limit_bytes=16 * 2**20
        ),
        name="update_items",
    )(partial, raw_gram, context_gram, raw)


def local(
    item_factor, context_factor, tile_count, tile_rows, tile_cols, tile_ctx, nz_offsets, nz_values
):
    axis_sizes = (lax.axis_size("user"), lax.axis_size("item"))
    users, items = axis_sizes
    rows, width = item_factor.shape
    side = math.isqrt(items)
    count = tile_count.reshape(1)
    ids = (tile_rows[0, 0], tile_cols[0, 0], tile_ctx[0, 0])
    offsets = nz_offsets[0, 0]
    values = nz_values[0, 0]
    item_pairs, context_pairs, gram_rows, context_gram = gather_items(
        item_factor, context_factor, axis_sizes, side
    )
    partial_users = mttkrp(
        0, count, ids, offsets, values, item_pairs.reshape(-1, width, PAIR), context_pairs,
        items * rows // TILE,
    )
    raw, user_pairs, raw_gram = update_users(
        partial_users.reshape(side, side, rows, width), gram_rows, context_gram, axis_sizes
    )
    partial_items = mttkrp(
        1, count, ids, offsets, values, user_pairs.reshape(-1, width, PAIR), context_pairs,
        users * rows // TILE,
    )
    new_items, user_factor = update_items(
        partial_items.reshape(users, rows, width), raw_gram, context_gram, raw, axis_sizes
    )
    return (user_factor, new_items)


def solution(mesh):
    in_specs = (
        P(("item", "user"), None),
        P(),
        P("user", "item"),
        P("user", "item", None),
        P("user", "item", None),
        P("user", "item", None),
        P("user", "item", None, None, None),
        P("user", "item", None, None),
    )
    out_specs = (P(("user", "item"), None), P(("item", "user"), None))
    return jax.shard_map(local, mesh=mesh, in_specs=in_specs, out_specs=out_specs, check_vma=False)
```
